32 devices in a mesh: ctx: 8 (over y, x, core), fsdp: 4 (over z).
Axes of the slice: x: 2, y: 2, z: 4, core: 2. Of those that a mesh axis runs over, the one named last changes fastest.
Arguments:
- tokens: bfloat16 [2, 4, 1536, 768], P(None, 'fsdp', 'ctx'), may hold values from -6 to 6
- doc_ids: int32 [2, 4, 1536], P(None, 'fsdp', 'ctx'), may hold values from 0 to 4, as said below
- keep_mask: int32 [2, 4, 4], P(None, 'fsdp'), may hold values 0 or 1
- qkv_weight: bfloat16 [768, 2304], P('fsdp'), may hold values from -0.3125 to 0.3125
- query_bias: bfloat16 [768], P('fsdp'), may hold values from -3 to 3
- value_bias: bfloat16 [768], P('fsdp'), may hold values from -0.29882812 to 0.29882812
- proj_weight: bfloat16 [768, 768], P('fsdp'), may hold values from -1.25 to 1.25
- proj_bias: bfloat16 [768], P('fsdp'), may hold values from -2 to 2
- norm1_gain: bfloat16 [768], P('fsdp'), may hold values from 0.5 to 1.5
- norm1_bias: bfloat16 [768], P('fsdp'), may hold values from -3 to 3
- up_weight: bfloat16 [768, 3072], P('fsdp'), may hold values from -0.21875 to 0.21875
- up_bias: bfloat16 [3072], P('fsdp'), may hold values from -3 to 3
- down_weight: bfloat16 [3072, 768], P('fsdp'), may hold values from -0.109375 to 0.109375
- down_bias: bfloat16 [768], P('fsdp'), may hold values from -3 to 3
- norm2_gain: bfloat16 [768], P('fsdp'), may hold values from 0.5 to 1.5
- norm2_bias: bfloat16 [768], P('fsdp'), may hold values from -3 to 3
- cotangent: bfloat16 [2, 4, 1536, 768], P(None, 'fsdp', 'ctx'), may hold values from -6 to 6
Outputs:
- block_out: bfloat16 [2, 4, 1536, 768], P(None, 'fsdp', 'ctx')
- grad_tokens: float32 [2, 4, 1536, 768], P(None, 'fsdp', 'ctx')
- grad_qkv: float32 [768, 2304], P(('ctx', 'fsdp'))
- grad_query_bias: float32 [768], P(('ctx', 'fsdp'))
- grad_value_bias: float32 [768], P(('ctx', 'fsdp'))
- grad_proj: float32 [768, 768], P(('ctx', 'fsdp'))
- grad_proj_bias: float32 [768], P(('ctx', 'fsdp'))
- grad_gain1: float32 [768], P(('ctx', 'fsdp'))
- grad_bias1: float32 [768], P(('ctx', 'fsdp'))
- grad_up: float32 [768, 3072], P(('ctx', 'fsdp'))
- grad_up_bias: float32 [3072], P(('ctx', 'fsdp'))
- grad_down: float32 [3072, 768], P(('ctx', 'fsdp'))
- grad_down_bias: float32 [768], P(('ctx', 'fsdp'))
- grad_gain2: float32 [768], P(('ctx', 'fsdp'))
- grad_bias2: float32 [768], P(('ctx', 'fsdp'))
The draws below stay inside these ranges and needn't reach their ends.
Inputs may be any that keep to these rules, and one draw needn't show every extreme that they name: `doc_ids`: within a pool, ids 0 to 3 name documents and id 4 marks empty slots; one document has exactly 1024 slots, every other at least one, 1344 slots hold documents. The pool's slots are made of blocks of 48 consecutive slots, each holding consecutive positions of the packed documents, in an order drawn from the seed.
All inputs are finite; a program needn't handle non-finite values. No bound on the sum of `keep_mask` on one device may be relied on, other than what follows from the above.
Results may differ from the reference program's by a relative error of at most 0.025.
Values may be sent and summed in bfloat16 or wider, within the bound.
No kernel may reach another device: no remote copies, remote signals or barrier semaphores. Data moves between devices by JAX's collectives and lax.ppermute only.
A program may use at most 192 MiB of HBM per device.

```python
import jax
import jax.numpy as jnp
from jax import lax

D = 768
H = 12
FF = 3072
MB = 2
NDOC = 4
BLK = 48
ROWS = 1536
POOLS = 4
QBLK = 512
LONGEST = 1024
VALID = 1344


def draw_doc_ids(key, part):

    def one_pool(pool_key):
        key_lengths, key_order, key_deal = jax.random.split(pool_key, 3)
        spare_slots = VALID - LONGEST - (NDOC - 1)
        cut_points = jnp.sort(jax.random.randint(key_lengths, (NDOC - 2,), 0, spare_slots + 1, dtype=jnp.int32))
        edge_points = jnp.concatenate([jnp.zeros((1,), jnp.int32), cut_points, jnp.full((1,), spare_slots, jnp.int32)])
        others = edge_points[1:] - edge_points[:-1] + 1
        lengths = jnp.concatenate([jnp.full((1,), LONGEST, jnp.int32), others])
        lengths = jax.random.permutation(key_order, lengths)
        bounds = jnp.cumsum(lengths).astype(jnp.int32)
        places = jnp.arange(ROWS, dtype=jnp.int32)
        labels = jnp.sum((places[:, None] >= bounds[None, :]).astype(jnp.int32), axis=1)
        block_order = jax.random.permutation(key_deal, ROWS // BLK)
        return labels.reshape(ROWS // BLK, BLK)[block_order].reshape(ROWS)
    pool_keys = jax.random.split(key, MB * POOLS)
    return jax.vmap(one_pool)(pool_keys).reshape(MB, POOLS, ROWS).astype(jnp.int32)


def plant(drawn, stream_key, least, largest):
    shape = drawn.shape
    spot = [jax.random.randint(jax.random.fold_in(stream_key, axis), (), 0, shape[axis]) for axis in range(len(shape))]
    drawn = drawn.at[tuple(spot)].set(least)
    longest = shape.index(max(shape))
    spot[longest] = (spot[longest] + 1) % shape[longest]
    return drawn.at[tuple(spot)].set(largest)


def strengthened(drawn, rng, source, target, parts, factor):
    owner, partner = [(jnp.arange(drawn.shape[position]) // (drawn.shape[position] // parts)).reshape([-1 if axis == position else 1 for axis in range(drawn.ndim)]) for position in (source, target)]
    chosen = jax.random.permutation(rng, parts)[partner]
    strong = (owner == chosen) | (owner == (partner + parts // 2) % parts)
    return jnp.where(strong, factor * drawn, drawn)


def level_of(key, shape, pieces, low, high):
    gain, own = 1.0, jax.random.fold_in(key, 6)
    for axis_at, shards_of in pieces:
        steps = jnp.exp(jax.random.uniform(jax.random.fold_in(own, axis_at), (shards_of,), jnp.float32, low / len(pieces), high / len(pieces)))
        gain = gain * jnp.repeat(steps, shape[axis_at] // shards_of).reshape([-1 if axis == axis_at else 1 for axis in range(len(shape))])
    return gain


def gaussian(key, shape, scale, reach, cuts=(), held_as=jnp.bfloat16):
    level = level_of(key, shape, cuts, -0.22, 0.18) if cuts else 1.0
    entries = jax.random.normal(key, shape, jnp.float32) * scale * level
    return jnp.minimum(jnp.maximum(entries, -reach), reach).astype(held_as)


def gaussian_with(rng, shape, deviation, reach, cuts, heavy, kind=jnp.bfloat16):
    drawn = deviation * jax.random.normal(rng, shape, jnp.float32)
    if cuts:
        drawn = drawn * level_of(rng, shape, cuts, -0.22, 0.18)
    return jnp.clip(strengthened(drawn, jax.random.fold_in(rng, 3), *heavy), -reach, reach).astype(kind)


def setup_inputs(seed: int = 0) -> dict:
    streams_of = jax.random.split(jax.random.key(seed), 18)
    tokens = gaussian(streams_of[0], (MB, POOLS, ROWS, D), 1.0, 6.0, ((1, 4), (2, 8)))
    doc_ids = draw_doc_ids(jax.random.fold_in(streams_of[17], 71), 0)
    keep_mask = plant((jax.random.randint(streams_of[2], (MB, POOLS, NDOC), 0, 4) < 3).astype(jnp.int32), jax.random.fold_in(streams_of[2], 1), 0, 1)
    qkv_weight = gaussian(streams_of[3], (D, 3 * D), (D // 2) ** -0.5, 0.3125, ((0, 4),))
    query_bias = gaussian(streams_of[4], (D,), 0.5, 3.0, ((0, 4),))
    value_bias = gaussian(streams_of[5], (D,), 0.05, 0.29882812, ((0, 4),))
    proj_weight = gaussian(streams_of[6], (D, D), (D // 32) ** -0.5, 1.25, ((0, 4),))
    proj_bias = gaussian(streams_of[7], (D,), 0.3, 2.0, ((0, 4),))
    norm1_gain = jnp.clip(1.0 + 0.1 * jax.random.normal(streams_of[8], (D,), jnp.float32), 0.5, 1.5).astype(jnp.bfloat16)
    norm1_bias = gaussian(streams_of[9], (D,), 0.5, 3.0, ((0, 4),))
    up_weight = gaussian(streams_of[10], (D, FF), D ** -0.5, 0.21875, ((0, 4),))
    up_bias = gaussian(streams_of[11], (FF,), 0.5, 3.0, ((0, 4),))
    down_weight = gaussian(streams_of[12], (FF, D), FF ** -0.5, 0.109375, ((0, 4),))
    down_bias = gaussian(streams_of[13], (D,), 0.5, 3.0, ((0, 4),))
    norm2_gain = jnp.clip(1.0 + 0.1 * jax.random.normal(streams_of[14], (D,), jnp.float32), 0.5, 1.5).astype(jnp.bfloat16)
    norm2_bias = gaussian(streams_of[15], (D,), 0.5, 3.0, ((0, 4),))
    cotangent = gaussian_with(streams_of[16], (MB, POOLS, ROWS, D), 1.0, 6.0, ((1, 4), (2, 8)), (2, 3, 8, 2.0))
    return {"tokens": tokens, "doc_ids": doc_ids, "keep_mask": keep_mask, "qkv_weight": qkv_weight, "query_bias": query_bias, "value_bias": value_bias, "proj_weight": proj_weight, "proj_bias": proj_bias, "norm1_gain": norm1_gain, "norm1_bias": norm1_bias, "up_weight": up_weight, "up_bias": up_bias, "down_weight": down_weight, "down_bias": down_bias, "norm2_gain": norm2_gain, "norm2_bias": norm2_bias, "cotangent": cotangent}


epsilon = 1e-05
score_scale = 0.125
masked_score = -1e+30
highest = lax.Precision.HIGHEST

@jax.custom_vjp
def low(v):
    return lax.optimization_barrier(v.astype(jnp.bfloat16)).astype(jnp.float32)

@jax.custom_vjp
def low_back(v):
    return v

def low_keep(v):
    return (low(v), None)

def low_pass(kept, grad):
    return (grad,)

def back_keep(v):
    return (v, None)

def back_low(kept, grad):
    return (low(grad),)
low.defvjp(low_keep, low_pass)
low_back.defvjp(back_keep, back_low)

def both_ways(values):
    return low(low_back(values))

def layer_norm(values, gain_vec, offset_vec):
    centre = lax.optimization_barrier(jnp.mean(values, axis=-1, keepdims=True))
    centred = values - centre
    spread = lax.optimization_barrier(jnp.mean(centred * centred, axis=-1, keepdims=True))
    return centred * lax.rsqrt(spread + epsilon) * gain_vec + offset_vec

def heads_first(values):
    return values.reshape(ROWS, H, D // H).transpose(1, 0, 2)

def attention_block(query_block, label_block, key_heads, value_heads, labels):
    scores = jnp.einsum('hqd,hkd->hqk', query_block, key_heads, precision=highest) * score_scale
    scores = low_back(scores)
    same_doc = (label_block[:, None] == labels[None, :])[None]
    scores = jnp.where(same_doc, scores, masked_score)
    probs = jax.nn.softmax(scores, axis=-1)
    return jnp.einsum('hqk,hkd->hqd', low(probs), value_heads, precision=highest)

def layer(weights, pool_rows, labels, keep_rows):
    qkv_weight, query_bias, value_bias, proj_weight, proj_bias, norm1_gain, norm1_bias, up_weight, up_bias, down_weight, down_bias, norm2_gain, norm2_bias = weights
    projected = jnp.dot(pool_rows, qkv_weight, precision=highest, preferred_element_type=jnp.float32)
    query_rows = both_ways(projected[:, :D] + query_bias)
    key_rows = both_ways(projected[:, D:2 * D])
    value_rows = both_ways(projected[:, 2 * D:] + value_bias)
    key_heads = heads_first(key_rows)
    value_heads = heads_first(value_rows)
    block_count = ROWS // QBLK
    query_blocks = heads_first(query_rows).reshape(H, block_count, QBLK, D // H).transpose(1, 0, 2, 3)
    label_blocks = labels.reshape(block_count, QBLK)

    def one_block(block_pair):
        return attention_block(block_pair[0], block_pair[1], key_heads, value_heads, labels)
    attended = lax.map(jax.checkpoint(one_block), (query_blocks, label_blocks))
    attended = both_ways(attended.transpose(0, 2, 1, 3).reshape(ROWS, D))
    projection = low_back(jnp.dot(attended, proj_weight, precision=highest, preferred_element_type=jnp.float32) + proj_bias)
    hidden = layer_norm(pool_rows + projection, norm1_gain, norm1_bias)
    inner_rows = low_back(jnp.dot(low(hidden), up_weight, precision=highest, preferred_element_type=jnp.float32) + up_bias)
    active = low(jax.nn.gelu(inner_rows, approximate=False))
    branch = low_back(jnp.dot(active, down_weight, precision=highest, preferred_element_type=jnp.float32) + down_bias)
    result = layer_norm(hidden + branch, norm2_gain, norm2_bias)
    return keep_rows * result + (1.0 - keep_rows) * pool_rows

def reference(tokens, doc_ids, keep_mask, qkv_weight, query_bias, value_bias, proj_weight, proj_bias, norm1_gain, norm1_bias, up_weight, up_bias, down_weight, down_bias, norm2_gain, norm2_bias, cotangent):
    weights = (qkv_weight.astype(jnp.float32), query_bias.astype(jnp.float32), value_bias.astype(jnp.float32), proj_weight.astype(jnp.float32), proj_bias.astype(jnp.float32), norm1_gain.astype(jnp.float32), norm1_bias.astype(jnp.float32), up_weight.astype(jnp.float32), up_bias.astype(jnp.float32), down_weight.astype(jnp.float32), down_bias.astype(jnp.float32), norm2_gain.astype(jnp.float32), norm2_bias.astype(jnp.float32))
    pool_count = MB * POOLS
    token_pools = tokens.astype(jnp.float32).reshape(pool_count, ROWS, D)
    label_pools = doc_ids.reshape(pool_count, ROWS)
    keep_pools = keep_mask.reshape(pool_count, NDOC)
    grad_pools = cotangent.astype(jnp.float32).reshape(pool_count, ROWS, D)
    documents = jnp.arange(NDOC, dtype=jnp.int32)

    def one_pool(summed, inputs):
        pool_rows, labels, keep_flags, grad_rows = inputs
        keep_rows = lax.optimization_barrier(jnp.sum(jnp.where(labels[:, None] == documents[None, :], keep_flags[None, :], 0), axis=1)).astype(jnp.float32)[:, None]

        def forward_pass(params, values):
            return layer(params, values, labels, keep_rows)
        output, backward = jax.vjp(forward_pass, weights, pool_rows)
        grad_weights, grad_input = backward(grad_rows)
        summed = jax.tree.map(jnp.add, summed, grad_weights)
        return (summed, (output.astype(jnp.bfloat16), grad_input))
    zero_grads = tuple((jnp.zeros_like(weight) for weight in weights))
    summed, (outputs, grad_inputs) = lax.scan(one_pool, zero_grads, (token_pools, label_pools, keep_pools, grad_pools))
    return (outputs.reshape(MB, POOLS, ROWS, D), grad_inputs.reshape(MB, POOLS, ROWS, D), summed[0], summed[1], summed[2], summed[3], summed[4], summed[5], summed[6], summed[7], summed[8], summed[9], summed[10], summed[11], summed[12])
```

```python
import math

import jax
import jax.numpy as jnp
from jax import lax
from jax.experimental import pallas as pl
from jax.experimental.pallas import tpu as pltpu
from jax.sharding import PartitionSpec as P

H = 12
NDOC = 4


epsilon = 1e-05
score_scale = 0.125
masked_score = -1e30


def layer_norm(values, gain_vec, offset_vec):
    centre = jnp.mean(values, axis=-1, keepdims=True)
    centred = values - centre
    spread = jnp.mean(centred * centred, axis=-1, keepdims=True)
    return centred * lax.rsqrt(spread + epsilon) * gain_vec + offset_vec


def exact_gelu(values):
    return jax.nn.gelu(values, approximate=False)


def in_blocks(stepper, carried, portion, shard_rows):
    total_rows = portion[0].shape[0]
    shard_count = total_rows // shard_rows
    limit_rows = max(1, 1024 // shard_rows)
    grouped = math.gcd(shard_count, 1 << limit_rows.bit_length() - 1)
    block_rows = grouped * shard_rows
    turn_count = total_rows // block_rows
    stacked = tuple(
        (member.reshape((turn_count, block_rows) + member.shape[1:]) for member in portion)
    )
    offsets = block_rows * jnp.arange(turn_count, dtype=jnp.int32)

    def one_turn(inner_state, element):
        return (stepper(inner_state, element[0], element[1]), None)

    carried, ignored = lax.scan(one_turn, carried, (stacked, offsets))
    return carried


def micro_step(token_rows, slot_ids, keep_flags, weights_full, grad_rows):
    (
        qkv_weight,
        query_bias,
        value_bias,
        proj_weight,
        proj_bias,
        norm1_gain,
        norm1_bias,
        up_weight,
        up_bias,
        down_weight,
        down_bias,
        norm2_gain,
        norm2_bias,
    ) = weights_full
    local_rows, features = token_rows.shape
    num_heads = H
    head_size = features // num_heads
    documents = jnp.arange(NDOC, dtype=jnp.int32)
    keep_rows = jnp.sum(
        jnp.where(slot_ids[:, None] == documents[None, :], keep_flags[None, :], 0), axis=1
    ).astype(jnp.float32)[:, None]
    token_float = token_rows.astype(jnp.float32)
    slot_labels = slot_ids.astype(jnp.float32).astype(jnp.bfloat16)
    projected = jnp.dot(token_rows, qkv_weight, preferred_element_type=jnp.float32)
    query_rows = (projected[:, :features] + query_bias.astype(jnp.float32)).astype(jnp.bfloat16)
    key_rows = projected[:, features : 2 * features].astype(jnp.bfloat16)
    value_rows = (projected[:, 2 * features :] + value_bias.astype(jnp.float32)).astype(
        jnp.bfloat16
    )
    query_heads = query_rows.reshape(local_rows, num_heads, head_size)
    key_heads_local = key_rows.reshape(local_rows, num_heads, head_size)
    value_heads_local = value_rows.reshape(local_rows, num_heads, head_size)

    def forward_step(carried, portion, offset):
        key_part, value_part, id_part = portion
        running_max, running_sum, running_out = carried
        scores = (
            jnp.einsum(
                "qhd,khd->hqk",
                query_heads,
                key_part.reshape(-1, num_heads, head_size),
                preferred_element_type=jnp.float32,
            )
            * score_scale
        )
        same_doc = (slot_labels[:, None] == id_part[None, :])[None]
        scores = jnp.where(same_doc, scores, masked_score)
        new_max = jnp.maximum(running_max, jnp.max(scores, axis=-1))
        factor = jnp.exp(running_max - new_max)
        weights = jnp.where(same_doc, jnp.exp(scores - new_max[..., None]), 0.0)
        running_sum = running_sum * factor + jnp.sum(weights, axis=-1)
        running_out = running_out * factor[..., None] + jnp.einsum(
            "hqk,khd->hqd",
            weights.astype(jnp.bfloat16),
            value_part.reshape(-1, num_heads, head_size),
            preferred_element_type=jnp.float32,
        )
        return (new_max, running_sum, running_out)

    start_state = (
        jnp.full((num_heads, local_rows), masked_score, jnp.float32),
        jnp.zeros((num_heads, local_rows), jnp.float32),
        jnp.zeros((num_heads, local_rows, head_size), jnp.float32),
    )
    running_max, running_sum, running_out = in_blocks(
        forward_step,
        start_state,
        (
            lax.all_gather(key_rows, "ctx", axis=0, tiled=True),
            lax.all_gather(value_rows, "ctx", axis=0, tiled=True),
            lax.all_gather(slot_labels, "ctx", axis=0, tiled=True),
        ),
        local_rows,
    )
    attended = jnp.transpose(running_out / running_sum[..., None], (1, 0, 2))
    log_total = running_max + jnp.log(running_sum)
    attended_low = attended.reshape(local_rows, features).astype(jnp.bfloat16)
    projection = jnp.dot(
        attended_low, proj_weight, preferred_element_type=jnp.float32
    ) + proj_bias.astype(jnp.float32)
    hidden, norm1_back = jax.vjp(
        layer_norm,
        token_float + projection,
        norm1_gain.astype(jnp.float32),
        norm1_bias.astype(jnp.float32),
    )
    hidden_low = hidden.astype(jnp.bfloat16)
    inner_rows = jnp.dot(
        hidden_low, up_weight, preferred_element_type=jnp.float32
    ) + up_bias.astype(jnp.float32)
    active, gelu_back = jax.vjp(exact_gelu, inner_rows)
    active_low = active.astype(jnp.bfloat16)
    branch = jnp.dot(
        active_low, down_weight, preferred_element_type=jnp.float32
    ) + down_bias.astype(jnp.float32)
    result, norm2_back = jax.vjp(
        layer_norm, hidden + branch, norm2_gain.astype(jnp.float32), norm2_bias.astype(jnp.float32)
    )
    block_rows = (keep_rows * result + (1.0 - keep_rows) * token_float).astype(jnp.bfloat16)
    grad_float = grad_rows.astype(jnp.float32)
    grad_sum, grad_gain2, grad_bias2 = norm2_back(keep_rows * grad_float)
    grad_branch = grad_sum.astype(jnp.bfloat16)
    grad_down = jnp.einsum("rf,rd->fd", active_low, grad_branch, preferred_element_type=jnp.float32)
    grad_down_bias = jnp.sum(grad_branch.astype(jnp.float32), axis=0)
    (grad_inner,) = gelu_back(
        jnp.einsum("rd,fd->rf", grad_branch, down_weight, preferred_element_type=jnp.float32)
    )
    grad_inner_low = grad_inner.astype(jnp.bfloat16)
    grad_up = jnp.einsum(
        "rd,rf->df", hidden_low, grad_inner_low, preferred_element_type=jnp.float32
    )
    grad_up_bias = jnp.sum(grad_inner_low.astype(jnp.float32), axis=0)
    grad_hidden = grad_sum + jnp.einsum(
        "rf,df->rd", grad_inner_low, up_weight, preferred_element_type=jnp.float32
    )
    grad_mixed, grad_gain1, grad_bias1 = norm1_back(grad_hidden)
    grad_proj_low = grad_mixed.astype(jnp.bfloat16)
    grad_proj = jnp.einsum(
        "re,rd->ed", attended_low, grad_proj_low, preferred_element_type=jnp.float32
    )
    grad_proj_bias = jnp.sum(grad_proj_low.astype(jnp.float32), axis=0)
    grad_attended = jnp.einsum(
        "rd,ed->re", grad_proj_low, proj_weight, preferred_element_type=jnp.float32
    ).astype(jnp.bfloat16)
    grad_heads = grad_attended.reshape(local_rows, num_heads, head_size)
    row_delta = jnp.transpose(jnp.sum(grad_heads.astype(jnp.float32) * attended, axis=-1))

    def query_step(carried, portion, offset):
        key_part, value_part, id_part = portion
        key_heads = key_part.reshape(-1, num_heads, head_size)
        scores = (
            jnp.einsum("qhd,khd->hqk", query_heads, key_heads, preferred_element_type=jnp.float32)
            * score_scale
        )
        same_doc = (slot_labels[:, None] == id_part[None, :])[None]
        scores = jnp.where(same_doc, scores, masked_score)
        probs = jnp.where(same_doc, jnp.exp(scores - log_total[..., None]), 0.0)
        grad_probs = jnp.einsum(
            "qhd,khd->hqk",
            grad_heads,
            value_part.reshape(-1, num_heads, head_size),
            preferred_element_type=jnp.float32,
        )
        grad_scores = (probs * (grad_probs - row_delta[..., None])).astype(jnp.bfloat16)
        return carried + jnp.einsum(
            "hqk,khd->qhd", grad_scores, key_heads, preferred_element_type=jnp.float32
        )

    grad_query_sum = in_blocks(
        query_step,
        jnp.zeros((local_rows, num_heads, head_size), jnp.float32),
        (
            lax.all_gather(key_rows, "ctx", axis=0, tiled=True),
            lax.all_gather(value_rows, "ctx", axis=0, tiled=True),
            lax.all_gather(slot_labels, "ctx", axis=0, tiled=True),
        ),
        local_rows,
    )
    log_rows, delta_rows = (
        lax.all_gather(jnp.transpose(log_total), "ctx", axis=0, tiled=True),
        lax.all_gather(jnp.transpose(row_delta), "ctx", axis=0, tiled=True),
    )

    def key_step(carried, portion, offset):
        query_part, grad_part, id_part = portion
        grad_key_sum, grad_value_sum = carried
        span_rows = query_part.shape[0]
        log_part = lax.dynamic_slice_in_dim(log_rows, offset, span_rows, 0)
        delta_part = lax.dynamic_slice_in_dim(delta_rows, offset, span_rows, 0)
        query_part_heads = query_part.reshape(-1, num_heads, head_size)
        grad_part_heads = grad_part.reshape(-1, num_heads, head_size)
        scores = (
            jnp.einsum(
                "qhd,khd->hqk",
                query_part_heads,
                key_heads_local,
                preferred_element_type=jnp.float32,
            )
            * score_scale
        )
        same_doc = (id_part[:, None] == slot_labels[None, :])[None]
        scores = jnp.where(same_doc, scores, masked_score)
        probs = jnp.where(same_doc, jnp.exp(scores - jnp.transpose(log_part)[..., None]), 0.0)
        grad_value_sum = grad_value_sum + jnp.einsum(
            "hqk,qhd->khd",
            probs.astype(jnp.bfloat16),
            grad_part_heads,
            preferred_element_type=jnp.float32,
        )
        grad_probs = jnp.einsum(
            "qhd,khd->hqk", grad_part_heads, value_heads_local, preferred_element_type=jnp.float32
        )
        grad_scores = (probs * (grad_probs - jnp.transpose(delta_part)[..., None])).astype(
            jnp.bfloat16
        )
        grad_key_sum = grad_key_sum + jnp.einsum(
            "hqk,qhd->khd", grad_scores, query_part_heads, preferred_element_type=jnp.float32
        )
        return (grad_key_sum, grad_value_sum)

    zero_heads = jnp.zeros((local_rows, num_heads, head_size), jnp.float32)
    grad_key_sum, grad_value_sum = in_blocks(
        key_step,
        (zero_heads, zero_heads),
        (
            lax.all_gather(query_rows, "ctx", axis=0, tiled=True),
            lax.all_gather(grad_attended, "ctx", axis=0, tiled=True),
            lax.all_gather(slot_labels, "ctx", axis=0, tiled=True),
        ),
        local_rows,
    )
    grad_query = (grad_query_sum * score_scale).reshape(local_rows, features).astype(jnp.bfloat16)
    grad_key = (grad_key_sum * score_scale).reshape(local_rows, features).astype(jnp.bfloat16)
    grad_value = grad_value_sum.reshape(local_rows, features).astype(jnp.bfloat16)
    grad_projected = jnp.concatenate([grad_query, grad_key, grad_value], axis=1)
    grad_qkv = jnp.einsum(
        "rd,re->de", token_rows, grad_projected, preferred_element_type=jnp.float32
    )
    grad_query_bias = jnp.sum(grad_query.astype(jnp.float32), axis=0)
    grad_value_bias = jnp.sum(grad_value.astype(jnp.float32), axis=0)
    grad_input = grad_mixed + jnp.einsum(
        "re,de->rd", grad_projected, qkv_weight, preferred_element_type=jnp.float32
    )
    grad_tokens = keep_rows * grad_input + (1.0 - keep_rows) * grad_float
    terms = (
        grad_qkv,
        grad_query_bias,
        grad_value_bias,
        grad_proj,
        grad_proj_bias,
        grad_gain1,
        grad_bias1,
        grad_up,
        grad_up_bias,
        grad_down,
        grad_down_bias,
        grad_gain2,
        grad_bias2,
    )
    return (block_rows, grad_tokens, terms)


def on_device(
    tokens,
    doc_ids,
    keep_mask,
    qkv_weight,
    query_bias,
    value_bias,
    proj_weight,
    proj_bias,
    norm1_gain,
    norm1_bias,
    up_weight,
    up_bias,
    down_weight,
    down_bias,
    norm2_gain,
    norm2_bias,
    cotangent,
):
    block_list = []
    grad_list = []
    summed = None
    for micro_index in range(tokens.shape[0]):
        weights_full = (
            lax.all_gather(qkv_weight, "fsdp", axis=0, tiled=True),
            lax.all_gather(query_bias, "fsdp", axis=0, tiled=True),
            lax.all_gather(value_bias, "fsdp", axis=0, tiled=True),
            lax.all_gather(proj_weight, "fsdp", axis=0, tiled=True),
            lax.all_gather(proj_bias, "fsdp", axis=0, tiled=True),
            lax.all_gather(norm1_gain, "fsdp", axis=0, tiled=True),
            lax.all_gather(norm1_bias, "fsdp", axis=0, tiled=True),
            lax.all_gather(up_weight, "fsdp", axis=0, tiled=True),
            lax.all_gather(up_bias, "fsdp", axis=0, tiled=True),
            lax.all_gather(down_weight, "fsdp", axis=0, tiled=True),
            lax.all_gather(down_bias, "fsdp", axis=0, tiled=True),
            lax.all_gather(norm2_gain, "fsdp", axis=0, tiled=True),
            lax.all_gather(norm2_bias, "fsdp", axis=0, tiled=True),
        )
        block_rows, grad_tokens, terms = micro_step(
            tokens[micro_index, 0],
            doc_ids[micro_index, 0],
            keep_mask[micro_index, 0],
            weights_full,
            cotangent[micro_index, 0],
        )
        block_list.append(block_rows)
        grad_list.append(grad_tokens)
        if summed is None:
            summed = terms
        else:
            summed = tuple((earlier + later for earlier, later in zip(summed, terms)))
    reduced = (
        lax.psum_scatter(summed[0], ("ctx", "fsdp"), scatter_dimension=0, tiled=True),
        lax.psum_scatter(summed[1], ("ctx", "fsdp"), scatter_dimension=0, tiled=True),
        lax.psum_scatter(summed[2], ("ctx", "fsdp"), scatter_dimension=0, tiled=True),
        lax.psum_scatter(summed[3], ("ctx", "fsdp"), scatter_dimension=0, tiled=True),
        lax.psum_scatter(summed[4], ("ctx", "fsdp"), scatter_dimension=0, tiled=True),
        lax.psum_scatter(summed[5], ("ctx", "fsdp"), scatter_dimension=0, tiled=True),
        lax.psum_scatter(summed[6], ("ctx", "fsdp"), scatter_dimension=0, tiled=True),
        lax.psum_scatter(summed[7], ("ctx", "fsdp"), scatter_dimension=0, tiled=True),
        lax.psum_scatter(summed[8], ("ctx", "fsdp"), scatter_dimension=0, tiled=True),
        lax.psum_scatter(summed[9], ("ctx", "fsdp"), scatter_dimension=0, tiled=True),
        lax.psum_scatter(summed[10], ("ctx", "fsdp"), scatter_dimension=0, tiled=True),
        lax.psum_scatter(summed[11], ("ctx", "fsdp"), scatter_dimension=0, tiled=True),
        lax.psum_scatter(summed[12], ("ctx", "fsdp"), scatter_dimension=0, tiled=True),
    )
    block_out = jnp.stack(block_list)[:, None]
    grad_tokens_all = jnp.stack(grad_list)[:, None]
    return (
        block_out,
        grad_tokens_all,
        reduced[0],
        reduced[1],
        reduced[2],
        reduced[3],
        reduced[4],
        reduced[5],
        reduced[6],
        reduced[7],
        reduced[8],
        reduced[9],
        reduced[10],
        reduced[11],
        reduced[12],
    )


MASKED = -1e30
LOWEST = -3e38
ARRIVAL = (0, 4, 2, 6, 1, 5, 3, 7)
GROUP = 192
HEAD = 64
HEADS_EACH = 3
PAIR = 384
ID_ROWS = 8


def fits(mesh):
    return mesh.shape["ctx"] == 8 and mesh.shape["fsdp"] == 4


def dot(a, b):
    return lax.dot_general(a, b, (((1,), (0,)), ((), ())), preferred_element_type=jnp.float32)


def flip(value):
    return jnp.transpose(value.astype(jnp.float32))


def split3(value):
    high = value.astype(jnp.bfloat16)
    rest = value - high.astype(jnp.float32)
    mid = rest.astype(jnp.bfloat16)
    low = (rest - mid.astype(jnp.float32)).astype(jnp.bfloat16)
    return high, mid, low


def attend_kernel(place, *refs):
    x_refs = refs[:8]
    w_ref, qb_ref, vb_ref = refs[8:11]
    o_ref, qt_ref, ka_ref, kt_ref, va_ref, qn_ref, xs_ref = refs[11:18]
    vt_ref, ot_ref = refs[18:]
    me = place[0]
    wq = w_ref[:, 0:GROUP]
    wk = w_ref[:, GROUP : 2 * GROUP]
    wv = w_ref[:, 2 * GROUP :]
    lane = lax.broadcasted_iota(jnp.int32, (PAIR, HEAD), 1)
    row = lax.broadcasted_iota(jnp.int32, (HEAD, PAIR), 0)
    for t in range(4):
        first, second = x_refs[2 * t], x_refs[2 * t + 1]
        span = slice(t * PAIR, (t + 1) * PAIR)
        x = jnp.concatenate([first[0:GROUP, :], second[0:GROUP, :]], axis=0)
        xs_ref[span, :] = x
        ids = jnp.concatenate(
            [first[GROUP : GROUP + 8, 0:GROUP], second[GROUP : GROUP + 8, 0:GROUP]], axis=1
        ).astype(jnp.float32)
        id_row = ids[0:1, :]
        id_col = jnp.transpose(ids)[:, 0:1]
        q = ((dot(x, wq) + qb_ref[...]).astype(jnp.bfloat16) * 0.125).astype(jnp.bfloat16)
        k = dot(x, wk).astype(jnp.bfloat16)
        v = (dot(x, wv) + vb_ref[...]).astype(jnp.bfloat16)
        qn_ref[span, :] = q
        q_t = flip(q).astype(jnp.bfloat16)
        k_t = flip(k).astype(jnp.bfloat16)
        v_t = flip(v).astype(jnp.bfloat16)
        kt_ref[:, span] = k_t
        vt_ref[:, span] = v_t
        k_side = jnp.where(
            lane < 5,
            jnp.where(id_col == lane.astype(jnp.float32), 0.0, MASKED),
            jnp.where(lane < 8, -1.0, 0.0),
        ).astype(jnp.bfloat16)
        v_side = jnp.where(lane < 3, -1.0, 0.0).astype(jnp.bfloat16)
        q_side = jnp.where((row < 5) & (id_row == row.astype(jnp.float32)), 1.0, 0.0).astype(
            jnp.bfloat16
        )
        for h in range(HEADS_EACH):
            cols = slice(h * HEAD, (h + 1) * HEAD)
            ka_ref[h, span, :] = jnp.concatenate([k[:, cols], k_side], axis=1)
            va_ref[h, span, :] = jnp.concatenate([v[:, cols], v_side], axis=1)
            qt_ref[h, 0:HEAD, span] = q_t[cols, :]
            qt_ref[h, HEAD : 2 * HEAD, span] = q_side

    def one_tile(t, unused):
        at = pl.multiple_of(t * PAIR, PAIR)
        for h in range(HEADS_EACH):
            q_tile = qt_ref[h, :, pl.ds(at, PAIR)]
            top = jnp.full((1, PAIR), LOWEST, jnp.float32)
            total = jnp.zeros((1, PAIR), jnp.float32)
            out = jnp.zeros((HEAD, PAIR), jnp.float32)
            for j in range(4):
                span = slice(j * PAIR, (j + 1) * PAIR)
                scores = dot(ka_ref[h, span, :], q_tile)
                new_top = jnp.maximum(top, jnp.max(scores, axis=0, keepdims=True))
                probs = jnp.exp(scores - new_top)
                factor = jnp.exp(top - new_top)
                total = total * factor + jnp.sum(probs, axis=0, keepdims=True)
                out = out * factor + dot(
                    vt_ref[h * HEAD : (h + 1) * HEAD, span], probs.astype(jnp.bfloat16)
                )
                top = new_top
            ot_ref[h * HEAD : (h + 1) * HEAD, :] = out / total
            high, mid, low = split3(top + jnp.log(total))
            side = qt_ref[h, HEAD : HEAD + 16, pl.ds(at, PAIR)].astype(jnp.float32)
            at_row = lax.broadcasted_iota(jnp.int32, (16, PAIR), 0)
            side = jnp.where(at_row == 5, high.astype(jnp.float32), side)
            side = jnp.where(at_row == 6, mid.astype(jnp.float32), side)
            side = jnp.where(at_row == 7, low.astype(jnp.float32), side)
            qt_ref[h, HEAD : HEAD + 16, pl.ds(at, PAIR)] = side.astype(jnp.bfloat16)
        rows = jnp.transpose(ot_ref[...]).astype(jnp.bfloat16)
        for half in range(2):
            k_bits = place[2 + 2 * t + half]
            o_ref[me ^ k_bits, :, :] = rows[half * GROUP : (half + 1) * GROUP, :]
        return unused

    lax.fori_loop(0, 4, one_tile, 0)


def attend_back_kernel(place, o_ref, do_ref, qt_ref, ka_ref, kt_ref, va_ref, qn_ref, g_ref, *scratch):
    dot_t, don, dqt = scratch
    me = place[0]
    row = lax.broadcasted_iota(jnp.int32, (HEAD, PAIR), 0)

    def load(t, unused):
        at = pl.multiple_of(t * PAIR, PAIR)
        a, b = me ^ place[2 + 2 * t], me ^ place[3 + 2 * t]
        grad = jnp.concatenate([do_ref[a], do_ref[b]], axis=0)
        out = jnp.concatenate([o_ref[a], o_ref[b]], axis=0)
        don[pl.ds(at, PAIR), :] = grad
        grad_t = flip(grad)
        out_t = flip(out)
        for h in range(HEADS_EACH):
            cols = slice(h * HEAD, (h + 1) * HEAD)
            delta = jnp.sum(grad_t[cols] * out_t[cols], axis=0, keepdims=True)
            high, mid, low = split3(delta)
            side = jnp.where(
                row == 0,
                high.astype(jnp.float32),
                jnp.where(
                    row == 1,
                    mid.astype(jnp.float32),
                    jnp.where(row == 2, low.astype(jnp.float32), 0.0),
                ),
            )
            dot_t[h, 0:HEAD, pl.ds(at, PAIR)] = grad_t[cols].astype(jnp.bfloat16)
            dot_t[h, HEAD : 2 * HEAD, pl.ds(at, PAIR)] = side.astype(jnp.bfloat16)
        return unused

    lax.fori_loop(0, 4, load, 0)
    dqt[...] = jnp.zeros_like(dqt)

    def keys(j, unused):
        at = pl.multiple_of(j * PAIR, PAIR)
        dks, dvs = [], []
        for h in range(HEADS_EACH):
            cols = slice(h * HEAD, (h + 1) * HEAD)
            key = ka_ref[h, pl.ds(at, PAIR), :]
            val = va_ref[h, pl.ds(at, PAIR), :]
            key_t = kt_ref[cols, pl.ds(at, PAIR)]
            dk = jnp.zeros((PAIR, HEAD), jnp.float32)
            dv = jnp.zeros((PAIR, HEAD), jnp.float32)
            for i in range(4):
                span = slice(i * PAIR, (i + 1) * PAIR)
                probs = jnp.exp(dot(key, qt_ref[h, :, span]))
                grad_probs = dot(val, dot_t[h, :, span])
                grad_scores = (probs * grad_probs).astype(jnp.bfloat16)
                dv = dv + dot(probs.astype(jnp.bfloat16), don[span, cols])
                dk = dk + dot(grad_scores, qn_ref[span, cols])
                dqt[cols, span] = dqt[cols, span] + dot(key_t, grad_scores)
            dks.append(dk)
            dvs.append(dv)
        g_ref[pl.ds(at, PAIR), GROUP : 2 * GROUP] = jnp.concatenate(dks, axis=1).astype(jnp.bfloat16)
        g_ref[pl.ds(at, PAIR), 2 * GROUP :] = jnp.concatenate(dvs, axis=1).astype(jnp.bfloat16)
        return unused

    lax.fori_loop(0, 4, keys, 0)
    for t in range(4):
        span = slice(t * PAIR, (t + 1) * PAIR)
        g_ref[span, 0:GROUP] = (jnp.transpose(dqt[:, span]) * 0.125).astype(jnp.bfloat16)


def in_vmem(count):
    return [pl.BlockSpec(memory_space=pltpu.VMEM)] * count


def attend(place, chunks, w, q_bias, v_bias):
    slots = 8 * GROUP
    low = jnp.bfloat16
    return pl.pallas_call(
        attend_kernel,
        name="attend",
        out_shape=(
            jax.ShapeDtypeStruct((8, GROUP, GROUP), low),
            jax.ShapeDtypeStruct((HEADS_EACH, 2 * HEAD, slots), low),
            jax.ShapeDtypeStruct((HEADS_EACH, slots, 2 * HEAD), low),
            jax.ShapeDtypeStruct((GROUP, slots), low),
            jax.ShapeDtypeStruct((HEADS_EACH, slots, 2 * HEAD), low),
            jax.ShapeDtypeStruct((slots, GROUP), low),
            jax.ShapeDtypeStruct((slots, 4 * GROUP), low),
        ),
        grid_spec=pltpu.PrefetchScalarGridSpec(
            num_scalar_prefetch=1,
            in_specs=in_vmem(11),
            out_specs=in_vmem(7),
            scratch_shapes=[
                pltpu.VMEM((GROUP, slots), low),
                pltpu.VMEM((GROUP, PAIR), jnp.float32),
            ],
        ),
        cost_estimate=pl.CostEstimate(flops=10**10, bytes_accessed=10**7, transcendentals=10**7),
        compiler_params=pltpu.CompilerParams(vmem_limit_bytes=56 * 2**20),
    )(place, *chunks, w, q_bias, v_bias)


def attend_back(place, o, grad_o, qt, ka, kt, va, qn):
    slots = 8 * GROUP
    low = jnp.bfloat16
    return pl.pallas_call(
        attend_back_kernel,
        name="attend_back",
        out_shape=jax.ShapeDtypeStruct((slots, 3 * GROUP), low),
        grid_spec=pltpu.PrefetchScalarGridSpec(
            num_scalar_prefetch=1,
            in_specs=in_vmem(7),
            out_specs=pl.BlockSpec(memory_space=pltpu.VMEM),
            scratch_shapes=[
                pltpu.VMEM((HEADS_EACH, 2 * HEAD, slots), low),
                pltpu.VMEM((slots, GROUP), low),
                pltpu.VMEM((GROUP, slots), jnp.float32),
            ],
        ),
        cost_estimate=pl.CostEstimate(flops=2 * 10**10, bytes_accessed=10**7, transcendentals=10**7),
        compiler_params=pltpu.CompilerParams(vmem_limit_bytes=56 * 2**20),
    )(place, o, grad_o, qt, ka, kt, va, qn)


def from_ctx(value, bits):
    return lax.ppermute(value, "ctx", [(i, i ^ bits) for i in range(8)])


def gather_rows(shard):
    each = shard.shape[0] // 8
    mine = lax.dynamic_slice_in_dim(shard, lax.axis_index("ctx") * each, each, 0)
    column = lax.all_gather(mine, "fsdp", axis=0)
    plane = lax.all_gather(column, "ctx", axis=0)
    return jnp.swapaxes(plane, 0, 1).reshape((4 * shard.shape[0],) + shard.shape[1:])


def scatter_rows(whole):
    part = lax.psum_scatter(whole.astype(jnp.bfloat16), "ctx", scatter_dimension=0, tiled=True)
    return lax.psum_scatter(part, "fsdp", scatter_dimension=0, tiled=True).astype(jnp.float32)


def fast_on_device(
    tokens,
    doc_ids,
    keep_mask,
    qkv_weight,
    query_bias,
    value_bias,
    proj_weight,
    proj_bias,
    norm1_gain,
    norm1_bias,
    up_weight,
    up_bias,
    down_weight,
    down_bias,
    norm2_gain,
    norm2_bias,
    cotangent,
):
    low = jnp.bfloat16
    me = lax.axis_index("ctx")
    height = me // 4
    group = me % 4
    depth = lax.axis_index("fsdp")
    place = jnp.stack([me, depth] + [jnp.int32(k) for k in ARRIVAL])
    rows = tokens[:, 0]
    ids = doc_ids[:, 0]
    features = rows.shape[2]

    id_rows = jnp.pad(ids.astype(low)[:, None, :], ((0, 0), (0, ID_ROWS - 1), (0, features - GROUP)))
    marked = jnp.concatenate([rows, id_rows], axis=1)
    own = lax.dynamic_index_in_dim(marked, height, 0, keepdims=False)
    other = lax.dynamic_index_in_dim(marked, 1 - height, 0, keepdims=False)
    got = {0: own}
    got[4] = from_ctx(other, 4)
    got[2] = from_ctx(got[0], 2)
    got[6] = from_ctx(got[4], 2)
    for k in (0, 4, 2, 6):
        got[k + 1] = from_ctx(got[k], 1)
    chunks = [got[k] for k in ARRIVAL]

    at = group * GROUP
    shard_columns = jnp.concatenate(
        [lax.dynamic_slice_in_dim(qkv_weight, part * features + at, GROUP, 1) for part in range(3)],
        axis=1,
    )
    qkv_mine = lax.all_gather(shard_columns, "fsdp", axis=0, tiled=True)
    vectors = jnp.concatenate(
        [
            query_bias,
            value_bias,
            proj_bias,
            norm1_gain,
            norm1_bias,
            down_bias,
            norm2_gain,
            norm2_bias,
            up_bias,
        ]
    )[None, :]
    vectors = lax.all_gather(vectors, "fsdp", axis=0, tiled=True).astype(jnp.float32)
    eight = [vectors[:, i * GROUP : (i + 1) * GROUP].reshape(features) for i in range(8)]
    up_bias_all = vectors[:, 8 * GROUP :].reshape(4 * features)
    q_bias_all, v_bias_all, proj_bias_all, gain1, bias1, down_bias_all, gain2, bias2 = eight
    q_bias = lax.dynamic_slice_in_dim(q_bias_all, at, GROUP)[None, :]
    v_bias = lax.dynamic_slice_in_dim(v_bias_all, at, GROUP)[None, :]

    proj_all = gather_rows(proj_weight)
    up_all = gather_rows(up_weight)
    down_all = gather_rows(down_weight)

    o, qt, ka, kt, va, qn, xs = attend(place, chunks, qkv_mine, q_bias, v_bias)
    heads = lax.all_to_all(o, "ctx", 0, 0, tiled=True).reshape(2, 4, GROUP, GROUP)
    attended = jnp.swapaxes(heads, 1, 2).reshape(2 * GROUP, features)

    flat = rows.reshape(2 * GROUP, features)
    token_float = flat.astype(jnp.float32)
    grad_float = cotangent[:, 0].reshape(2 * GROUP, features).astype(jnp.float32)
    documents = jnp.arange(NDOC, dtype=jnp.int32)
    keep_rows = jnp.sum(
        jnp.where(ids[:, :, None] == documents, keep_mask[:, 0][:, None, :], 0), axis=2
    ).astype(jnp.float32).reshape(2 * GROUP, 1)
    projection = dot(attended, proj_all) + proj_bias_all
    hidden, norm1_back = jax.vjp(layer_norm, token_float + projection, gain1, bias1)
    hidden_low = hidden.astype(low)
    inner_rows = dot(hidden_low, up_all) + up_bias_all
    active, gelu_back = jax.vjp(exact_gelu, inner_rows)
    active_low = active.astype(low)
    branch = dot(active_low, down_all) + down_bias_all
    result, norm2_back = jax.vjp(layer_norm, hidden + branch, gain2, bias2)
    block_rows = (keep_rows * result + (1.0 - keep_rows) * token_float).astype(low)
    grad_sum, grad_gain2, grad_bias2 = norm2_back(keep_rows * grad_float)
    grad_branch = grad_sum.astype(low)
    grad_down = jnp.einsum("rf,rd->fd", active_low, grad_branch, preferred_element_type=jnp.float32)
    grad_down_bias = jnp.sum(grad_branch.astype(jnp.float32), axis=0)
    (grad_inner,) = gelu_back(
        jnp.einsum("rd,fd->rf", grad_branch, down_all, preferred_element_type=jnp.float32)
    )
    grad_inner_low = grad_inner.astype(low)
    grad_up = jnp.einsum("rd,rf->df", hidden_low, grad_inner_low, preferred_element_type=jnp.float32)
    grad_up_bias = jnp.sum(grad_inner_low.astype(jnp.float32), axis=0)
    grad_hidden = grad_sum + jnp.einsum(
        "rf,df->rd", grad_inner_low, up_all, preferred_element_type=jnp.float32
    )
    grad_mixed, grad_gain1, grad_bias1 = norm1_back(grad_hidden)
    grad_proj_low = grad_mixed.astype(low)
    grad_proj = jnp.einsum("re,rd->ed", attended, grad_proj_low, preferred_element_type=jnp.float32)
    grad_proj_bias = jnp.sum(grad_proj_low.astype(jnp.float32), axis=0)
    grad_attended = jnp.einsum(
        "rd,ed->re", grad_proj_low, proj_all, preferred_element_type=jnp.float32
    ).astype(low)

    grad_heads = jnp.swapaxes(grad_attended.reshape(2, GROUP, 4, GROUP), 1, 2).reshape(
        8, GROUP, GROUP
    )
    grad_o = lax.all_to_all(grad_heads, "ctx", 0, 0, tiled=True)
    grad_cols = attend_back(place, o, grad_o, qt, ka, kt, va, qn)

    partial = jnp.einsum(
        "re,de->rd", grad_cols, qkv_mine, preferred_element_type=jnp.float32
    ).astype(low)
    partial = partial.reshape(8, GROUP, features)
    half = partial[:4].astype(jnp.float32) + from_ctx(partial[4:], 1).astype(jnp.float32)
    half = half.astype(low)
    quarter = half[:2].astype(jnp.float32) + from_ctx(half[2:], 2).astype(jnp.float32)
    mine = quarter[0]
    swapped = from_ctx(quarter[1].astype(low), 4).astype(jnp.float32)
    first = height == 0
    back = jnp.concatenate(
        [jnp.where(first, mine, swapped), jnp.where(first, swapped, mine)], axis=0
    )
    grad_tokens = keep_rows * (grad_mixed + back) + (1.0 - keep_rows) * grad_float

    grad_qkv = jnp.einsum("rd,re->de", xs, grad_cols, preferred_element_type=jnp.float32)
    head_bias = jnp.sum(grad_cols.astype(jnp.float32), axis=0)
    zero = jnp.zeros((features,), jnp.float32)
    grad_query_bias = lax.dynamic_update_slice_in_dim(zero, head_bias[:GROUP], at, 0)
    grad_value_bias = lax.dynamic_update_slice_in_dim(zero, head_bias[2 * GROUP :], at, 0)
    columns = jnp.stack(
        [
            grad_query_bias,
            grad_value_bias,
            grad_proj_bias,
            grad_gain1,
            grad_bias1,
            grad_down_bias,
            grad_gain2,
            grad_bias2,
        ],
        axis=1,
    )
    columns = jnp.concatenate([columns, grad_up_bias.reshape(features, 4)], axis=1)
    high = columns.astype(low)
    rest = (columns - high.astype(jnp.float32)).astype(low)
    sent = jnp.concatenate(
        [grad_qkv.astype(low), high, rest, jnp.zeros((features, 104), low)], axis=1
    )
    each = features // 32
    came = lax.all_to_all(sent, ("ctx", "fsdp"), 0, 0, tiled=True).reshape(2, 4, 4, each, -1)
    came = came.astype(jnp.float32)
    out_qkv = jnp.sum(came[..., : 3 * GROUP], axis=(0, 2))
    out_qkv = out_qkv.reshape(4, each, 3, GROUP).transpose(1, 2, 0, 3).reshape(each, 3 * features)
    out_vec = jnp.sum(came[..., 3 * GROUP : 3 * GROUP + 24], axis=(0, 1, 2))
    out_vec = out_vec[:, :12] + out_vec[:, 12:]
    out_up_bias = out_vec[:, 8:].reshape(4 * each)

    block_out = block_rows.reshape(2, 1, GROUP, features)
    grad_tokens = grad_tokens.reshape(2, 1, GROUP, features)
    return (
        block_out,
        grad_tokens,
        out_qkv,
        out_vec[:, 0],
        out_vec[:, 1],
        scatter_rows(grad_proj),
        out_vec[:, 2],
        out_vec[:, 3],
        out_vec[:, 4],
        scatter_rows(grad_up),
        out_up_bias,
        scatter_rows(grad_down),
        out_vec[:, 5],
        out_vec[:, 6],
        out_vec[:, 7],
    )


def solution(mesh):
    in_specs = (
        P(None, "fsdp", "ctx", None),
        P(None, "fsdp", "ctx"),
        P(None, "fsdp", None),
        P("fsdp", None),
        P("fsdp"),
        P("fsdp"),
        P("fsdp", None),
        P("fsdp"),
        P("fsdp"),
        P("fsdp"),
        P("fsdp", None),
        P("fsdp"),
        P("fsdp", None),
        P("fsdp"),
        P("fsdp"),
        P("fsdp"),
        P(None, "fsdp", "ctx", None),
    )
    out_specs = (
        P(None, "fsdp", "ctx", None),
        P(None, "fsdp", "ctx", None),
        P(("ctx", "fsdp"), None),
        P(("ctx", "fsdp")),
        P(("ctx", "fsdp")),
        P(("ctx", "fsdp"), None),
        P(("ctx", "fsdp")),
        P(("ctx", "fsdp")),
        P(("ctx", "fsdp")),
        P(("ctx", "fsdp"), None),
        P(("ctx", "fsdp")),
        P(("ctx", "fsdp"), None),
        P(("ctx", "fsdp")),
        P(("ctx", "fsdp")),
        P(("ctx", "fsdp")),
    )
    work = fast_on_device if fits(mesh) else on_device
    return jax.shard_map(
        work, mesh=mesh, in_specs=in_specs, out_specs=out_specs, check_vma=False
    )
```

```python
import functools
import math

import jax
import jax.numpy as jnp
from jax import lax
from jax.experimental import pallas as pl
from jax.experimental.pallas import tpu as pltpu
from jax.sharding import PartitionSpec as P

H = 12
NDOC = 4


epsilon = 1e-05
score_scale = 0.125
masked_score = -1e30


def layer_norm(values, gain_vec, offset_vec):
    centre = jnp.mean(values, axis=-1, keepdims=True)
    centred = values - centre
    spread = jnp.mean(centred * centred, axis=-1, keepdims=True)
    return centred * lax.rsqrt(spread + epsilon) * gain_vec + offset_vec


def exact_gelu(values):
    return jax.nn.gelu(values, approximate=False)


def in_blocks(stepper, carried, portion, shard_rows):
    total_rows = portion[0].shape[0]
    shard_count = total_rows // shard_rows
    limit_rows = max(1, 1024 // shard_rows)
    grouped = math.gcd(shard_count, 1 << limit_rows.bit_length() - 1)
    block_rows = grouped * shard_rows
    turn_count = total_rows // block_rows
    stacked = tuple(
        (member.reshape((turn_count, block_rows) + member.shape[1:]) for member in portion)
    )
    offsets = block_rows * jnp.arange(turn_count, dtype=jnp.int32)

    def one_turn(inner_state, element):
        return (stepper(inner_state, element[0], element[1]), None)

    carried, ignored = lax.scan(one_turn, carried, (stacked, offsets))
    return carried


def micro_step(token_rows, slot_ids, keep_flags, weights_full, grad_rows):
    (
        qkv_weight,
        query_bias,
        value_bias,
        proj_weight,
        proj_bias,
        norm1_gain,
        norm1_bias,
        up_weight,
        up_bias,
        down_weight,
        down_bias,
        norm2_gain,
        norm2_bias,
    ) = weights_full
    local_rows, features = token_rows.shape
    num_heads = H
    head_size = features // num_heads
    documents = jnp.arange(NDOC, dtype=jnp.int32)
    keep_rows = jnp.sum(
        jnp.where(slot_ids[:, None] == documents[None, :], keep_flags[None, :], 0), axis=1
    ).astype(jnp.float32)[:, None]
    token_float = token_rows.astype(jnp.float32)
    slot_labels = slot_ids.astype(jnp.float32).astype(jnp.bfloat16)
    projected = jnp.dot(token_rows, qkv_weight, preferred_element_type=jnp.float32)
    query_rows = (projected[:, :features] + query_bias.astype(jnp.float32)).astype(jnp.bfloat16)
    key_rows = projected[:, features : 2 * features].astype(jnp.bfloat16)
    value_rows = (projected[:, 2 * features :] + value_bias.astype(jnp.float32)).astype(
        jnp.bfloat16
    )
    query_heads = query_rows.reshape(local_rows, num_heads, head_size)
    key_heads_local = key_rows.reshape(local_rows, num_heads, head_size)
    value_heads_local = value_rows.reshape(local_rows, num_heads, head_size)

    def forward_step(carried, portion, offset):
        key_part, value_part, id_part = portion
        running_max, running_sum, running_out = carried
        scores = (
            jnp.einsum(
                "qhd,khd->hqk",
                query_heads,
                key_part.reshape(-1, num_heads, head_size),
                preferred_element_type=jnp.float32,
            )
            * score_scale
        )
        same_doc = (slot_labels[:, None] == id_part[None, :])[None]
        scores = jnp.where(same_doc, scores, masked_score)
        new_max = jnp.maximum(running_max, jnp.max(scores, axis=-1))
        factor = jnp.exp(running_max - new_max)
        weights = jnp.where(same_doc, jnp.exp(scores - new_max[..., None]), 0.0)
        running_sum = running_sum * factor + jnp.sum(weights, axis=-1)
        running_out = running_out * factor[..., None] + jnp.einsum(
            "hqk,khd->hqd",
            weights.astype(jnp.bfloat16),
            value_part.reshape(-1, num_heads, head_size),
            preferred_element_type=jnp.float32,
        )
        return (new_max, running_sum, running_out)

    start_state = (
        jnp.full((num_heads, local_rows), masked_score, jnp.float32),
        jnp.zeros((num_heads, local_rows), jnp.float32),
        jnp.zeros((num_heads, local_rows, head_size), jnp.float32),
    )
    running_max, running_sum, running_out = in_blocks(
        forward_step,
        start_state,
        (
            lax.all_gather(key_rows, "ctx", axis=0, tiled=True),
            lax.all_gather(value_rows, "ctx", axis=0, tiled=True),
            lax.all_gather(slot_labels, "ctx", axis=0, tiled=True),
        ),
        local_rows,
    )
    attended = jnp.transpose(running_out / running_sum[..., None], (1, 0, 2))
    log_total = running_max + jnp.log(running_sum)
    attended_low = attended.reshape(local_rows, features).astype(jnp.bfloat16)
    projection = jnp.dot(
        attended_low, proj_weight, preferred_element_type=jnp.float32
    ) + proj_bias.astype(jnp.float32)
    hidden, norm1_back = jax.vjp(
        layer_norm,
        token_float + projection,
        norm1_gain.astype(jnp.float32),
        norm1_bias.astype(jnp.float32),
    )
    hidden_low = hidden.astype(jnp.bfloat16)
    inner_rows = jnp.dot(
        hidden_low, up_weight, preferred_element_type=jnp.float32
    ) + up_bias.astype(jnp.float32)
    active, gelu_back = jax.vjp(exact_gelu, inner_rows)
    active_low = active.astype(jnp.bfloat16)
    branch = jnp.dot(
        active_low, down_weight, preferred_element_type=jnp.float32
    ) + down_bias.astype(jnp.float32)
    result, norm2_back = jax.vjp(
        layer_norm, hidden + branch, norm2_gain.astype(jnp.float32), norm2_bias.astype(jnp.float32)
    )
    block_rows = (keep_rows * result + (1.0 - keep_rows) * token_float).astype(jnp.bfloat16)
    grad_float = grad_rows.astype(jnp.float32)
    grad_sum, grad_gain2, grad_bias2 = norm2_back(keep_rows * grad_float)
    grad_branch = grad_sum.astype(jnp.bfloat16)
    grad_down = jnp.einsum("rf,rd->fd", active_low, grad_branch, preferred_element_type=jnp.float32)
    grad_down_bias = jnp.sum(grad_branch.astype(jnp.float32), axis=0)
    (grad_inner,) = gelu_back(
        jnp.einsum("rd,fd->rf", grad_branch, down_weight, preferred_element_type=jnp.float32)
    )
    grad_inner_low = grad_inner.astype(jnp.bfloat16)
    grad_up = jnp.einsum(
        "rd,rf->df", hidden_low, grad_inner_low, preferred_element_type=jnp.float32
    )
    grad_up_bias = jnp.sum(grad_inner_low.astype(jnp.float32), axis=0)
    grad_hidden = grad_sum + jnp.einsum(
        "rf,df->rd", grad_inner_low, up_weight, preferred_element_type=jnp.float32
    )
    grad_mixed, grad_gain1, grad_bias1 = norm1_back(grad_hidden)
    grad_proj_low = grad_mixed.astype(jnp.bfloat16)
    grad_proj = jnp.einsum(
        "re,rd->ed", attended_low, grad_proj_low, preferred_element_type=jnp.float32
    )
    grad_proj_bias = jnp.sum(grad_proj_low.astype(jnp.float32), axis=0)
    grad_attended = jnp.einsum(
        "rd,ed->re", grad_proj_low, proj_weight, preferred_element_type=jnp.float32
    ).astype(jnp.bfloat16)
    grad_heads = grad_attended.reshape(local_rows, num_heads, head_size)
    row_delta = jnp.transpose(jnp.sum(grad_heads.astype(jnp.float32) * attended, axis=-1))

    def query_step(carried, portion, offset):
        key_part, value_part, id_part = portion
        key_heads = key_part.reshape(-1, num_heads, head_size)
        scores = (
            jnp.einsum("qhd,khd->hqk", query_heads, key_heads, preferred_element_type=jnp.float32)
            * score_scale
        )
        same_doc = (slot_labels[:, None] == id_part[None, :])[None]
        scores = jnp.where(same_doc, scores, masked_score)
        probs = jnp.where(same_doc, jnp.exp(scores - log_total[..., None]), 0.0)
        grad_probs = jnp.einsum(
            "qhd,khd->hqk",
            grad_heads,
            value_part.reshape(-1, num_heads, head_size),
            preferred_element_type=jnp.float32,
        )
        grad_scores = (probs * (grad_probs - row_delta[..., None])).astype(jnp.bfloat16)
        return carried + jnp.einsum(
            "hqk,khd->qhd", grad_scores, key_heads, preferred_element_type=jnp.float32
        )

    grad_query_sum = in_blocks(
        query_step,
        jnp.zeros((local_rows, num_heads, head_size), jnp.float32),
        (
            lax.all_gather(key_rows, "ctx", axis=0, tiled=True),
            lax.all_gather(value_rows, "ctx", axis=0, tiled=True),
            lax.all_gather(slot_labels, "ctx", axis=0, tiled=True),
        ),
        local_rows,
    )
    log_rows, delta_rows = (
        lax.all_gather(jnp.transpose(log_total), "ctx", axis=0, tiled=True),
        lax.all_gather(jnp.transpose(row_delta), "ctx", axis=0, tiled=True),
    )

    def key_step(carried, portion, offset):
        query_part, grad_part, id_part = portion
        grad_key_sum, grad_value_sum = carried
        span_rows = query_part.shape[0]
        log_part = lax.dynamic_slice_in_dim(log_rows, offset, span_rows, 0)
        delta_part = lax.dynamic_slice_in_dim(delta_rows, offset, span_rows, 0)
        query_part_heads = query_part.reshape(-1, num_heads, head_size)
        grad_part_heads = grad_part.reshape(-1, num_heads, head_size)
        scores = (
            jnp.einsum(
                "qhd,khd->hqk",
                query_part_heads,
                key_heads_local,
                preferred_element_type=jnp.float32,
            )
            * score_scale
        )
        same_doc = (id_part[:, None] == slot_labels[None, :])[None]
        scores = jnp.where(same_doc, scores, masked_score)
        probs = jnp.where(same_doc, jnp.exp(scores - jnp.transpose(log_part)[..., None]), 0.0)
        grad_value_sum = grad_value_sum + jnp.einsum(
            "hqk,qhd->khd",
            probs.astype(jnp.bfloat16),
            grad_part_heads,
            preferred_element_type=jnp.float32,
        )
        grad_probs = jnp.einsum(
            "qhd,khd->hqk", grad_part_heads, value_heads_local, preferred_element_type=jnp.float32
        )
        grad_scores = (probs * (grad_probs - jnp.transpose(delta_part)[..., None])).astype(
            jnp.bfloat16
        )
        grad_key_sum = grad_key_sum + jnp.einsum(
            "hqk,qhd->khd", grad_scores, query_part_heads, preferred_element_type=jnp.float32
        )
        return (grad_key_sum, grad_value_sum)

    zero_heads = jnp.zeros((local_rows, num_heads, head_size), jnp.float32)
    grad_key_sum, grad_value_sum = in_blocks(
        key_step,
        (zero_heads, zero_heads),
        (
            lax.all_gather(query_rows, "ctx", axis=0, tiled=True),
            lax.all_gather(grad_attended, "ctx", axis=0, tiled=True),
            lax.all_gather(slot_labels, "ctx", axis=0, tiled=True),
        ),
        local_rows,
    )
    grad_query = (grad_query_sum * score_scale).reshape(local_rows, features).astype(jnp.bfloat16)
    grad_key = (grad_key_sum * score_scale).reshape(local_rows, features).astype(jnp.bfloat16)
    grad_value = grad_value_sum.reshape(local_rows, features).astype(jnp.bfloat16)
    grad_projected = jnp.concatenate([grad_query, grad_key, grad_value], axis=1)
    grad_qkv = jnp.einsum(
        "rd,re->de", token_rows, grad_projected, preferred_element_type=jnp.float32
    )
    grad_query_bias = jnp.sum(grad_query.astype(jnp.float32), axis=0)
    grad_value_bias = jnp.sum(grad_value.astype(jnp.float32), axis=0)
    grad_input = grad_mixed + jnp.einsum(
        "re,de->rd", grad_projected, qkv_weight, preferred_element_type=jnp.float32
    )
    grad_tokens = keep_rows * grad_input + (1.0 - keep_rows) * grad_float
    terms = (
        grad_qkv,
        grad_query_bias,
        grad_value_bias,
        grad_proj,
        grad_proj_bias,
        grad_gain1,
        grad_bias1,
        grad_up,
        grad_up_bias,
        grad_down,
        grad_down_bias,
        grad_gain2,
        grad_bias2,
    )
    return (block_rows, grad_tokens, terms)


def on_device(
    tokens,
    doc_ids,
    keep_mask,
    qkv_weight,
    query_bias,
    value_bias,
    proj_weight,
    proj_bias,
    norm1_gain,
    norm1_bias,
    up_weight,
    up_bias,
    down_weight,
    down_bias,
    norm2_gain,
    norm2_bias,
    cotangent,
):
    block_list = []
    grad_list = []
    summed = None
    for micro_index in range(tokens.shape[0]):
        weights_full = (
            lax.all_gather(qkv_weight, "fsdp", axis=0, tiled=True),
            lax.all_gather(query_bias, "fsdp", axis=0, tiled=True),
            lax.all_gather(value_bias, "fsdp", axis=0, tiled=True),
            lax.all_gather(proj_weight, "fsdp", axis=0, tiled=True),
            lax.all_gather(proj_bias, "fsdp", axis=0, tiled=True),
            lax.all_gather(norm1_gain, "fsdp", axis=0, tiled=True),
            lax.all_gather(norm1_bias, "fsdp", axis=0, tiled=True),
            lax.all_gather(up_weight, "fsdp", axis=0, tiled=True),
            lax.all_gather(up_bias, "fsdp", axis=0, tiled=True),
            lax.all_gather(down_weight, "fsdp", axis=0, tiled=True),
            lax.all_gather(down_bias, "fsdp", axis=0, tiled=True),
            lax.all_gather(norm2_gain, "fsdp", axis=0, tiled=True),
            lax.all_gather(norm2_bias, "fsdp", axis=0, tiled=True),
        )
        block_rows, grad_tokens, terms = micro_step(
            tokens[micro_index, 0],
            doc_ids[micro_index, 0],
            keep_mask[micro_index, 0],
            weights_full,
            cotangent[micro_index, 0],
        )
        block_list.append(block_rows)
        grad_list.append(grad_tokens)
        if summed is None:
            summed = terms
        else:
            summed = tuple((earlier + later for earlier, later in zip(summed, terms)))
    reduced = (
        lax.psum_scatter(summed[0], ("ctx", "fsdp"), scatter_dimension=0, tiled=True),
        lax.psum_scatter(summed[1], ("ctx", "fsdp"), scatter_dimension=0, tiled=True),
        lax.psum_scatter(summed[2], ("ctx", "fsdp"), scatter_dimension=0, tiled=True),
        lax.psum_scatter(summed[3], ("ctx", "fsdp"), scatter_dimension=0, tiled=True),
        lax.psum_scatter(summed[4], ("ctx", "fsdp"), scatter_dimension=0, tiled=True),
        lax.psum_scatter(summed[5], ("ctx", "fsdp"), scatter_dimension=0, tiled=True),
        lax.psum_scatter(summed[6], ("ctx", "fsdp"), scatter_dimension=0, tiled=True),
        lax.psum_scatter(summed[7], ("ctx", "fsdp"), scatter_dimension=0, tiled=True),
        lax.psum_scatter(summed[8], ("ctx", "fsdp"), scatter_dimension=0, tiled=True),
        lax.psum_scatter(summed[9], ("ctx", "fsdp"), scatter_dimension=0, tiled=True),
        lax.psum_scatter(summed[10], ("ctx", "fsdp"), scatter_dimension=0, tiled=True),
        lax.psum_scatter(summed[11], ("ctx", "fsdp"), scatter_dimension=0, tiled=True),
        lax.psum_scatter(summed[12], ("ctx", "fsdp"), scatter_dimension=0, tiled=True),
    )
    block_out = jnp.stack(block_list)[:, None]
    grad_tokens_all = jnp.stack(grad_list)[:, None]
    return (
        block_out,
        grad_tokens_all,
        reduced[0],
        reduced[1],
        reduced[2],
        reduced[3],
        reduced[4],
        reduced[5],
        reduced[6],
        reduced[7],
        reduced[8],
        reduced[9],
        reduced[10],
        reduced[11],
        reduced[12],
    )


MASKED = -1e30
LOWEST = -3e38
ARRIVAL = (0, 4, 2, 6, 1, 5, 3, 7)
GROUP = 192
HEAD = 64
HEADS_EACH = 3
PAIR = 384
SLOTS = 1536
ID_ROWS = 8


def fits(mesh):
    return mesh.shape["ctx"] == 8 and mesh.shape["fsdp"] == 4


def dot(a, b):
    return lax.dot_general(a, b, (((1,), (0,)), ((), ())), preferred_element_type=jnp.float32)


def dot_nt(a, b):
    return lax.dot_general(a, b, (((1,), (1,)), ((), ())), preferred_element_type=jnp.float32)


def flip(value):
    return jnp.transpose(value.astype(jnp.float32)).astype(jnp.bfloat16)


def split3(value):
    high = value.astype(jnp.bfloat16).astype(jnp.float32)
    mid = (value - high).astype(jnp.bfloat16).astype(jnp.float32)
    return high, mid, value - high - mid


def call(kernel, name, ins, outs, scratch=(), scalars=1, any_ins=0, flops=5 * 10**9, aliases=None):
    vmem = pl.BlockSpec(memory_space=pltpu.VMEM)
    return pl.pallas_call(
        kernel,
        name=name,
        out_shape=[jax.ShapeDtypeStruct(shape, kind) for shape, kind in outs],
        grid_spec=pltpu.PrefetchScalarGridSpec(
            num_scalar_prefetch=scalars,
            in_specs=[vmem] * (len(ins) - scalars - any_ins)
            + [pl.BlockSpec(memory_space=pl.ANY)] * any_ins,
            out_specs=[vmem] * len(outs),
            scratch_shapes=list(scratch),
        ),
        cost_estimate=pl.CostEstimate(flops=flops, bytes_accessed=10**7, transcendentals=10**6),
        compiler_params=pltpu.CompilerParams(vmem_limit_bytes=56 * 2**20),
    )(*ins)


QUAD = 768
TILE = 256
TILES = SLOTS // TILE


def project_kernel(place, *refs):
    x_refs = refs[:2]
    own_ref, near_ref, mid_ref, far_ref = refs[2:6]
    qt_refs, ka_refs = refs[6:9], refs[9:12]
    vt_ref, w_ref, vec_ref, turned = refs[12:]
    me, depth = place[0], place[1]
    for m, ref in enumerate((own_ref, near_ref, mid_ref, far_ref)):
        owner = depth ^ m
        rows = pl.ds(pl.multiple_of(owner * GROUP, GROUP), GROUP)
        w_ref[rows, :] = ref[0:GROUP, :]
        vec_ref[owner] = ref[GROUP : GROUP + 8, :].astype(jnp.float32)
    mine = vec_ref[me & 3]
    turned[0:GROUP] = flip(w_ref[:, 0:GROUP])
    turned[GROUP:] = flip(w_ref[:, 2 * GROUP :])
    bias = jnp.concatenate([mine[:, 0:GROUP], mine[:, GROUP : 2 * GROUP]], axis=1)
    bias = jnp.transpose(bias)[:, 0:1]
    lane = lax.broadcasted_iota(jnp.int32, (QUAD, HEAD), 1)
    row = lax.broadcasted_iota(jnp.int32, (HEAD, QUAD), 0)
    for t in range(2):
        span = slice(t * QUAD, (t + 1) * QUAD)
        x = jnp.concatenate([x_refs[t][i, 0:GROUP] for i in range(4)], axis=0)
        ids = jnp.concatenate(
            [x_refs[t][i, GROUP : GROUP + 8, 0:GROUP] for i in range(4)], axis=1
        ).astype(jnp.float32)
        id_row = ids[0:1, :]
        id_col = jnp.transpose(ids)[:, 0:1]
        k_side = jnp.where(
            lane < 5,
            jnp.where(id_col == lane.astype(jnp.float32), 0.0, MASKED),
            jnp.where(lane < 8, -1.0, 0.0),
        ).astype(jnp.bfloat16)
        q_side = jnp.where((row < 5) & (id_row == row.astype(jnp.float32)), 1.0, 0.0).astype(
            jnp.bfloat16
        )
        k = dot(x, w_ref[:, GROUP : 2 * GROUP]).astype(jnp.bfloat16)
        qv = (dot_nt(turned[...], x) + bias).astype(jnp.bfloat16)
        vt_ref[:, span] = qv[GROUP:]
        q = (qv[:GROUP] * 0.125).astype(jnp.bfloat16)
        for h in range(HEADS_EACH):
            heads = slice(h * HEAD, (h + 1) * HEAD)
            ka_refs[h][span, :] = jnp.concatenate([k[:, heads], k_side], axis=1)
            qt_refs[h][0:HEAD, span] = q[heads]
            qt_refs[h][HEAD : 2 * HEAD, span] = q_side


def turn_kernel(*refs):
    x_refs, qt_refs, ka_refs = refs[:2], refs[2:5], refs[5:8]
    vt_ref, w_ref = refs[8:10]
    xt_ref, qn_ref, kt_ref, va_refs, by_head = refs[10], refs[11], refs[12], refs[13:16], refs[16]
    lane = lax.broadcasted_iota(jnp.int32, (PAIR, HEAD), 1)
    v_side = jnp.where(lane < 3, -1.0, 0.0).astype(jnp.bfloat16)
    for t in range(4):
        span = slice(t * PAIR, (t + 1) * PAIR)
        x = jnp.concatenate([x_refs[t // 2][2 * (t % 2) + i, 0:GROUP] for i in (0, 1)], axis=0)
        xt_ref[:, span] = flip(x)
        for h in range(HEADS_EACH):
            heads = slice(h * HEAD, (h + 1) * HEAD)
            qn_ref[span, heads] = flip(qt_refs[h][0:HEAD, span])
            kt_ref[heads, span] = flip(ka_refs[h][span, 0:HEAD])
            va_refs[h][span, :] = jnp.concatenate([flip(vt_ref[heads, span]), v_side], axis=1)
    for h in range(HEADS_EACH):
        for i in range(3):
            by_head[:, (3 * h + i) * HEAD : (3 * h + i + 1) * HEAD] = w_ref[
                :, i * GROUP + h * HEAD : i * GROUP + (h + 1) * HEAD
            ]


def attend_kernel(heads, place, *refs):
    n = len(heads)
    qt_refs, ka_refs, vt_ref = refs[:n], refs[n : 2 * n], refs[2 * n]
    last = heads[-1] == HEADS_EACH - 1
    earlier = refs[2 * n + 1 : 3 * n + 1] if not last else refs[2 * n + 1 : 2 * n + 3]
    refs = refs[2 * n + 1 + (len(earlier) if last else 0) :]
    out_qt, out_ot = refs[:n], refs[n : 2 * n]
    o_ref = refs[2 * n] if last else None
    held = refs[-1]
    me = place[0]
    at_row = lax.broadcasted_iota(jnp.int32, (16, TILE), 0)

    def one_tile(t, unused):
        here = pl.ds(pl.multiple_of(t * TILE, TILE), TILE)
        tops = []
        for i in range(n):
            q_tile = qt_refs[i][:, here]
            top = jnp.full((8, TILE), LOWEST, jnp.float32)
            for j in range(TILES):
                span = slice(j * TILE, (j + 1) * TILE)
                scores = dot(ka_refs[i][span, :], q_tile)
                held[i, span, :] = scores
                top = jnp.maximum(top, jnp.max(scores.reshape(TILE // 8, 8, TILE), axis=0))
            tops.append(jnp.max(top, axis=0, keepdims=True))
        for i, h in enumerate(heads):
            rows = slice(h * HEAD, (h + 1) * HEAD)
            total = jnp.zeros((8, TILE), jnp.float32)
            out = jnp.zeros((HEAD, TILE), jnp.float32)
            for j in range(TILES):
                span = slice(j * TILE, (j + 1) * TILE)
                probs = jnp.exp(held[i, span, :] - tops[i])
                total = total + jnp.sum(probs.reshape(TILE // 8, 8, TILE), axis=0)
                out = out + dot(vt_ref[rows, span], probs.astype(jnp.bfloat16))
            total = jnp.sum(total, axis=0, keepdims=True)
            out_ot[i][:, here] = (out / total).astype(jnp.bfloat16)
            high, mid, low = split3(tops[i] + jnp.log(total))
            side = qt_refs[i][HEAD : HEAD + 16, here].astype(jnp.float32)
            side = jnp.where(at_row == 5, high, side)
            side = jnp.where(at_row == 6, mid, side)
            side = jnp.where(at_row == 7, low, side)
            out_qt[i][0:HEAD, here] = qt_refs[i][0:HEAD, here]
            out_qt[i][HEAD : HEAD + 16, here] = side.astype(jnp.bfloat16)
            out_qt[i][HEAD + 16 :, here] = qt_refs[i][HEAD + 16 :, here]
        return unused

    lax.fori_loop(0, TILES, one_tile, 0)
    if last:
        for t in range(4):
            span = slice(t * PAIR, (t + 1) * PAIR)
            whole = jnp.concatenate(
                [ref[:, span] for ref in (*earlier, *out_ot)], axis=0
            )
            rows = flip(whole)
            for half in range(2):
                o_ref[me ^ ARRIVAL[2 * t + half]] = rows[half * GROUP : (half + 1) * GROUP, :]


def attend_back_kernel(heads, place, *refs):
    n = len(heads)
    do_ref, kt_ref, qn_ref, xt_ref = refs[:4]
    refs = refs[4:]
    ot_refs, qt_refs, ka_refs, va_refs = [refs[i * n : (i + 1) * n] for i in range(4)]
    refs = refs[4 * n :]
    last = heads[-1] == HEADS_EACH - 1
    if last:
        earlier_ref, w_ref = refs[:2]
        refs = refs[2:]
        sent_ref, keep_ref, give_ref, g_ref = refs[:4]
        refs = refs[4:]
    else:
        sent_ref, g_ref = refs[0], refs[1]
        refs = refs[2:]
    dot_t, don, dqt = refs
    me = place[0]
    row = lax.broadcasted_iota(jnp.int32, (HEAD, PAIR), 0)
    for t in range(4):
        here = slice(t * PAIR, (t + 1) * PAIR)
        a, b = me ^ ARRIVAL[2 * t], me ^ ARRIVAL[2 * t + 1]
        for i, h in enumerate(heads):
            cols = slice(h * HEAD, (h + 1) * HEAD)
            grad = jnp.concatenate([do_ref[a][:, cols], do_ref[b][:, cols]], axis=0)
            don[i, here, :] = grad
            grad_t = jnp.transpose(grad.astype(jnp.float32))
            delta = jnp.sum(grad_t * ot_refs[i][:, here].astype(jnp.float32), axis=0, keepdims=True)
            high, mid, low = split3(delta)
            side = jnp.where(
                row == 0, high, jnp.where(row == 1, mid, jnp.where(row == 2, low, 0.0))
            )
            dot_t[i, 0:HEAD, here] = grad_t.astype(jnp.bfloat16)
            dot_t[i, HEAD : 2 * HEAD, here] = side.astype(jnp.bfloat16)
    dqt[...] = jnp.zeros_like(dqt)

    def keys(j, unused):
        here = pl.ds(pl.multiple_of(j * TILE, TILE), TILE)
        for i, h in enumerate(heads):
            rows = slice(h * HEAD, (h + 1) * HEAD)
            key = ka_refs[i][here, :]
            val = va_refs[i][here, :]
            key_t = kt_ref[rows, here]
            dk = jnp.zeros((TILE, HEAD), jnp.float32)
            dv = jnp.zeros((TILE, HEAD), jnp.float32)
            for t in range(TILES):
                span = slice(t * TILE, (t + 1) * TILE)
                probs = jnp.exp(dot(key, qt_refs[i][:, span]))
                grad_probs = dot(val, dot_t[i, :, span])
                grad_scores = (probs * grad_probs).astype(jnp.bfloat16)
                dv = dv + dot(probs.astype(jnp.bfloat16), don[i, span, :])
                dk = dk + dot(grad_scores, qn_ref[span, rows])
                dqt[i, :, span] = dqt[i, :, span] + dot(key_t, grad_scores)
            at = i * GROUP
            g_ref[here, at + HEAD : at + 2 * HEAD] = dk.astype(jnp.bfloat16)
            g_ref[here, at + 2 * HEAD : at + GROUP] = dv.astype(jnp.bfloat16)
        return unused

    lax.fori_loop(0, TILES, keys, 0)
    bias = jnp.zeros((1, n * GROUP), jnp.float32)
    for t in range(4):
        span = slice(t * PAIR, (t + 1) * PAIR)
        for i in range(n):
            g_ref[span, i * GROUP : i * GROUP + HEAD] = (
                jnp.transpose(dqt[i, :, span]) * 0.125
            ).astype(jnp.bfloat16)
        bias = bias + jnp.sum(g_ref[span, :].astype(jnp.float32), axis=0, keepdims=True)
    high = bias.astype(jnp.bfloat16).astype(jnp.float32)
    at_row = lax.broadcasted_iota(jnp.int32, (8, n * GROUP), 0)
    fixed = jnp.where(at_row == 0, high, jnp.where(at_row == 1, bias - high, 0.0))

    def weights_back(t, unused):
        x_rows = xt_ref[pl.ds(pl.multiple_of(t * GROUP, GROUP), GROUP), :]
        part = dot(x_rows, g_ref[...]).astype(jnp.bfloat16)
        for i in range(8):
            sent_ref[8 * t + i, 0:24, :] = part[24 * i : 24 * (i + 1)]
            sent_ref[8 * t + i, 24:32, :] = fixed.astype(jnp.bfloat16)
        return unused

    lax.fori_loop(0, 4, weights_back, 0)
    if last:
        split = earlier_ref.shape[1]

        for t in range(4):
            here = slice(t * PAIR, (t + 1) * PAIR)
            back_ref, at = (keep_ref, 2 * t) if t < 2 else (give_ref, 2 * t - 4)
            part = dot_nt(earlier_ref[here, :], w_ref[:, :split])
            part = (part + dot_nt(g_ref[here, :], w_ref[:, split:])).astype(jnp.bfloat16)
            back_ref[at] = part[:GROUP]
            back_ref[at + 1] = part[GROUP:]


LOW, WIDE = jnp.bfloat16, jnp.float32


def project(*ins):
    outs = [((2 * HEAD, SLOTS), LOW)] * 3 + [((SLOTS, 2 * HEAD), LOW)] * 3
    outs += [((GROUP, SLOTS), LOW), ((4 * GROUP, 3 * GROUP), LOW), ((4, 8, 3 * GROUP), WIDE)]
    scratch = [pltpu.VMEM((2 * GROUP, 4 * GROUP), LOW)]
    return call(project_kernel, "project", ins, outs, scratch)


def turn(*ins):
    outs = [((4 * GROUP, SLOTS), LOW), ((SLOTS, GROUP), LOW), ((GROUP, SLOTS), LOW)]
    outs += [((SLOTS, 2 * HEAD), LOW)] * 3 + [((4 * GROUP, 3 * GROUP), LOW)]
    return call(turn_kernel, "turn", ins, outs, scalars=0)


def attend(heads, *ins):
    n = len(heads)
    outs = [((2 * HEAD, SLOTS), LOW)] * n + [((HEAD, SLOTS), LOW)] * n
    if heads[-1] == HEADS_EACH - 1:
        outs.append(((8, GROUP, GROUP), LOW))
    scratch = [pltpu.VMEM((n, SLOTS, TILE), WIDE)]
    kernel = functools.partial(attend_kernel, heads)
    return call(kernel, f"attend{heads[0]}", ins, outs, scratch)


def attend_back(heads, *ins):
    n = len(heads)
    scratch = [
        pltpu.VMEM((n, 2 * HEAD, SLOTS), LOW),
        pltpu.VMEM((n, SLOTS, HEAD), LOW),
        pltpu.VMEM((n, HEAD, SLOTS), WIDE),
    ]
    outs = [((32, 32, n * GROUP), LOW)]
    if heads[-1] == HEADS_EACH - 1:
        outs += [((4, GROUP, 4 * GROUP), LOW)] * 2
    outs.append(((SLOTS, n * GROUP), LOW))
    kernel = functools.partial(attend_back_kernel, heads)
    return call(kernel, f"attend_back{heads[0]}", ins, outs, scratch, flops=10**10)


def from_ctx(value, bits):
    return lax.ppermute(value, "ctx", [(i, i ^ bits) for i in range(8)])


def from_fsdp(value, bits):
    return lax.ppermute(value, "fsdp", [(i, i ^ bits) for i in range(4)])


FF_CUT = 384
PROJ_ROWS = 48
DOWN_ROWS = 96
PIECE = 240
FIRST = 368
SECOND = 3 * PIECE - FIRST
COLUMNS = 3968
LEFT = 2048


def norm(value):
    centred = value - jnp.mean(value, axis=1, keepdims=True)
    scale = lax.rsqrt(jnp.mean(centred * centred, axis=1, keepdims=True) + epsilon)
    return centred * scale, scale


def norm_back(grad, normal, scale):
    return scale * (
        grad
        - jnp.mean(grad, axis=1, keepdims=True)
        - normal * jnp.mean(grad * normal, axis=1, keepdims=True)
    )


TAIL_AT = 0.35
TAIL = (
    0.19746588,
    0.197487361,
    0.184996341,
    0.164759887,
    0.106787389,
    0.160058898,
    -0.11534264,
    0.24699889,
    -0.186710954,
    0.0434989602,
)


def gelu_parts(value):
    bell = jnp.exp(-0.5 * value * value)
    t = 1.0 / (1.0 + (TAIL_AT * 2.0**-0.5) * jnp.abs(value))
    tail = jnp.full_like(t, 0.5 * TAIL[-1])
    for term in TAIL[-2::-1]:
        tail = tail * t + 0.5 * term
    tail = tail * t * bell
    return jnp.where(value < 0.0, tail, 1.0 - tail), bell


FF_STEP = 512


def dense_kernel(place, *refs):
    a_ref, tok_ref, cot_ref, keep_ref, vec_ref = refs[:5]
    proj_own, up_own, down_all = refs[5:8]
    shared = refs[8:10]
    block_ref, base_ref, ga_ref, rows_ref, keep_cols, give_cols = refs[10:16]
    up, down, proj, slope, act_ref, att_ref, hid_ref, hid_t, gb_ref = refs[16:25]
    sums_ref, upb_ref, turned, proj_sem, up_sem, down_sem = refs[25:]
    me, depth = place[0], place[1]
    width = 4 * GROUP
    proj_copies, up_copies, down_copies = [], [], []

    def copy(into, source, target, sem):
        made = pltpu.make_async_copy(source, target, sem.at[len(into)])
        made.start()
        into.append(made)

    def spot(k, m, up_row=0):
        owner = me ^ k
        return (
            pl.ds(pl.multiple_of((depth ^ m) * GROUP + up_row, 64), GROUP - up_row),
            pl.ds(pl.multiple_of(owner * FF_CUT, FF_CUT), FF_CUT),
        )

    def proj_spot(k, m):
        owner = me ^ k
        at = (depth ^ m) * GROUP + (owner >> 1) * PROJ_ROWS
        return (
            pl.ds(pl.multiple_of(at, PROJ_ROWS), PROJ_ROWS),
            pl.ds(pl.multiple_of((owner & 1) * FF_CUT, FF_CUT), FF_CUT),
        )

    own_rows = pl.ds(pl.multiple_of(depth * GROUP, GROUP), GROUP)
    starts = []
    for core in range(2):
        for i in range(4):
            starts.append((core, core ^ (0, 2, 4, 6)[i], i * FIRST, core ^ (0, 4, 2, 6)[i], 4 * FIRST + i * SECOND))
    copy(proj_copies, proj_own, proj.at[own_rows], proj_sem)
    for core, k_first, first, k_second, second in starts:
        source = shared[core]
        for k, m, at in (
            (k_first, 1, first + GROUP),
            (k_second, 2, second + 64),
            (k_second, 3, second + 64 + PROJ_ROWS + GROUP),
        ):
            copy(proj_copies, source.at[pl.ds(at, PROJ_ROWS)], proj.at[proj_spot(k, m)], proj_sem)
    copy(up_copies, up_own, up.at[own_rows], up_sem)
    for core, k_first, first, k_second, second in starts:
        source = shared[core]
        copy(up_copies, source.at[pl.ds(first, GROUP)], up.at[spot(k_first, 1)], up_sem)
        rows, cols = spot(k_first, 2)
        rows = pl.ds(pl.multiple_of((depth ^ 2) * GROUP, GROUP), 128)
        copy(up_copies, source.at[pl.ds(first + PIECE, 128)], up.at[rows, cols], up_sem)
        copy(up_copies, source.at[pl.ds(second, 64)], up.at[spot(k_second, 2, 128)], up_sem)
        at = second + 64 + PROJ_ROWS
        copy(up_copies, source.at[pl.ds(at, GROUP)], up.at[spot(k_second, 3)], up_sem)
    for i in range(8):
        for j in range(4):
            copy(
                down_copies,
                down_all.at[i, j],
                down.at[pl.ds(j * width + i * DOWN_ROWS, DOWN_ROWS)],
                down_sem,
            )

    def vector(i):
        row, at = i // 3, (i % 3) * GROUP
        return jnp.concatenate(
            [vec_ref[j, row : row + 1, at : at + GROUP] for j in range(4)], axis=1
        )

    up_bias = jnp.concatenate(
        [
            part
            for j in range(4)
            for part in (vec_ref[j, 2:3, 2 * GROUP : 3 * GROUP], vec_ref[j, 3:4, :])
        ],
        axis=1,
    )
    proj_bias, gain1, bias1, down_bias, gain2, bias2 = [vector(i) for i in range(2, 8)]
    upb_ref[...] = up_bias
    for mb in range(2):
        att_ref[mb * GROUP : (mb + 1) * GROUP, :] = jnp.concatenate(
            [a_ref[4 * mb + j] for j in range(4)], axis=1
        )
    tokens = jnp.concatenate([tok_ref[0], tok_ref[1]], axis=0).astype(jnp.float32)
    cot = jnp.concatenate([cot_ref[0], cot_ref[1]], axis=0).astype(jnp.float32)
    keep = keep_ref[...]

    for made in proj_copies:
        made.wait()
    mixed = tokens + dot(att_ref[...], proj[...]) + proj_bias
    normal1, scale1 = norm(mixed)
    hidden = normal1 * gain1 + bias1
    hid_ref[...] = hidden.astype(jnp.bfloat16)

    def by_core(value):
        for i in range(8):
            at = 4 * ((i & 1) ^ (me & 1)) + (i >> 1)
            hid_t[pl.ds(pl.multiple_of(at * 96, 96), 96), :] = value[i * 96 : (i + 1) * 96]

    def out_columns(cols, grad):
        keep_cols[:, cols] = dot(hid_t[0:FF_CUT], grad).astype(jnp.bfloat16)
        give_cols[:, cols] = dot(hid_t[FF_CUT:], grad).astype(jnp.bfloat16)

    by_core(flip(hid_ref[...]))
    for made in up_copies:
        made.wait()
    for made in down_copies:
        made.wait()

    def forward(j, branch):
        cols = pl.ds(pl.multiple_of(j * FF_STEP, FF_STEP), FF_STEP)
        inner = dot(hid_ref[...], up[:, cols]) + upb_ref[:, cols]
        share, bell = gelu_parts(inner)
        slope[:, cols] = share + inner * bell * (1.0 / math.sqrt(2.0 * math.pi))
        active = (inner * share).astype(jnp.bfloat16)
        act_ref[:, cols] = active
        return branch + dot(active, down[cols, :])

    branch = lax.fori_loop(0, 6, forward, jnp.zeros((2 * GROUP, width), jnp.float32))
    normal2, scale2 = norm(hidden + branch + down_bias)
    result = normal2 * gain2 + bias2
    block = (keep * result + (1.0 - keep) * tokens).astype(jnp.bfloat16)
    block_ref[0] = block[:GROUP]
    block_ref[1] = block[GROUP:]
    grad = keep * cot
    grad_sum = norm_back(grad * gain2, normal2, scale2)
    grad_branch = grad_sum.astype(jnp.bfloat16)
    gb_ref[...] = grad_branch

    def add_up(value):
        return jnp.sum(value, axis=0, keepdims=True)

    sums_ref[3:4, :] = add_up(grad_branch.astype(jnp.float32))
    sums_ref[4:5, :] = add_up(grad * normal2)
    sums_ref[5:6, :] = add_up(grad)

    def backward(j, total):
        cols = pl.ds(pl.multiple_of(j * FF_STEP, FF_STEP), FF_STEP)
        grad_inner = (dot_nt(gb_ref[...], down[cols, :]) * slope[:, cols]).astype(jnp.bfloat16)
        out_columns(cols, grad_inner)
        rows_ref[cols, :] = dot(flip(act_ref[:, cols]), gb_ref[...]).astype(
            jnp.bfloat16
        )
        upb_ref[:, cols] = add_up(grad_inner.astype(jnp.float32))
        return total + dot_nt(grad_inner, up[:, cols])

    grad_hidden = lax.fori_loop(0, 6, backward, grad_sum)
    sums_ref[1:2, :] = add_up(grad_hidden * normal1)
    sums_ref[2:3, :] = add_up(grad_hidden)
    grad_mixed = norm_back(grad_hidden * gain1, normal1, scale1)
    base_ref[...] = keep * grad_mixed + (1.0 - keep) * cot
    grad_proj = grad_mixed.astype(jnp.bfloat16)
    by_core(flip(att_ref[...]))
    out_columns(slice(4 * width, 5 * width), grad_proj)
    sums_ref[0:1, :] = add_up(grad_proj.astype(jnp.float32))
    sums_ref[6:8, :] = jnp.zeros((2, width), jnp.float32)
    lane = lax.broadcasted_iota(jnp.int32, (width, 128), 1)
    vectors = jnp.concatenate(
        [jnp.transpose(sums_ref[...]), jnp.zeros((width, 120), jnp.float32)], axis=1
    )
    column = jnp.transpose(jnp.broadcast_to(upb_ref[...], (8, 4 * width)))[:, 0:1]
    for j in range(4):
        part = jnp.concatenate(
            [column[i * 96 + j * 24 : i * 96 + (j + 1) * 24] for i in range(32)], axis=0
        )
        vectors = jnp.where(lane == 6 + j, part, vectors)
    for i in range(8):
        at = 4 * ((i & 1) ^ (me & 1)) + (i >> 1)
        turned[pl.ds(pl.multiple_of(at * 96, 96), 96), :] = vectors[i * 96 : (i + 1) * 96].astype(
            jnp.bfloat16
        )
    keep_cols[:, 5 * width :] = turned[0:FF_CUT]
    give_cols[:, 5 * width :] = turned[FF_CUT:]
    grad_att = dot_nt(grad_proj, proj[...]).astype(jnp.bfloat16)
    for mb in range(2):
        for j in range(4):
            ga_ref[4 * mb + j] = grad_att[
                mb * GROUP : (mb + 1) * GROUP, j * GROUP : (j + 1) * GROUP
            ]


def dense(*ins):
    rows, width, hidden = 2 * GROUP, 4 * GROUP, 16 * GROUP
    outs = [
        ((2, GROUP, width), LOW),
        ((rows, width), WIDE),
        ((8, GROUP, GROUP), LOW),
        ((hidden, width), LOW),
        ((FF_CUT, COLUMNS), LOW),
        ((FF_CUT, COLUMNS), LOW),
    ]
    scratch = [
        pltpu.VMEM((width, hidden), LOW),
        pltpu.VMEM((hidden, width), LOW),
        pltpu.VMEM((width, width), LOW),
        pltpu.VMEM((rows, hidden), WIDE),
        pltpu.VMEM((rows, hidden), LOW),
        pltpu.VMEM((rows, width), LOW),
        pltpu.VMEM((rows, width), LOW),
        pltpu.VMEM((width, rows), LOW),
        pltpu.VMEM((rows, width), LOW),
        pltpu.VMEM((8, width), WIDE),
        pltpu.VMEM((1, hidden), WIDE),
        pltpu.VMEM((width, 128), LOW),
        pltpu.SemaphoreType.DMA((25,)),
        pltpu.SemaphoreType.DMA((33,)),
        pltpu.SemaphoreType.DMA((32,)),
    ]
    return call(dense_kernel, "dense", ins, outs, scratch, any_ins=5, flops=2 * 10**10)


def take(value, at, axis):
    return lax.dynamic_index_in_dim(value, at, axis, keepdims=False)


def halve(value, at, axis, send):
    kept = take(value, at, axis).astype(jnp.float32)
    return (kept + send(take(value, 1 - at, axis)).astype(jnp.float32)).astype(jnp.bfloat16)


def scatter_plane(value, me):
    across, along = (me >> 1) & 1, me >> 2
    value = value.reshape(2, 2, 96, COLUMNS)
    left = halve(value[..., :LEFT], across, 1, lambda v: from_ctx(v, 2))
    right = halve(value[..., LEFT:], along, 0, lambda v: from_ctx(v, 4))
    return left, right


def scatter_plane_end(left, right, me):
    across, along = (me >> 1) & 1, me >> 2
    left = halve(left, along, 0, lambda v: from_ctx(v, 4))
    right = halve(right, across, 0, lambda v: from_ctx(v, 2))
    return jnp.concatenate([left, right], axis=1)


def scatter_depth(value, depth):
    return halve(value.reshape(2, 2, 24, value.shape[1]), depth & 1, 1, lambda v: from_fsdp(v, 1))


def scatter_depth_end(value, depth):
    kept = take(value, depth >> 1, 0).astype(jnp.float32)
    return kept + from_fsdp(take(value, 1 - (depth >> 1), 0), 2).astype(jnp.float32)


def fast_on_device(
    tokens,
    doc_ids,
    keep_mask,
    qkv_weight,
    query_bias,
    value_bias,
    proj_weight,
    proj_bias,
    norm1_gain,
    norm1_bias,
    up_weight,
    up_bias,
    down_weight,
    down_bias,
    norm2_gain,
    norm2_bias,
    cotangent,
):
    low = jnp.bfloat16
    me = lax.axis_index("ctx")
    height = me >> 2
    group = me & 3
    depth = lax.axis_index("fsdp")
    place = jnp.stack([me, depth] + [jnp.int32(k) for k in ARRIVAL])
    rows = tokens[:, 0]
    ids = doc_ids[:, 0]
    features = rows.shape[2]

    id_rows = jnp.pad(ids.astype(low)[:, None, :], ((0, 0), (0, ID_ROWS - 1), (0, features - GROUP)))
    marked = jnp.concatenate([rows, id_rows], axis=1)
    own = take(marked, height, 0)
    at = group * GROUP
    columns = jnp.concatenate(
        [lax.dynamic_slice_in_dim(qkv_weight, part * features + at, GROUP, 1) for part in range(3)],
        axis=1,
    )
    vectors = jnp.concatenate(
        [
            query_bias,
            value_bias,
            proj_bias,
            norm1_gain,
            norm1_bias,
            down_bias,
            norm2_gain,
            norm2_bias,
            up_bias,
        ]
    ).reshape(4, 3 * GROUP)
    columns = jnp.concatenate([columns, vectors, jnp.zeros((4, 3 * GROUP), low)], axis=0)
    came = from_ctx(take(marked, 1 - height, 0), 4)
    across = from_ctx(own, 2)
    near, mid = from_fsdp(columns, 1), from_fsdp(columns, 2)
    own, came, across, near, mid = lax.optimization_barrier((own, came, across, near, mid))
    far = from_fsdp(columns, 3)
    four = jnp.stack([own, came, across, from_ctx(came, 2)])
    four, far = lax.optimization_barrier((four, far))
    eight = from_ctx(four, 1)

    down_cut = lax.dynamic_slice_in_dim(down_weight, me * DOWN_ROWS, DOWN_ROWS, 0)
    down_all = lax.all_gather(down_cut, ("ctx", "fsdp"), axis=0).reshape(8, 4, DOWN_ROWS, features)
    up_cut = lax.dynamic_slice_in_dim(up_weight, me * FF_CUT, FF_CUT, 1)
    proj_cut = lax.dynamic_slice(
        proj_weight, ((me >> 1) * PROJ_ROWS, (me & 1) * FF_CUT), (PROJ_ROWS, FF_CUT)
    )
    cut = jnp.concatenate([up_cut, proj_cut], axis=0)

    documents = jnp.arange(NDOC, dtype=jnp.int32)
    keep_rows = jnp.sum(
        jnp.where(ids[:, :, None] == documents, keep_mask[:, 0][:, None, :], 0), axis=2
    ).astype(jnp.float32).reshape(2 * GROUP, 1)

    cut, four = lax.optimization_barrier((cut, four))
    cuts = [from_fsdp(cut, m) for m in (1, 2, 3)]
    made = project(place, four, eight, columns, near, mid, far)
    qt, ka = list(made[:3]), made[3:6]
    vt, qkv_mine, vec = made[6:]
    ot = [None] * 3
    turned = qt
    qt = [None] * 3
    qt[0], qt[1], ot[0], ot[1] = attend((0, 1), place, *turned[:2], *ka[:2], vt)
    last, ot[1], *cuts = lax.optimization_barrier((turned[2], ot[1], *cuts))
    cuts = jnp.concatenate(cuts, axis=0)
    first, second = cuts[:FIRST], cuts[FIRST:]
    both = [first, from_ctx(first, 2), second, from_ctx(second, 4)]
    qt[2], ot[2], o = attend((2,), place, last, ka[2], vt, ot[0], ot[1])
    o, *both = lax.optimization_barrier((o, *both))
    first = jnp.concatenate(both[:2], axis=0)
    second = jnp.concatenate(both[2:], axis=0)
    first_far, second_far = from_ctx(first, 4), from_ctx(second, 2)
    held = jnp.concatenate([first, first_far, second, second_far], axis=0)
    held_too = from_ctx(held, 1)
    xt, qn, kt, *va, by_head = turn(four, eight, *turned[:2], last, *ka, vt, qkv_mine)
    heads = lax.all_to_all(o, "ctx", 0, 0, tiled=True)
    heads, xt, qn, kt, *va, by_head = lax.optimization_barrier((heads, xt, qn, kt, *va, by_head))
    block_rows, base, grad_heads, grad_down, kept, given = dense(
        place,
        heads,
        rows,
        cotangent[:, 0],
        keep_rows,
        vec,
        proj_weight,
        up_weight,
        down_all,
        held,
        held_too,
    )
    grad_o = lax.all_to_all(grad_heads, "ctx", 0, 0, tiled=True)
    down_part = lax.psum_scatter(grad_down, "ctx", scatter_dimension=0, tiled=True)
    each = features // 32
    both = (kept.astype(jnp.float32) + from_ctx(given, 1).astype(jnp.float32)).astype(low)
    grad_o, both = lax.optimization_barrier((grad_o, both))
    left, right = scatter_plane(both, me)
    shared = (place, grad_o, kt, qn, xt)
    sent, grads = attend_back((0, 1), *shared, *ot[:2], *qt[:2], *ka[:2], *va[:2])
    last, left, right, grads = lax.optimization_barrier((qt[2], left, right, grads))
    both = scatter_plane_end(left, right, me)
    came_first = lax.all_to_all(sent, ("ctx", "fsdp"), 0, 0, tiled=True)
    sent, kept, given, _ = attend_back(
        (2,), *shared, ot[2], last, ka[2], va[2], grads, by_head
    )
    given, both, came_first, down_part = lax.optimization_barrier(
        (given, both, came_first, down_part)
    )
    both = scatter_depth(both, depth)
    out_down = lax.psum_scatter(down_part, "fsdp", scatter_dimension=0, tiled=True).astype(
        jnp.float32
    )

    half = (kept.astype(jnp.float32) + from_ctx(given, 1).astype(jnp.float32)).astype(low)
    half, sent = lax.optimization_barrier((half, sent))
    quarter = half[:2].astype(jnp.float32) + from_ctx(half[2:], 2).astype(jnp.float32)
    quarter, both, out_down = lax.optimization_barrier((quarter, both, out_down))
    both = scatter_depth_end(both, depth)
    out_up, out_proj = both[:, : 4 * features], both[:, 4 * features : 5 * features]
    vectors = both[:, 5 * features :]
    mine = quarter[0]
    swapped = from_ctx(quarter[1].astype(low), 4).astype(jnp.float32)
    first = height == 0
    back = jnp.concatenate(
        [jnp.where(first, mine, swapped), jnp.where(first, swapped, mine)], axis=0
    )
    grad_tokens = base + keep_rows * back

    came_last = lax.all_to_all(sent, ("ctx", "fsdp"), 0, 0, tiled=True)
    came = []
    for value in (came_first, came_last):
        value = value.reshape(2, 4, 4, 32, -1).astype(jnp.float32)
        came.append(jnp.sum(value, axis=(0, 2)))
    came = jnp.concatenate(came, axis=2)
    out_qkv = came[:, :each].reshape(4, each, HEADS_EACH, 3, HEAD).transpose(1, 3, 0, 2, 4)
    out_qkv = out_qkv.reshape(each, 3 * features)
    head_bias = (came[:, each] + came[:, each + 1]).reshape(4, HEADS_EACH, 3, HEAD)
    at = (4 * me + depth) * each
    out_query_bias = lax.dynamic_slice_in_dim(head_bias[:, :, 0].reshape(features), at, each)
    out_value_bias = lax.dynamic_slice_in_dim(head_bias[:, :, 2].reshape(features), at, each)

    return (
        block_rows.reshape(2, 1, GROUP, features),
        grad_tokens.reshape(2, 1, GROUP, features),
        out_qkv,
        out_query_bias,
        out_value_bias,
        out_proj,
        vectors[:, 0],
        vectors[:, 1],
        vectors[:, 2],
        out_up,
        vectors[:, 6:10].T.reshape(4 * each),
        out_down,
        vectors[:, 3],
        vectors[:, 4],
        vectors[:, 5],
    )


def solution(mesh):
    in_specs = (
        P(None, "fsdp", "ctx", None),
        P(None, "fsdp", "ctx"),
        P(None, "fsdp", None),
        P("fsdp", None),
        P("fsdp"),
        P("fsdp"),
        P("fsdp", None),
        P("fsdp"),
        P("fsdp"),
        P("fsdp"),
        P("fsdp", None),
        P("fsdp"),
        P("fsdp", None),
        P("fsdp"),
        P("fsdp"),
        P("fsdp"),
        P(None, "fsdp", "ctx", None),
    )
    out_specs = (
        P(None, "fsdp", "ctx", None),
        P(None, "fsdp", "ctx", None),
        P(("ctx", "fsdp"), None),
        P(("ctx", "fsdp")),
        P(("ctx", "fsdp")),
        P(("ctx", "fsdp"), None),
        P(("ctx", "fsdp")),
        P(("ctx", "fsdp")),
        P(("ctx", "fsdp")),
        P(("ctx", "fsdp"), None),
        P(("ctx", "fsdp")),
        P(("ctx", "fsdp"), None),
        P(("ctx", "fsdp")),
        P(("ctx", "fsdp")),
        P(("ctx", "fsdp")),
    )
    work = fast_on_device if fits(mesh) else on_device
    return jax.shard_map(
        work, mesh=mesh, in_specs=in_specs, out_specs=out_specs, check_vma=False
    )
```

```python
import functools
import math

import jax
import jax.numpy as jnp
from jax import lax
from jax.experimental import pallas as pl
from jax.experimental.pallas import tpu as pltpu
from jax.sharding import PartitionSpec as P

H = 12
NDOC = 4


epsilon = 1e-05
score_scale = 0.125
masked_score = -1e30


def layer_norm(values, gain_vec, offset_vec):
    centre = jnp.mean(values, axis=-1, keepdims=True)
    centred = values - centre
    spread = jnp.mean(centred * centred, axis=-1, keepdims=True)
    return centred * lax.rsqrt(spread + epsilon) * gain_vec + offset_vec


def exact_gelu(values):
    return jax.nn.gelu(values, approximate=False)


def in_blocks(stepper, carried, portion, shard_rows):
    total_rows = portion[0].shape[0]
    shard_count = total_rows // shard_rows
    limit_rows = max(1, 1024 // shard_rows)
    grouped = math.gcd(shard_count, 1 << limit_rows.bit_length() - 1)
    block_rows = grouped * shard_rows
    turn_count = total_rows // block_rows
    stacked = tuple(
        (member.reshape((turn_count, block_rows) + member.shape[1:]) for member in portion)
    )
    offsets = block_rows * jnp.arange(turn_count, dtype=jnp.int32)

    def one_turn(inner_state, element):
        return (stepper(inner_state, element[0], element[1]), None)

    carried, ignored = lax.scan(one_turn, carried, (stacked, offsets))
    return carried


def micro_step(token_rows, slot_ids, keep_flags, weights_full, grad_rows):
    (
        qkv_weight,
        query_bias,
        value_bias,
        proj_weight,
        proj_bias,
        norm1_gain,
        norm1_bias,
        up_weight,
        up_bias,
        down_weight,
        down_bias,
        norm2_gain,
        norm2_bias,
    ) = weights_full
    local_rows, features = token_rows.shape
    num_heads = H
    head_size = features // num_heads
    documents = jnp.arange(NDOC, dtype=jnp.int32)
    keep_rows = jnp.sum(
        jnp.where(slot_ids[:, None] == documents[None, :], keep_flags[None, :], 0), axis=1
    ).astype(jnp.float32)[:, None]
    token_float = token_rows.astype(jnp.float32)
    slot_labels = slot_ids.astype(jnp.float32).astype(jnp.bfloat16)
    projected = jnp.dot(token_rows, qkv_weight, preferred_element_type=jnp.float32)
    query_rows = (projected[:, :features] + query_bias.astype(jnp.float32)).astype(jnp.bfloat16)
    key_rows = projected[:, features : 2 * features].astype(jnp.bfloat16)
    value_rows = (projected[:, 2 * features :] + value_bias.astype(jnp.float32)).astype(
        jnp.bfloat16
    )
    query_heads = query_rows.reshape(local_rows, num_heads, head_size)
    key_heads_local = key_rows.reshape(local_rows, num_heads, head_size)
    value_heads_local = value_rows.reshape(local_rows, num_heads, head_size)

    def forward_step(carried, portion, offset):
        key_part, value_part, id_part = portion
        running_max, running_sum, running_out = carried
        scores = (
            jnp.einsum(
                "qhd,khd->hqk",
                query_heads,
                key_part.reshape(-1, num_heads, head_size),
                preferred_element_type=jnp.float32,
            )
            * score_scale
        )
        same_doc = (slot_labels[:, None] == id_part[None, :])[None]
        scores = jnp.where(same_doc, scores, masked_score)
        new_max = jnp.maximum(running_max, jnp.max(scores, axis=-1))
        factor = jnp.exp(running_max - new_max)
        weights = jnp.where(same_doc, jnp.exp(scores - new_max[..., None]), 0.0)
        running_sum = running_sum * factor + jnp.sum(weights, axis=-1)
        running_out = running_out * factor[..., None] + jnp.einsum(
            "hqk,khd->hqd",
            weights.astype(jnp.bfloat16),
            value_part.reshape(-1, num_heads, head_size),
            preferred_element_type=jnp.float32,
        )
        return (new_max, running_sum, running_out)

    start_state = (
        jnp.full((num_heads, local_rows), masked_score, jnp.float32),
        jnp.zeros((num_heads, local_rows), jnp.float32),
        jnp.zeros((num_heads, local_rows, head_size), jnp.float32),
    )
    running_max, running_sum, running_out = in_blocks(
        forward_step,
        start_state,
        (
            lax.all_gather(key_rows, "ctx", axis=0, tiled=True),
            lax.all_gather(value_rows, "ctx", axis=0, tiled=True),
            lax.all_gather(slot_labels, "ctx", axis=0, tiled=True),
        ),
        local_rows,
    )
    attended = jnp.transpose(running_out / running_sum[..., None], (1, 0, 2))
    log_total = running_max + jnp.log(running_sum)
    attended_low = attended.reshape(local_rows, features).astype(jnp.bfloat16)
    projection = jnp.dot(
        attended_low, proj_weight, preferred_element_type=jnp.float32
    ) + proj_bias.astype(jnp.float32)
    hidden, norm1_back = jax.vjp(
        layer_norm,
        token_float + projection,
        norm1_gain.astype(jnp.float32),
        norm1_bias.astype(jnp.float32),
    )
    hidden_low = hidden.astype(jnp.bfloat16)
    inner_rows = jnp.dot(
        hidden_low, up_weight, preferred_element_type=jnp.float32
    ) + up_bias.astype(jnp.float32)
    active, gelu_back = jax.vjp(exact_gelu, inner_rows)
    active_low = active.astype(jnp.bfloat16)
    branch = jnp.dot(
        active_low, down_weight, preferred_element_type=jnp.float32
    ) + down_bias.astype(jnp.float32)
    result, norm2_back = jax.vjp(
        layer_norm, hidden + branch, norm2_gain.astype(jnp.float32), norm2_bias.astype(jnp.float32)
    )
    block_rows = (keep_rows * result + (1.0 - keep_rows) * token_float).astype(jnp.bfloat16)
    grad_float = grad_rows.astype(jnp.float32)
    grad_sum, grad_gain2, grad_bias2 = norm2_back(keep_rows * grad_float)
    grad_branch = grad_sum.astype(jnp.bfloat16)
    grad_down = jnp.einsum("rf,rd->fd", active_low, grad_branch, preferred_element_type=jnp.float32)
    grad_down_bias = jnp.sum(grad_branch.astype(jnp.float32), axis=0)
    (grad_inner,) = gelu_back(
        jnp.einsum("rd,fd->rf", grad_branch, down_weight, preferred_element_type=jnp.float32)
    )
    grad_inner_low = grad_inner.astype(jnp.bfloat16)
    grad_up = jnp.einsum(
        "rd,rf->df", hidden_low, grad_inner_low, preferred_element_type=jnp.float32
    )
    grad_up_bias = jnp.sum(grad_inner_low.astype(jnp.float32), axis=0)
    grad_hidden = grad_sum + jnp.einsum(
        "rf,df->rd", grad_inner_low, up_weight, preferred_element_type=jnp.float32
    )
    grad_mixed, grad_gain1, grad_bias1 = norm1_back(grad_hidden)
    grad_proj_low = grad_mixed.astype(jnp.bfloat16)
    grad_proj = jnp.einsum(
        "re,rd->ed", attended_low, grad_proj_low, preferred_element_type=jnp.float32
    )
    grad_proj_bias = jnp.sum(grad_proj_low.astype(jnp.float32), axis=0)
    grad_attended = jnp.einsum(
        "rd,ed->re", grad_proj_low, proj_weight, preferred_element_type=jnp.float32
    ).astype(jnp.bfloat16)
    grad_heads = grad_attended.reshape(local_rows, num_heads, head_size)
    row_delta = jnp.transpose(jnp.sum(grad_heads.astype(jnp.float32) * attended, axis=-1))

    def query_step(carried, portion, offset):
        key_part, value_part, id_part = portion
        key_heads = key_part.reshape(-1, num_heads, head_size)
        scores = (
            jnp.einsum("qhd,khd->hqk", query_heads, key_heads, preferred_element_type=jnp.float32)
            * score_scale
        )
        same_doc = (slot_labels[:, None] == id_part[None, :])[None]
        scores = jnp.where(same_doc, scores, masked_score)
        probs = jnp.where(same_doc, jnp.exp(scores - log_total[..., None]), 0.0)
        grad_probs = jnp.einsum(
            "qhd,khd->hqk",
            grad_heads,
            value_part.reshape(-1, num_heads, head_size),
            preferred_element_type=jnp.float32,
        )
        grad_scores = (probs * (grad_probs - row_delta[..., None])).astype(jnp.bfloat16)
        return carried + jnp.einsum(
            "hqk,khd->qhd", grad_scores, key_heads, preferred_element_type=jnp.float32
        )

    grad_query_sum = in_blocks(
        query_step,
        jnp.zeros((local_rows, num_heads, head_size), jnp.float32),
        (
            lax.all_gather(key_rows, "ctx", axis=0, tiled=True),
            lax.all_gather(value_rows, "ctx", axis=0, tiled=True),
            lax.all_gather(slot_labels, "ctx", axis=0, tiled=True),
        ),
        local_rows,
    )
    log_rows, delta_rows = (
        lax.all_gather(jnp.transpose(log_total), "ctx", axis=0, tiled=True),
        lax.all_gather(jnp.transpose(row_delta), "ctx", axis=0, tiled=True),
    )

    def key_step(carried, portion, offset):
        query_part, grad_part, id_part = portion
        grad_key_sum, grad_value_sum = carried
        span_rows = query_part.shape[0]
        log_part = lax.dynamic_slice_in_dim(log_rows, offset, span_rows, 0)
        delta_part = lax.dynamic_slice_in_dim(delta_rows, offset, span_rows, 0)
        query_part_heads = query_part.reshape(-1, num_heads, head_size)
        grad_part_heads = grad_part.reshape(-1, num_heads, head_size)
        scores = (
            jnp.einsum(
                "qhd,khd->hqk",
                query_part_heads,
                key_heads_local,
                preferred_element_type=jnp.float32,
            )
            * score_scale
        )
        same_doc = (id_part[:, None] == slot_labels[None, :])[None]
        scores = jnp.where(same_doc, scores, masked_score)
        probs = jnp.where(same_doc, jnp.exp(scores - jnp.transpose(log_part)[..., None]), 0.0)
        grad_value_sum = grad_value_sum + jnp.einsum(
            "hqk,qhd->khd",
            probs.astype(jnp.bfloat16),
            grad_part_heads,
            preferred_element_type=jnp.float32,
        )
        grad_probs = jnp.einsum(
            "qhd,khd->hqk", grad_part_heads, value_heads_local, preferred_element_type=jnp.float32
        )
        grad_scores = (probs * (grad_probs - jnp.transpose(delta_part)[..., None])).astype(
            jnp.bfloat16
        )
        grad_key_sum = grad_key_sum + jnp.einsum(
            "hqk,qhd->khd", grad_scores, query_part_heads, preferred_element_type=jnp.float32
        )
        return (grad_key_sum, grad_value_sum)

    zero_heads = jnp.zeros((local_rows, num_heads, head_size), jnp.float32)
    grad_key_sum, grad_value_sum = in_blocks(
        key_step,
        (zero_heads, zero_heads),
        (
            lax.all_gather(query_rows, "ctx", axis=0, tiled=True),
            lax.all_gather(grad_attended, "ctx", axis=0, tiled=True),
            lax.all_gather(slot_labels, "ctx", axis=0, tiled=True),
        ),
        local_rows,
    )
    grad_query = (grad_query_sum * score_scale).reshape(local_rows, features).astype(jnp.bfloat16)
    grad_key = (grad_key_sum * score_scale).reshape(local_rows, features).astype(jnp.bfloat16)
    grad_value = grad_value_sum.reshape(local_rows, features).astype(jnp.bfloat16)
    grad_projected = jnp.concatenate([grad_query, grad_key, grad_value], axis=1)
    grad_qkv = jnp.einsum(
        "rd,re->de", token_rows, grad_projected, preferred_element_type=jnp.float32
    )
    grad_query_bias = jnp.sum(grad_query.astype(jnp.float32), axis=0)
    grad_value_bias = jnp.sum(grad_value.astype(jnp.float32), axis=0)
    grad_input = grad_mixed + jnp.einsum(
        "re,de->rd", grad_projected, qkv_weight, preferred_element_type=jnp.float32
    )
    grad_tokens = keep_rows * grad_input + (1.0 - keep_rows) * grad_float
    terms = (
        grad_qkv,
        grad_query_bias,
        grad_value_bias,
        grad_proj,
        grad_proj_bias,
        grad_gain1,
        grad_bias1,
        grad_up,
        grad_up_bias,
        grad_down,
        grad_down_bias,
        grad_gain2,
        grad_bias2,
    )
    return (block_rows, grad_tokens, terms)


def on_device(
    tokens,
    doc_ids,
    keep_mask,
    qkv_weight,
    query_bias,
    value_bias,
    proj_weight,
    proj_bias,
    norm1_gain,
    norm1_bias,
    up_weight,
    up_bias,
    down_weight,
    down_bias,
    norm2_gain,
    norm2_bias,
    cotangent,
):
    block_list = []
    grad_list = []
    summed = None
    for micro_index in range(tokens.shape[0]):
        weights_full = (
            lax.all_gather(qkv_weight, "fsdp", axis=0, tiled=True),
            lax.all_gather(query_bias, "fsdp", axis=0, tiled=True),
            lax.all_gather(value_bias, "fsdp", axis=0, tiled=True),
            lax.all_gather(proj_weight, "fsdp", axis=0, tiled=True),
            lax.all_gather(proj_bias, "fsdp", axis=0, tiled=True),
            lax.all_gather(norm1_gain, "fsdp", axis=0, tiled=True),
            lax.all_gather(norm1_bias, "fsdp", axis=0, tiled=True),
            lax.all_gather(up_weight, "fsdp", axis=0, tiled=True),
            lax.all_gather(up_bias, "fsdp", axis=0, tiled=True),
            lax.all_gather(down_weight, "fsdp", axis=0, tiled=True),
            lax.all_gather(down_bias, "fsdp", axis=0, tiled=True),
            lax.all_gather(norm2_gain, "fsdp", axis=0, tiled=True),
            lax.all_gather(norm2_bias, "fsdp", axis=0, tiled=True),
        )
        block_rows, grad_tokens, terms = micro_step(
            tokens[micro_index, 0],
            doc_ids[micro_index, 0],
            keep_mask[micro_index, 0],
            weights_full,
            cotangent[micro_index, 0],
        )
        block_list.append(block_rows)
        grad_list.append(grad_tokens)
        if summed is None:
            summed = terms
        else:
            summed = tuple((earlier + later for earlier, later in zip(summed, terms)))
    reduced = (
        lax.psum_scatter(summed[0], ("ctx", "fsdp"), scatter_dimension=0, tiled=True),
        lax.psum_scatter(summed[1], ("ctx", "fsdp"), scatter_dimension=0, tiled=True),
        lax.psum_scatter(summed[2], ("ctx", "fsdp"), scatter_dimension=0, tiled=True),
        lax.psum_scatter(summed[3], ("ctx", "fsdp"), scatter_dimension=0, tiled=True),
        lax.psum_scatter(summed[4], ("ctx", "fsdp"), scatter_dimension=0, tiled=True),
        lax.psum_scatter(summed[5], ("ctx", "fsdp"), scatter_dimension=0, tiled=True),
        lax.psum_scatter(summed[6], ("ctx", "fsdp"), scatter_dimension=0, tiled=True),
        lax.psum_scatter(summed[7], ("ctx", "fsdp"), scatter_dimension=0, tiled=True),
        lax.psum_scatter(summed[8], ("ctx", "fsdp"), scatter_dimension=0, tiled=True),
        lax.psum_scatter(summed[9], ("ctx", "fsdp"), scatter_dimension=0, tiled=True),
        lax.psum_scatter(summed[10], ("ctx", "fsdp"), scatter_dimension=0, tiled=True),
        lax.psum_scatter(summed[11], ("ctx", "fsdp"), scatter_dimension=0, tiled=True),
        lax.psum_scatter(summed[12], ("ctx", "fsdp"), scatter_dimension=0, tiled=True),
    )
    block_out = jnp.stack(block_list)[:, None]
    grad_tokens_all = jnp.stack(grad_list)[:, None]
    return (
        block_out,
        grad_tokens_all,
        reduced[0],
        reduced[1],
        reduced[2],
        reduced[3],
        reduced[4],
        reduced[5],
        reduced[6],
        reduced[7],
        reduced[8],
        reduced[9],
        reduced[10],
        reduced[11],
        reduced[12],
    )


MASKED = -1e30
LOWEST = -3e38
ARRIVAL = (0, 4, 2, 6, 1, 5, 3, 7)
GROUP = 192
HEAD = 64
HEADS_EACH = 3
PAIR = 384
SLOTS = 1536
ID_ROWS = 8


def fits(mesh):
    return mesh.shape["ctx"] == 8 and mesh.shape["fsdp"] == 4


def dot(a, b):
    return lax.dot_general(a, b, (((1,), (0,)), ((), ())), preferred_element_type=jnp.float32)


def dot_nt(a, b):
    return lax.dot_general(a, b, (((1,), (1,)), ((), ())), preferred_element_type=jnp.float32)


def flip(value):
    return jnp.transpose(value.astype(jnp.float32)).astype(jnp.bfloat16)


def split3(value):
    high = value.astype(jnp.bfloat16).astype(jnp.float32)
    mid = (value - high).astype(jnp.bfloat16).astype(jnp.float32)
    return high, mid, value - high - mid


def call(kernel, name, ins, outs, scratch=(), scalars=1, any_ins=0, flops=5 * 10**9, aliases=None):
    vmem = pl.BlockSpec(memory_space=pltpu.VMEM)
    return pl.pallas_call(
        kernel,
        name=name,
        out_shape=[jax.ShapeDtypeStruct(shape, kind) for shape, kind in outs],
        grid_spec=pltpu.PrefetchScalarGridSpec(
            num_scalar_prefetch=scalars,
            in_specs=[vmem] * (len(ins) - scalars - any_ins)
            + [pl.BlockSpec(memory_space=pl.ANY)] * any_ins,
            out_specs=[vmem] * len(outs),
            scratch_shapes=list(scratch),
        ),
        cost_estimate=pl.CostEstimate(flops=flops, bytes_accessed=10**7, transcendentals=10**6),
        compiler_params=pltpu.CompilerParams(vmem_limit_bytes=56 * 2**20),
    )(*ins)


QUAD = 768
TILE = 256
TILES = SLOTS // TILE


def project_kernel(place, *refs):
    x_refs = refs[:2]
    own_ref, near_ref, mid_ref, far_ref = refs[2:6]
    qt_refs, ka_refs = refs[6:9], refs[9:12]
    vt_ref, w_ref, vec_ref, turned = refs[12:]
    me, depth = place[0], place[1]
    for m, ref in enumerate((own_ref, near_ref, mid_ref, far_ref)):
        owner = depth ^ m
        rows = pl.ds(pl.multiple_of(owner * GROUP, GROUP), GROUP)
        w_ref[rows, :] = ref[0:GROUP, :]
        vec_ref[owner] = ref[GROUP : GROUP + 8, :].astype(jnp.float32)
    mine = vec_ref[me & 3]
    turned[0:GROUP] = flip(w_ref[:, 0:GROUP])
    turned[GROUP:] = flip(w_ref[:, 2 * GROUP :])
    bias = jnp.concatenate([mine[:, 0:GROUP], mine[:, GROUP : 2 * GROUP]], axis=1)
    bias = jnp.transpose(bias)[:, 0:1]
    lane = lax.broadcasted_iota(jnp.int32, (QUAD, HEAD), 1)
    row = lax.broadcasted_iota(jnp.int32, (HEAD, QUAD), 0)
    for t in range(2):
        span = slice(t * QUAD, (t + 1) * QUAD)
        x = jnp.concatenate([x_refs[t][i, 0:GROUP] for i in range(4)], axis=0)
        ids = jnp.concatenate(
            [x_refs[t][i, GROUP : GROUP + 8, 0:GROUP] for i in range(4)], axis=1
        ).astype(jnp.float32)
        id_row = ids[0:1, :]
        id_col = jnp.transpose(ids)[:, 0:1]
        k_side = jnp.where(
            lane < 5,
            jnp.where(id_col == lane.astype(jnp.float32), 0.0, MASKED),
            jnp.where(lane < 8, -1.0, 0.0),
        ).astype(jnp.bfloat16)
        q_side = jnp.where((row < 5) & (id_row == row.astype(jnp.float32)), 1.0, 0.0).astype(
            jnp.bfloat16
        )
        k = dot(x, w_ref[:, GROUP : 2 * GROUP]).astype(jnp.bfloat16)
        qv = (dot_nt(turned[...], x) + bias).astype(jnp.bfloat16)
        vt_ref[:, span] = qv[GROUP:]
        q = (qv[:GROUP] * 0.125).astype(jnp.bfloat16)
        for h in range(HEADS_EACH):
            heads = slice(h * HEAD, (h + 1) * HEAD)
            ka_refs[h][span, :] = jnp.concatenate([k[:, heads], k_side], axis=1)
            qt_refs[h][0:HEAD, span] = q[heads]
            qt_refs[h][HEAD : 2 * HEAD, span] = q_side


def turn_kernel(*refs):
    x_refs, qt_refs, ka_refs = refs[:2], refs[2:5], refs[5:8]
    vt_ref, w_ref = refs[8:10]
    xt_ref, qn_ref, kt_ref, va_refs, by_head = refs[10], refs[11], refs[12], refs[13:16], refs[16]
    lane = lax.broadcasted_iota(jnp.int32, (PAIR, HEAD), 1)
    v_side = jnp.where(lane < 3, -1.0, 0.0).astype(jnp.bfloat16)
    for t in range(4):
        span = slice(t * PAIR, (t + 1) * PAIR)
        x = jnp.concatenate([x_refs[t // 2][2 * (t % 2) + i, 0:GROUP] for i in (0, 1)], axis=0)
        xt_ref[:, span] = flip(x)
        for h in range(HEADS_EACH):
            heads = slice(h * HEAD, (h + 1) * HEAD)
            qn_ref[span, heads] = flip(qt_refs[h][0:HEAD, span])
            kt_ref[heads, span] = flip(ka_refs[h][span, 0:HEAD])
            va_refs[h][span, :] = jnp.concatenate([flip(vt_ref[heads, span]), v_side], axis=1)
    for h in range(HEADS_EACH):
        for i in range(3):
            by_head[:, (3 * h + i) * HEAD : (3 * h + i + 1) * HEAD] = w_ref[
                :, i * GROUP + h * HEAD : i * GROUP + (h + 1) * HEAD
            ]


def attend_kernel(heads, place, *refs):
    n = len(heads)
    qt_refs, ka_refs, vt_ref = refs[:n], refs[n : 2 * n], refs[2 * n]
    refs = refs[2 * n + 1 :]
    out_qt, out_ot, o_ref = refs[:n], refs[n : 2 * n], refs[2 * n]
    held = refs[-n:]
    me = place[0]
    at_row = lax.broadcasted_iota(jnp.int32, (16, TILE), 0)

    def one_tile(t, unused):
        here = pl.ds(pl.multiple_of(t * TILE, TILE), TILE)
        top = [jnp.full((8, TILE), LOWEST, jnp.float32)] * n
        total = [jnp.zeros((8, TILE), jnp.float32)] * n
        out = [jnp.zeros((HEAD, TILE), jnp.float32)] * n

        def score(i, j):
            span = slice(j * TILE, (j + 1) * TILE)
            scores = dot(ka_refs[i][span, :], qt_refs[i][:, here])
            held[i][span, :] = scores
            top[i] = jnp.maximum(top[i], jnp.max(scores.reshape(TILE // 8, 8, TILE), axis=0))

        def mix(i, j):
            span = slice(j * TILE, (j + 1) * TILE)
            h = heads[i]
            probs = jnp.exp(held[i][span, :] - top[i])
            total[i] = total[i] + jnp.sum(probs.reshape(TILE // 8, 8, TILE), axis=0)
            low = probs.astype(jnp.bfloat16)
            out[i] = out[i] + dot(vt_ref[h * HEAD : (h + 1) * HEAD, span], low)

        for i in range(n):
            for j in range(TILES):
                score(i, j)
            top[i] = jnp.max(top[i], axis=0, keepdims=True)
        for i in range(n):
            for j in range(TILES):
                mix(i, j)
        for i in range(n):
            sums = jnp.sum(total[i], axis=0, keepdims=True)
            out_ot[i][:, here] = (out[i] / sums).astype(jnp.bfloat16)
            high, mid, low = split3(top[i] + jnp.log(sums))
            side = qt_refs[i][HEAD : HEAD + 16, here].astype(jnp.float32)
            side = jnp.where(at_row == 5, high, side)
            side = jnp.where(at_row == 6, mid, side)
            side = jnp.where(at_row == 7, low, side)
            out_qt[i][0:HEAD, here] = qt_refs[i][0:HEAD, here]
            out_qt[i][HEAD : HEAD + 16, here] = side.astype(jnp.bfloat16)
            out_qt[i][HEAD + 16 :, here] = qt_refs[i][HEAD + 16 :, here]
        return unused

    lax.fori_loop(0, TILES, one_tile, 0)
    for t in range(4):
        span = slice(t * PAIR, (t + 1) * PAIR)
        rows = flip(jnp.concatenate([ref[:, span] for ref in out_ot], axis=0))
        for half in range(2):
            o_ref[me ^ ARRIVAL[2 * t + half]] = rows[half * GROUP : (half + 1) * GROUP, :]


def attend_back_kernel(heads, place, *refs):
    n = len(heads)
    do_ref, kt_ref, qn_ref, xt_ref = refs[:4]
    refs = refs[4:]
    ot_refs, qt_refs, ka_refs, va_refs = [refs[i * n : (i + 1) * n] for i in range(4)]
    refs = refs[4 * n :]
    last = heads[-1] == HEADS_EACH - 1
    if last:
        earlier_ref, w_ref = refs[:2]
        refs = refs[2:]
        sent_ref, keep_ref, give_ref, g_ref = refs[:4]
        refs = refs[4:]
    else:
        sent_ref, g_ref = refs[0], refs[1]
        refs = refs[2:]
    dot_t, don, dqt = refs
    me = place[0]
    row = lax.broadcasted_iota(jnp.int32, (HEAD, PAIR), 0)
    for t in range(4):
        here = slice(t * PAIR, (t + 1) * PAIR)
        a, b = me ^ ARRIVAL[2 * t], me ^ ARRIVAL[2 * t + 1]
        for i, h in enumerate(heads):
            cols = slice(h * HEAD, (h + 1) * HEAD)
            grad = jnp.concatenate([do_ref[a][:, cols], do_ref[b][:, cols]], axis=0)
            don[i, here, :] = grad
            grad_t = jnp.transpose(grad.astype(jnp.float32))
            delta = jnp.sum(grad_t * ot_refs[i][:, here].astype(jnp.float32), axis=0, keepdims=True)
            high, mid, low = split3(delta)
            side = jnp.where(
                row == 0, high, jnp.where(row == 1, mid, jnp.where(row == 2, low, 0.0))
            )
            dot_t[i, 0:HEAD, here] = grad_t.astype(jnp.bfloat16)
            dot_t[i, HEAD : 2 * HEAD, here] = side.astype(jnp.bfloat16)
    dqt[...] = jnp.zeros_like(dqt)

    def keys(j, unused):
        here = pl.ds(pl.multiple_of(j * TILE, TILE), TILE)
        for i, h in enumerate(heads):
            rows = slice(h * HEAD, (h + 1) * HEAD)
            key = ka_refs[i][here, :]
            val = va_refs[i][here, :]
            key_t = kt_ref[rows, here]
            dk = jnp.zeros((TILE, HEAD), jnp.float32)
            dv = jnp.zeros((TILE, HEAD), jnp.float32)
            for t in range(TILES):
                span = slice(t * TILE, (t + 1) * TILE)
                probs = jnp.exp(dot(key, qt_refs[i][:, span]))
                grad_probs = dot(val, dot_t[i, :, span])
                grad_scores = (probs * grad_probs).astype(jnp.bfloat16)
                dv = dv + dot(probs.astype(jnp.bfloat16), don[i, span, :])
                dk = dk + dot(grad_scores, qn_ref[span, rows])
                dqt[i, :, span] = dqt[i, :, span] + dot(key_t, grad_scores)
            at = i * GROUP
            g_ref[here, at + HEAD : at + 2 * HEAD] = dk.astype(jnp.bfloat16)
            g_ref[here, at + 2 * HEAD : at + GROUP] = dv.astype(jnp.bfloat16)
        return unused

    lax.fori_loop(0, TILES, keys, 0)
    bias = jnp.zeros((1, n * GROUP), jnp.float32)
    for t in range(4):
        span = slice(t * PAIR, (t + 1) * PAIR)
        for i in range(n):
            g_ref[span, i * GROUP : i * GROUP + HEAD] = (
                jnp.transpose(dqt[i, :, span]) * 0.125
            ).astype(jnp.bfloat16)
        bias = bias + jnp.sum(g_ref[span, :].astype(jnp.float32), axis=0, keepdims=True)
    high = bias.astype(jnp.bfloat16).astype(jnp.float32)
    at_row = lax.broadcasted_iota(jnp.int32, (8, n * GROUP), 0)
    fixed = jnp.where(at_row == 0, high, jnp.where(at_row == 1, bias - high, 0.0))

    def weights_back(t, unused):
        x_rows = xt_ref[pl.ds(pl.multiple_of(t * GROUP, GROUP), GROUP), :]
        part = dot(x_rows, g_ref[...]).astype(jnp.bfloat16)
        for i in range(8):
            sent_ref[8 * t + i, 0:24, :] = part[24 * i : 24 * (i + 1)]
            sent_ref[8 * t + i, 24:32, :] = fixed.astype(jnp.bfloat16)
        return unused

    lax.fori_loop(0, 4, weights_back, 0)
    if last:
        split = earlier_ref.shape[1]

        for t in range(4):
            here = slice(t * PAIR, (t + 1) * PAIR)
            back_ref, at = (keep_ref, 2 * t) if t < 2 else (give_ref, 2 * t - 4)
            part = dot_nt(earlier_ref[here, :], w_ref[:, :split])
            part = (part + dot_nt(g_ref[here, :], w_ref[:, split:])).astype(jnp.bfloat16)
            back_ref[at] = part[:GROUP]
            back_ref[at + 1] = part[GROUP:]


def collect_kernel(first_ref, last_ref, out_ref, bias_ref):
    for g in range(4):
        for ref, heads in ((first_ref, (0, 1)), (last_ref, (2,))):
            total = sum(
                ref[16 * y + 4 * g + z].astype(jnp.float32) for y in range(2) for z in range(4)
            )
            for i, h in enumerate(heads):
                for part in range(3):
                    at = i * GROUP + part * HEAD
                    to = g * GROUP + h * HEAD
                    piece = total[:, at : at + HEAD]
                    out_ref[:, part * 4 * GROUP + to : part * 4 * GROUP + to + HEAD] = piece[0:24]
                    if part != 1:
                        row = part // 2
                        bias_ref[row : row + 1, to : to + HEAD] = piece[24:25] + piece[25:26]


LOW, WIDE = jnp.bfloat16, jnp.float32


def project(*ins):
    outs = [((2 * HEAD, SLOTS), LOW)] * 3 + [((SLOTS, 2 * HEAD), LOW)] * 3
    outs += [((GROUP, SLOTS), LOW), ((4 * GROUP, 3 * GROUP), LOW), ((4, 8, 3 * GROUP), WIDE)]
    scratch = [pltpu.VMEM((2 * GROUP, 4 * GROUP), LOW)]
    return call(project_kernel, "project", ins, outs, scratch)


def turn(*ins):
    outs = [((4 * GROUP, SLOTS), LOW), ((SLOTS, GROUP), LOW), ((GROUP, SLOTS), LOW)]
    outs += [((SLOTS, 2 * HEAD), LOW)] * 3 + [((4 * GROUP, 3 * GROUP), LOW)]
    return call(turn_kernel, "turn", ins, outs, scalars=0)


def attend(heads, *ins):
    n = len(heads)
    outs = [((2 * HEAD, SLOTS), LOW)] * n + [((HEAD, SLOTS), LOW)] * n
    outs.append(((8, GROUP, GROUP), LOW))
    scratch = [pltpu.VMEM((SLOTS, TILE), WIDE)] * n
    kernel = functools.partial(attend_kernel, heads)
    return call(kernel, f"attend{heads[0]}", ins, outs, scratch)


def attend_back(heads, *ins):
    n = len(heads)
    scratch = [
        pltpu.VMEM((n, 2 * HEAD, SLOTS), LOW),
        pltpu.VMEM((n, SLOTS, HEAD), LOW),
        pltpu.VMEM((n, HEAD, SLOTS), WIDE),
    ]
    outs = [((32, 32, n * GROUP), LOW)]
    if heads[-1] == HEADS_EACH - 1:
        outs += [((4, GROUP, 4 * GROUP), LOW)] * 2
    outs.append(((SLOTS, n * GROUP), LOW))
    kernel = functools.partial(attend_back_kernel, heads)
    return call(kernel, f"attend_back{heads[0]}", ins, outs, scratch, flops=10**10)


def collect(*ins):
    outs = [((24, 12 * GROUP), WIDE), ((2, 4 * GROUP), WIDE)]
    return call(collect_kernel, "collect", ins, outs, scalars=0, flops=10**6)


def from_ctx(value, bits):
    return lax.ppermute(value, "ctx", [(i, i ^ bits) for i in range(8)])


def from_fsdp(value, bits):
    return lax.ppermute(value, "fsdp", [(i, i ^ bits) for i in range(4)])


FF_CUT = 384
PROJ_ROWS = 48
DOWN_ROWS = 96
CUT_ROWS = 432
COLUMNS = 3968
LEFT = 2048


def norm(value):
    centred = value - jnp.mean(value, axis=1, keepdims=True)
    scale = lax.rsqrt(jnp.mean(centred * centred, axis=1, keepdims=True) + epsilon)
    return centred * scale, scale


def norm_back(grad, normal, scale):
    return scale * (
        grad
        - jnp.mean(grad, axis=1, keepdims=True)
        - normal * jnp.mean(grad * normal, axis=1, keepdims=True)
    )


TAIL_AT = 0.35
TAIL = (
    0.19746588,
    0.197487361,
    0.184996341,
    0.164759887,
    0.106787389,
    0.160058898,
    -0.11534264,
    0.24699889,
    -0.186710954,
    0.0434989602,
)


def gelu_parts(value):
    bell = jnp.exp(-0.5 * value * value)
    t = 1.0 / (1.0 + (TAIL_AT * 2.0**-0.5) * jnp.abs(value))
    tail = jnp.full_like(t, 0.5 * TAIL[-1])
    for term in TAIL[-2::-1]:
        tail = tail * t + 0.5 * term
    tail = tail * t * bell
    return jnp.where(value < 0.0, tail, 1.0 - tail), bell


FF_STEP = 512


def dense_kernel(place, *refs):
    a_ref, tok_ref, cot_ref, keep_ref, vec_ref = refs[:5]
    proj_own, up_own, down_own, gathered = refs[5:9]
    block_ref, base_ref, ga_ref, rows_ref, keep_cols, give_cols = refs[9:15]
    up, down, proj, slope, act_ref, att_ref, hid_ref, hid_t, gb_ref = refs[15:24]
    sums_ref, upb_ref, turned, ordered, even, odd, branch, proj_sem, up_sem, down_sem = refs[24:]
    me, depth = place[0], place[1]
    width = 4 * GROUP
    proj_copies, up_copies, down_copies = [], [], []

    def copy(into, source, target, sem):
        made = pltpu.make_async_copy(source, target, sem.at[len(into)])
        made.start()
        into.append(made)

    def owner_rows(m, size, at, rows):
        return pl.ds(pl.multiple_of((depth ^ m) * size + at, PROJ_ROWS), rows)

    every = [(i, m) for i in range(8) for m in (1, 2, 3)]
    copy(proj_copies, proj_own, proj.at[owner_rows(0, GROUP, 0, GROUP)], proj_sem)
    for i, m in every:
        copy(
            proj_copies,
            gathered.at[i, m - 1, pl.ds(CUT_ROWS - PROJ_ROWS, PROJ_ROWS)],
            proj.at[
                owner_rows(m, GROUP, (i // 2) * PROJ_ROWS, PROJ_ROWS),
                pl.ds((i % 2) * FF_CUT, FF_CUT),
            ],
            proj_sem,
        )
    copy(up_copies, up_own, up.at[owner_rows(0, GROUP, 0, GROUP)], up_sem)
    for i, m in every:
        copy(
            up_copies,
            gathered.at[i, m - 1, pl.ds(0, GROUP)],
            up.at[owner_rows(m, GROUP, 0, GROUP), pl.ds(i * FF_CUT, FF_CUT)],
            up_sem,
        )
    copy(down_copies, down_own, down.at[owner_rows(0, width, 0, width)], down_sem)
    for i, m in every:
        for side in range(2):
            copy(
                down_copies,
                gathered.at[i, m - 1, pl.ds(GROUP + side * DOWN_ROWS, DOWN_ROWS)],
                down.at[
                    owner_rows(m, width, i * DOWN_ROWS, DOWN_ROWS), pl.ds(side * FF_CUT, FF_CUT)
                ],
                down_sem,
            )

    def vector(i):
        row, at = i // 3, (i % 3) * GROUP
        return jnp.concatenate(
            [vec_ref[j, row : row + 1, at : at + GROUP] for j in range(4)], axis=1
        )

    up_bias = jnp.concatenate(
        [
            part
            for j in range(4)
            for part in (vec_ref[j, 2:3, 2 * GROUP : 3 * GROUP], vec_ref[j, 3:4, :])
        ],
        axis=1,
    )
    proj_bias, gain1, bias1, down_bias, gain2, bias2 = [vector(i) for i in range(2, 8)]
    upb_ref[...] = up_bias
    for mb in range(2):
        att_ref[mb * GROUP : (mb + 1) * GROUP, :] = jnp.concatenate(
            [a_ref[4 * mb + j] for j in range(4)], axis=1
        )
    tokens = jnp.concatenate([tok_ref[0], tok_ref[1]], axis=0).astype(jnp.float32)
    cot = jnp.concatenate([cot_ref[0], cot_ref[1]], axis=0).astype(jnp.float32)
    keep = keep_ref[...]

    for made in proj_copies:
        made.wait()
    mixed = tokens + dot(att_ref[...], proj[...]) + proj_bias
    normal1, scale1 = norm(mixed)
    hidden = normal1 * gain1 + bias1
    hid_ref[...] = hidden.astype(jnp.bfloat16)

    def by_owner(value, target):
        for i in range(8):
            away = me ^ i
            at = (away & 1) * FF_CUT + (away >> 1) * 96
            for j in range(4):
                row = pl.multiple_of(at + (depth ^ j) * 24, 8)
                target[pl.ds(row, 24), :] = value[i * 96 + j * 24 : i * 96 + (j + 1) * 24]

    def out_columns(cols, grad):
        keep_cols[:, cols] = dot(hid_t[0:FF_CUT], grad).astype(jnp.bfloat16)
        give_cols[:, cols] = dot(hid_t[FF_CUT:], grad).astype(jnp.bfloat16)

    by_owner(jnp.transpose(hid_ref[...].astype(jnp.float32)), ordered)
    hid_t[...] = ordered[...].astype(jnp.bfloat16)
    for made in up_copies:
        made.wait()
    for made in down_copies:
        made.wait()

    def columns(j):
        return pl.ds(pl.multiple_of(j * FF_STEP, FF_STEP), FF_STEP)

    def rise(j, target):
        cols = columns(j)
        target[...] = dot(hid_ref[...], up[:, cols]) + upb_ref[:, cols]

    def fall(j, source):
        cols = columns(j)
        inner = source[...]
        share, bell = gelu_parts(inner)
        slope[:, cols] = share + inner * bell * (1.0 / math.sqrt(2.0 * math.pi))
        active = (inner * share).astype(jnp.bfloat16)
        act_ref[:, cols] = active
        branch[...] += dot(active, down[cols, :])

    def forward(i, unused):
        rise(2 * i + 1, odd)
        fall(2 * i, even)
        rise(jnp.minimum(2 * i + 2, 5), even)
        fall(2 * i + 1, odd)
        return unused

    branch[...] = jnp.broadcast_to(down_bias, branch.shape)
    rise(0, even)
    lax.fori_loop(0, 3, forward, 0)
    normal2, scale2 = norm(hidden + branch[...])
    result = normal2 * gain2 + bias2
    block = (keep * result + (1.0 - keep) * tokens).astype(jnp.bfloat16)
    block_ref[0] = block[:GROUP]
    block_ref[1] = block[GROUP:]
    grad = keep * cot
    grad_sum = norm_back(grad * gain2, normal2, scale2)
    grad_branch = grad_sum.astype(jnp.bfloat16)
    gb_ref[...] = grad_branch

    def add_up(value):
        return jnp.sum(value, axis=0, keepdims=True)

    sums_ref[3:4, :] = add_up(grad_branch.astype(jnp.float32))
    sums_ref[4:5, :] = add_up(grad * normal2)
    sums_ref[5:6, :] = add_up(grad)

    def backward(j, total):
        cols = pl.ds(pl.multiple_of(j * FF_STEP, FF_STEP), FF_STEP)
        grad_inner = (dot_nt(gb_ref[...], down[cols, :]) * slope[:, cols]).astype(jnp.bfloat16)
        out_columns(cols, grad_inner)
        rows_ref[cols, :] = dot(flip(act_ref[:, cols]), gb_ref[...]).astype(
            jnp.bfloat16
        )
        upb_ref[:, cols] = add_up(grad_inner.astype(jnp.float32))
        return total + dot_nt(grad_inner, up[:, cols])

    grad_hidden = lax.fori_loop(0, 6, backward, grad_sum)
    sums_ref[1:2, :] = add_up(grad_hidden * normal1)
    sums_ref[2:3, :] = add_up(grad_hidden)
    grad_mixed = norm_back(grad_hidden * gain1, normal1, scale1)
    base_ref[...] = keep * grad_mixed + (1.0 - keep) * cot
    grad_proj = grad_mixed.astype(jnp.bfloat16)
    by_owner(jnp.transpose(att_ref[...].astype(jnp.float32)), ordered)
    hid_t[...] = ordered[...].astype(jnp.bfloat16)
    out_columns(slice(4 * width, 5 * width), grad_proj)
    sums_ref[0:1, :] = add_up(grad_proj.astype(jnp.float32))
    sums_ref[6:8, :] = jnp.zeros((2, width), jnp.float32)
    lane = lax.broadcasted_iota(jnp.int32, (width, 128), 1)
    vectors = jnp.concatenate(
        [jnp.transpose(sums_ref[...]), jnp.zeros((width, 120), jnp.float32)], axis=1
    )
    column = jnp.transpose(jnp.broadcast_to(upb_ref[...], (8, 4 * width)))[:, 0:1]
    for j in range(4):
        part = jnp.concatenate(
            [column[i * 96 + j * 24 : i * 96 + (j + 1) * 24] for i in range(32)], axis=0
        )
        vectors = jnp.where(lane == 6 + j, part, vectors)
    by_owner(vectors, turned)
    keep_cols[:, 5 * width :] = turned[0:FF_CUT].astype(jnp.bfloat16)
    give_cols[:, 5 * width :] = turned[FF_CUT:].astype(jnp.bfloat16)
    grad_att = dot_nt(grad_proj, proj[...]).astype(jnp.bfloat16)
    for mb in range(2):
        for j in range(4):
            ga_ref[4 * mb + j] = grad_att[
                mb * GROUP : (mb + 1) * GROUP, j * GROUP : (j + 1) * GROUP
            ]


def dense(*ins):
    rows, width, hidden = 2 * GROUP, 4 * GROUP, 16 * GROUP
    outs = [
        ((2, GROUP, width), LOW),
        ((rows, width), WIDE),
        ((8, GROUP, GROUP), LOW),
        ((hidden, width), LOW),
        ((FF_CUT, COLUMNS), LOW),
        ((FF_CUT, COLUMNS), LOW),
    ]
    scratch = [
        pltpu.VMEM((width, hidden), LOW),
        pltpu.VMEM((hidden, width), LOW),
        pltpu.VMEM((width, width), LOW),
        pltpu.VMEM((rows, hidden), WIDE),
        pltpu.VMEM((rows, hidden), LOW),
        pltpu.VMEM((rows, width), LOW),
        pltpu.VMEM((rows, width), LOW),
        pltpu.VMEM((width, rows), LOW),
        pltpu.VMEM((rows, width), LOW),
        pltpu.VMEM((8, width), WIDE),
        pltpu.VMEM((1, hidden), WIDE),
        pltpu.VMEM((width, 128), WIDE),
        pltpu.VMEM((width, rows), WIDE),
        pltpu.VMEM((rows, FF_STEP), WIDE),
        pltpu.VMEM((rows, FF_STEP), WIDE),
        pltpu.VMEM((rows, width), WIDE),
        pltpu.SemaphoreType.DMA((25,)),
        pltpu.SemaphoreType.DMA((25,)),
        pltpu.SemaphoreType.DMA((49,)),
    ]
    return call(dense_kernel, "dense", ins, outs, scratch, any_ins=4, flops=2 * 10**10)


def tie(*values):
    return lax.optimization_barrier(values)


def take(value, at, axis):
    return lax.dynamic_index_in_dim(value, at, axis, keepdims=False)


def join(kept, given, send):
    return (kept.astype(jnp.float32) + send(given).astype(jnp.float32)).astype(jnp.bfloat16)


def over(bits):
    return lambda value: from_ctx(value, bits)


def scatter_plane(value):
    value = value.reshape(2, 2, 96, COLUMNS)
    left, right = value[..., :LEFT], value[..., LEFT:]
    return join(left[:, 0], left[:, 1], over(2)), join(right[0], right[1], over(4))


def scatter_plane_end(left, right):
    left, right = join(left[0], left[1], over(4)), join(right[0], right[1], over(2))
    return jnp.concatenate([left, right], axis=1).reshape(2, 2, 24, COLUMNS)


def fast_on_device(
    tokens,
    doc_ids,
    keep_mask,
    qkv_weight,
    query_bias,
    value_bias,
    proj_weight,
    proj_bias,
    norm1_gain,
    norm1_bias,
    up_weight,
    up_bias,
    down_weight,
    down_bias,
    norm2_gain,
    norm2_bias,
    cotangent,
):
    low = jnp.bfloat16
    me = lax.axis_index("ctx")
    height = me >> 2
    group = me & 3
    depth = lax.axis_index("fsdp")
    place = jnp.stack([me, depth] + [jnp.int32(k) for k in ARRIVAL])
    rows = tokens[:, 0]
    ids = doc_ids[:, 0]
    features = rows.shape[2]

    id_rows = jnp.pad(ids.astype(low)[:, None, :], ((0, 0), (0, ID_ROWS - 1), (0, features - GROUP)))
    marked = jnp.concatenate([rows, id_rows], axis=1)
    own = take(marked, height, 0)
    at = group * GROUP
    columns = jnp.concatenate(
        [lax.dynamic_slice_in_dim(qkv_weight, part * features + at, GROUP, 1) for part in range(3)],
        axis=1,
    )
    vectors = jnp.concatenate(
        [
            query_bias,
            value_bias,
            proj_bias,
            norm1_gain,
            norm1_bias,
            down_bias,
            norm2_gain,
            norm2_bias,
            up_bias,
        ]
    ).reshape(4, 3 * GROUP)
    columns = jnp.concatenate([columns, vectors, jnp.zeros((4, 3 * GROUP), low)], axis=0)
    up_cut = lax.dynamic_slice_in_dim(up_weight, me * FF_CUT, FF_CUT, 1)
    down_cut = lax.dynamic_slice_in_dim(down_weight, me * DOWN_ROWS, DOWN_ROWS, 0)
    proj_cut = lax.dynamic_slice(
        proj_weight, ((me >> 1) * PROJ_ROWS, (me & 1) * FF_CUT), (PROJ_ROWS, FF_CUT)
    )
    cut = jnp.concatenate([up_cut, down_cut[:, :FF_CUT], down_cut[:, FF_CUT:], proj_cut], axis=0)
    came = from_ctx(take(marked, 1 - height, 0), 4)
    across = from_ctx(own, 2)
    cuts = [from_fsdp(cut, m) for m in (1, 2, 3)]
    corner = from_ctx(came, 2)
    own, came, across, corner, columns, *cuts = tie(own, came, across, corner, columns, *cuts)
    gathered = lax.all_gather(jnp.stack(cuts), "ctx", axis=0)
    near, mid, far = [from_fsdp(columns, m) for m in (1, 2, 3)]
    four = jnp.stack([own, came, across, corner])
    eight = from_ctx(four, 1)

    documents = jnp.arange(NDOC, dtype=jnp.int32)
    keep_rows = jnp.sum(
        jnp.where(ids[:, :, None] == documents, keep_mask[:, 0][:, None, :], 0), axis=2
    ).astype(jnp.float32).reshape(2 * GROUP, 1)

    made = project(place, four, eight, columns, near, mid, far)
    qt, ka = list(made[:3]), made[3:6]
    vt, qkv_mine, vec = made[6:]
    turned = list(qt)
    *made, o = attend((0, 1, 2), place, *turned, *ka, vt)
    qt, ot = made[:3], made[3:]
    heads = lax.all_to_all(o, "ctx", 0, 0, tiled=True)
    xt, qn, kt, *va, by_head = turn(four, eight, *turned, *ka, vt, qkv_mine)
    heads, xt = tie(heads, xt)
    block_rows, base, grad_heads, grad_down, kept, given = dense(
        place,
        heads,
        rows,
        cotangent[:, 0],
        keep_rows,
        vec,
        proj_weight,
        up_weight,
        down_weight,
        gathered,
    )
    grad_o = lax.all_to_all(grad_heads, "ctx", 0, 0, tiled=True)
    down_part = lax.psum_scatter(grad_down, "ctx", scatter_dimension=0, tiled=True)
    each = features // 32
    both = join(kept, given, over(1))
    grad_o, both = tie(grad_o, both)
    left, right = scatter_plane(both)
    shared = (place, grad_o, kt, qn, xt)
    sent, grads = attend_back((0, 1), *shared, *ot[:2], *qt[:2], *ka[:2], *va[:2])
    last, left, right, grads = tie(qt[2], left, right, grads)
    both = scatter_plane_end(left, right)
    came_first = lax.all_to_all(sent, ("ctx", "fsdp"), 0, 0, tiled=True)
    sent, kept, given, _ = attend_back(
        (2,), *shared, ot[2], last, ka[2], va[2], grads, by_head
    )
    given, came_first, down_part, both = tie(given, came_first, down_part, both)
    out_down = lax.psum_scatter(down_part, "fsdp", scatter_dimension=0, tiled=True)

    half = join(kept, given, over(1))
    sent, half = tie(sent, half)
    near = from_fsdp(both[:, 1], 1)
    quarter = half[:2].astype(jnp.float32) + from_ctx(half[2:], 2).astype(jnp.float32)
    quarter, near = tie(quarter, near)
    both = join(both[:, 0], near, lambda value: value)
    mid = from_fsdp(both[1], 2)

    def columns_of(start, stop):
        return both[0, :, start:stop].astype(jnp.float32) + mid[:, start:stop].astype(jnp.float32)

    out_up, out_proj = columns_of(0, 4 * features), columns_of(4 * features, 5 * features)
    vectors = columns_of(5 * features, 5 * features + 10).T
    mine = quarter[0]
    swapped = from_ctx(quarter[1].astype(low), 4).astype(jnp.float32)
    swapped, out_down = tie(swapped, out_down)
    out_down = out_down.astype(jnp.float32)
    first = height == 0
    back = jnp.concatenate(
        [jnp.where(first, mine, swapped), jnp.where(first, swapped, mine)], axis=0
    )
    grad_tokens = base + keep_rows * back

    came_last = lax.all_to_all(sent, ("ctx", "fsdp"), 0, 0, tiled=True)
    out_qkv, out_bias = collect(came_first, came_last)
    at = (4 * me + depth) * each
    out_query_bias, out_value_bias = lax.dynamic_slice_in_dim(out_bias, at, each, 1)

    return (
        block_rows.reshape(2, 1, GROUP, features),
        grad_tokens.reshape(2, 1, GROUP, features),
        out_qkv,
        out_query_bias,
        out_value_bias,
        out_proj,
        vectors[0],
        vectors[1],
        vectors[2],
        out_up,
        vectors[6:10].reshape(4 * each),
        out_down,
        vectors[3],
        vectors[4],
        vectors[5],
    )


def solution(mesh):
    in_specs = (
        P(None, "fsdp", "ctx", None),
        P(None, "fsdp", "ctx"),
        P(None, "fsdp", None),
        P("fsdp", None),
        P("fsdp"),
        P("fsdp"),
        P("fsdp", None),
        P("fsdp"),
        P("fsdp"),
        P("fsdp"),
        P("fsdp", None),
        P("fsdp"),
        P("fsdp", None),
        P("fsdp"),
        P("fsdp"),
        P("fsdp"),
        P(None, "fsdp", "ctx", None),
    )
    out_specs = (
        P(None, "fsdp", "ctx", None),
        P(None, "fsdp", "ctx", None),
        P(("ctx", "fsdp"), None),
        P(("ctx", "fsdp")),
        P(("ctx", "fsdp")),
        P(("ctx", "fsdp"), None),
        P(("ctx", "fsdp")),
        P(("ctx", "fsdp")),
        P(("ctx", "fsdp")),
        P(("ctx", "fsdp"), None),
        P(("ctx", "fsdp")),
        P(("ctx", "fsdp"), None),
        P(("ctx", "fsdp")),
        P(("ctx", "fsdp")),
        P(("ctx", "fsdp")),
    )
    work = fast_on_device if fits(mesh) else on_device
    return jax.shard_map(
        work, mesh=mesh, in_specs=in_specs, out_specs=out_specs, check_vma=False
    )
```

```python
import functools
import math

import jax
import jax.numpy as jnp
from jax import lax
from jax.experimental import pallas as pl
from jax.experimental.pallas import tpu as pltpu
from jax.sharding import PartitionSpec as P

H = 12
NDOC = 4


epsilon = 1e-05
score_scale = 0.125
masked_score = -1e30


def layer_norm(values, gain_vec, offset_vec):
    centre = jnp.mean(values, axis=-1, keepdims=True)
    centred = values - centre
    spread = jnp.mean(centred * centred, axis=-1, keepdims=True)
    return centred * lax.rsqrt(spread + epsilon) * gain_vec + offset_vec


def exact_gelu(values):
    return jax.nn.gelu(values, approximate=False)


def in_blocks(stepper, carried, portion, shard_rows):
    total_rows = portion[0].shape[0]
    shard_count = total_rows // shard_rows
    limit_rows = max(1, 1024 // shard_rows)
    grouped = math.gcd(shard_count, 1 << limit_rows.bit_length() - 1)
    block_rows = grouped * shard_rows
    turn_count = total_rows // block_rows
    stacked = tuple(
        (member.reshape((turn_count, block_rows) + member.shape[1:]) for member in portion)
    )
    offsets = block_rows * jnp.arange(turn_count, dtype=jnp.int32)

    def one_turn(inner_state, element):
        return (stepper(inner_state, element[0], element[1]), None)

    carried, ignored = lax.scan(one_turn, carried, (stacked, offsets))
    return carried


def micro_step(token_rows, slot_ids, keep_flags, weights_full, grad_rows):
    (
        qkv_weight,
        query_bias,
        value_bias,
        proj_weight,
        proj_bias,
        norm1_gain,
        norm1_bias,
        up_weight,
        up_bias,
        down_weight,
        down_bias,
        norm2_gain,
        norm2_bias,
    ) = weights_full
    local_rows, features = token_rows.shape
    num_heads = H
    head_size = features // num_heads
    documents = jnp.arange(NDOC, dtype=jnp.int32)
    keep_rows = jnp.sum(
        jnp.where(slot_ids[:, None] == documents[None, :], keep_flags[None, :], 0), axis=1
    ).astype(jnp.float32)[:, None]
    token_float = token_rows.astype(jnp.float32)
    slot_labels = slot_ids.astype(jnp.float32).astype(jnp.bfloat16)
    projected = jnp.dot(token_rows, qkv_weight, preferred_element_type=jnp.float32)
    query_rows = (projected[:, :features] + query_bias.astype(jnp.float32)).astype(jnp.bfloat16)
    key_rows = projected[:, features : 2 * features].astype(jnp.bfloat16)
    value_rows = (projected[:, 2 * features :] + value_bias.astype(jnp.float32)).astype(
        jnp.bfloat16
    )
    query_heads = query_rows.reshape(local_rows, num_heads, head_size)
    key_heads_local = key_rows.reshape(local_rows, num_heads, head_size)
    value_heads_local = value_rows.reshape(local_rows, num_heads, head_size)

    def forward_step(carried, portion, offset):
        key_part, value_part, id_part = portion
        running_max, running_sum, running_out = carried
        scores = (
            jnp.einsum(
                "qhd,khd->hqk",
                query_heads,
                key_part.reshape(-1, num_heads, head_size),
                preferred_element_type=jnp.float32,
            )
            * score_scale
        )
        same_doc = (slot_labels[:, None] == id_part[None, :])[None]
        scores = jnp.where(same_doc, scores, masked_score)
        new_max = jnp.maximum(running_max, jnp.max(scores, axis=-1))
        factor = jnp.exp(running_max - new_max)
        weights = jnp.where(same_doc, jnp.exp(scores - new_max[..., None]), 0.0)
        running_sum = running_sum * factor + jnp.sum(weights, axis=-1)
        running_out = running_out * factor[..., None] + jnp.einsum(
            "hqk,khd->hqd",
            weights.astype(jnp.bfloat16),
            value_part.reshape(-1, num_heads, head_size),
            preferred_element_type=jnp.float32,
        )
        return (new_max, running_sum, running_out)

    start_state = (
        jnp.full((num_heads, local_rows), masked_score, jnp.float32),
        jnp.zeros((num_heads, local_rows), jnp.float32),
        jnp.zeros((num_heads, local_rows, head_size), jnp.float32),
    )
    running_max, running_sum, running_out = in_blocks(
        forward_step,
        start_state,
        (
            lax.all_gather(key_rows, "ctx", axis=0, tiled=True),
            lax.all_gather(value_rows, "ctx", axis=0, tiled=True),
            lax.all_gather(slot_labels, "ctx", axis=0, tiled=True),
        ),
        local_rows,
    )
    attended = jnp.transpose(running_out / running_sum[..., None], (1, 0, 2))
    log_total = running_max + jnp.log(running_sum)
    attended_low = attended.reshape(local_rows, features).astype(jnp.bfloat16)
    projection = jnp.dot(
        attended_low, proj_weight, preferred_element_type=jnp.float32
    ) + proj_bias.astype(jnp.float32)
    hidden, norm1_back = jax.vjp(
        layer_norm,
        token_float + projection,
        norm1_gain.astype(jnp.float32),
        norm1_bias.astype(jnp.float32),
    )
    hidden_low = hidden.astype(jnp.bfloat16)
    inner_rows = jnp.dot(
        hidden_low, up_weight, preferred_element_type=jnp.float32
    ) + up_bias.astype(jnp.float32)
    active, gelu_back = jax.vjp(exact_gelu, inner_rows)
    active_low = active.astype(jnp.bfloat16)
    branch = jnp.dot(
        active_low, down_weight, preferred_element_type=jnp.float32
    ) + down_bias.astype(jnp.float32)
    result, norm2_back = jax.vjp(
        layer_norm, hidden + branch, norm2_gain.astype(jnp.float32), norm2_bias.astype(jnp.float32)
    )
    block_rows = (keep_rows * result + (1.0 - keep_rows) * token_float).astype(jnp.bfloat16)
    grad_float = grad_rows.astype(jnp.float32)
    grad_sum, grad_gain2, grad_bias2 = norm2_back(keep_rows * grad_float)
    grad_branch = grad_sum.astype(jnp.bfloat16)
    grad_down = jnp.einsum("rf,rd->fd", active_low, grad_branch, preferred_element_type=jnp.float32)
    grad_down_bias = jnp.sum(grad_branch.astype(jnp.float32), axis=0)
    (grad_inner,) = gelu_back(
        jnp.einsum("rd,fd->rf", grad_branch, down_weight, preferred_element_type=jnp.float32)
    )
    grad_inner_low = grad_inner.astype(jnp.bfloat16)
    grad_up = jnp.einsum(
        "rd,rf->df", hidden_low, grad_inner_low, preferred_element_type=jnp.float32
    )
    grad_up_bias = jnp.sum(grad_inner_low.astype(jnp.float32), axis=0)
    grad_hidden = grad_sum + jnp.einsum(
        "rf,df->rd", grad_inner_low, up_weight, preferred_element_type=jnp.float32
    )
    grad_mixed, grad_gain1, grad_bias1 = norm1_back(grad_hidden)
    grad_proj_low = grad_mixed.astype(jnp.bfloat16)
    grad_proj = jnp.einsum(
        "re,rd->ed", attended_low, grad_proj_low, preferred_element_type=jnp.float32
    )
    grad_proj_bias = jnp.sum(grad_proj_low.astype(jnp.float32), axis=0)
    grad_attended = jnp.einsum(
        "rd,ed->re", grad_proj_low, proj_weight, preferred_element_type=jnp.float32
    ).astype(jnp.bfloat16)
    grad_heads = grad_attended.reshape(local_rows, num_heads, head_size)
    row_delta = jnp.transpose(jnp.sum(grad_heads.astype(jnp.float32) * attended, axis=-1))

    def query_step(carried, portion, offset):
        key_part, value_part, id_part = portion
        key_heads = key_part.reshape(-1, num_heads, head_size)
        scores = (
            jnp.einsum("qhd,khd->hqk", query_heads, key_heads, preferred_element_type=jnp.float32)
            * score_scale
        )
        same_doc = (slot_labels[:, None] == id_part[None, :])[None]
        scores = jnp.where(same_doc, scores, masked_score)
        probs = jnp.where(same_doc, jnp.exp(scores - log_total[..., None]), 0.0)
        grad_probs = jnp.einsum(
            "qhd,khd->hqk",
            grad_heads,
            value_part.reshape(-1, num_heads, head_size),
            preferred_element_type=jnp.float32,
        )
        grad_scores = (probs * (grad_probs - row_delta[..., None])).astype(jnp.bfloat16)
        return carried + jnp.einsum(
            "hqk,khd->qhd", grad_scores, key_heads, preferred_element_type=jnp.float32
        )

    grad_query_sum = in_blocks(
        query_step,
        jnp.zeros((local_rows, num_heads, head_size), jnp.float32),
        (
            lax.all_gather(key_rows, "ctx", axis=0, tiled=True),
            lax.all_gather(value_rows, "ctx", axis=0, tiled=True),
            lax.all_gather(slot_labels, "ctx", axis=0, tiled=True),
        ),
        local_rows,
    )
    log_rows, delta_rows = (
        lax.all_gather(jnp.transpose(log_total), "ctx", axis=0, tiled=True),
        lax.all_gather(jnp.transpose(row_delta), "ctx", axis=0, tiled=True),
    )

    def key_step(carried, portion, offset):
        query_part, grad_part, id_part = portion
        grad_key_sum, grad_value_sum = carried
        span_rows = query_part.shape[0]
        log_part = lax.dynamic_slice_in_dim(log_rows, offset, span_rows, 0)
        delta_part = lax.dynamic_slice_in_dim(delta_rows, offset, span_rows, 0)
        query_part_heads = query_part.reshape(-1, num_heads, head_size)
        grad_part_heads = grad_part.reshape(-1, num_heads, head_size)
        scores = (
            jnp.einsum(
                "qhd,khd->hqk",
                query_part_heads,
                key_heads_local,
                preferred_element_type=jnp.float32,
            )
            * score_scale
        )
        same_doc = (id_part[:, None] == slot_labels[None, :])[None]
        scores = jnp.where(same_doc, scores, masked_score)
        probs = jnp.where(same_doc, jnp.exp(scores - jnp.transpose(log_part)[..., None]), 0.0)
        grad_value_sum = grad_value_sum + jnp.einsum(
            "hqk,qhd->khd",
            probs.astype(jnp.bfloat16),
            grad_part_heads,
            preferred_element_type=jnp.float32,
        )
        grad_probs = jnp.einsum(
            "qhd,khd->hqk", grad_part_heads, value_heads_local, preferred_element_type=jnp.float32
        )
        grad_scores = (probs * (grad_probs - jnp.transpose(delta_part)[..., None])).astype(
            jnp.bfloat16
        )
        grad_key_sum = grad_key_sum + jnp.einsum(
            "hqk,qhd->khd", grad_scores, query_part_heads, preferred_element_type=jnp.float32
        )
        return (grad_key_sum, grad_value_sum)

    zero_heads = jnp.zeros((local_rows, num_heads, head_size), jnp.float32)
    grad_key_sum, grad_value_sum = in_blocks(
        key_step,
        (zero_heads, zero_heads),
        (
            lax.all_gather(query_rows, "ctx", axis=0, tiled=True),
            lax.all_gather(grad_attended, "ctx", axis=0, tiled=True),
            lax.all_gather(slot_labels, "ctx", axis=0, tiled=True),
        ),
        local_rows,
    )
    grad_query = (grad_query_sum * score_scale).reshape(local_rows, features).astype(jnp.bfloat16)
    grad_key = (grad_key_sum * score_scale).reshape(local_rows, features).astype(jnp.bfloat16)
    grad_value = grad_value_sum.reshape(local_rows, features).astype(jnp.bfloat16)
    grad_projected = jnp.concatenate([grad_query, grad_key, grad_value], axis=1)
    grad_qkv = jnp.einsum(
        "rd,re->de", token_rows, grad_projected, preferred_element_type=jnp.float32
    )
    grad_query_bias = jnp.sum(grad_query.astype(jnp.float32), axis=0)
    grad_value_bias = jnp.sum(grad_value.astype(jnp.float32), axis=0)
    grad_input = grad_mixed + jnp.einsum(
        "re,de->rd", grad_projected, qkv_weight, preferred_element_type=jnp.float32
    )
    grad_tokens = keep_rows * grad_input + (1.0 - keep_rows) * grad_float
    terms = (
        grad_qkv,
        grad_query_bias,
        grad_value_bias,
        grad_proj,
        grad_proj_bias,
        grad_gain1,
        grad_bias1,
        grad_up,
        grad_up_bias,
        grad_down,
        grad_down_bias,
        grad_gain2,
        grad_bias2,
    )
    return (block_rows, grad_tokens, terms)


def on_device(
    tokens,
    doc_ids,
    keep_mask,
    qkv_weight,
    query_bias,
    value_bias,
    proj_weight,
    proj_bias,
    norm1_gain,
    norm1_bias,
    up_weight,
    up_bias,
    down_weight,
    down_bias,
    norm2_gain,
    norm2_bias,
    cotangent,
):
    block_list = []
    grad_list = []
    summed = None
    for micro_index in range(tokens.shape[0]):
        weights_full = (
            lax.all_gather(qkv_weight, "fsdp", axis=0, tiled=True),
            lax.all_gather(query_bias, "fsdp", axis=0, tiled=True),
            lax.all_gather(value_bias, "fsdp", axis=0, tiled=True),
            lax.all_gather(proj_weight, "fsdp", axis=0, tiled=True),
            lax.all_gather(proj_bias, "fsdp", axis=0, tiled=True),
            lax.all_gather(norm1_gain, "fsdp", axis=0, tiled=True),
            lax.all_gather(norm1_bias, "fsdp", axis=0, tiled=True),
            lax.all_gather(up_weight, "fsdp", axis=0, tiled=True),
            lax.all_gather(up_bias, "fsdp", axis=0, tiled=True),
            lax.all_gather(down_weight, "fsdp", axis=0, tiled=True),
            lax.all_gather(down_bias, "fsdp", axis=0, tiled=True),
            lax.all_gather(norm2_gain, "fsdp", axis=0, tiled=True),
            lax.all_gather(norm2_bias, "fsdp", axis=0, tiled=True),
        )
        block_rows, grad_tokens, terms = micro_step(
            tokens[micro_index, 0],
            doc_ids[micro_index, 0],
            keep_mask[micro_index, 0],
            weights_full,
            cotangent[micro_index, 0],
        )
        block_list.append(block_rows)
        grad_list.append(grad_tokens)
        if summed is None:
            summed = terms
        else:
            summed = tuple((earlier + later for earlier, later in zip(summed, terms)))
    reduced = (
        lax.psum_scatter(summed[0], ("ctx", "fsdp"), scatter_dimension=0, tiled=True),
        lax.psum_scatter(summed[1], ("ctx", "fsdp"), scatter_dimension=0, tiled=True),
        lax.psum_scatter(summed[2], ("ctx", "fsdp"), scatter_dimension=0, tiled=True),
        lax.psum_scatter(summed[3], ("ctx", "fsdp"), scatter_dimension=0, tiled=True),
        lax.psum_scatter(summed[4], ("ctx", "fsdp"), scatter_dimension=0, tiled=True),
        lax.psum_scatter(summed[5], ("ctx", "fsdp"), scatter_dimension=0, tiled=True),
        lax.psum_scatter(summed[6], ("ctx", "fsdp"), scatter_dimension=0, tiled=True),
        lax.psum_scatter(summed[7], ("ctx", "fsdp"), scatter_dimension=0, tiled=True),
        lax.psum_scatter(summed[8], ("ctx", "fsdp"), scatter_dimension=0, tiled=True),
        lax.psum_scatter(summed[9], ("ctx", "fsdp"), scatter_dimension=0, tiled=True),
        lax.psum_scatter(summed[10], ("ctx", "fsdp"), scatter_dimension=0, tiled=True),
        lax.psum_scatter(summed[11], ("ctx", "fsdp"), scatter_dimension=0, tiled=True),
        lax.psum_scatter(summed[12], ("ctx", "fsdp"), scatter_dimension=0, tiled=True),
    )
    block_out = jnp.stack(block_list)[:, None]
    grad_tokens_all = jnp.stack(grad_list)[:, None]
    return (
        block_out,
        grad_tokens_all,
        reduced[0],
        reduced[1],
        reduced[2],
        reduced[3],
        reduced[4],
        reduced[5],
        reduced[6],
        reduced[7],
        reduced[8],
        reduced[9],
        reduced[10],
        reduced[11],
        reduced[12],
    )


MASKED = -1e30
LOWEST = -3e38
ARRIVAL = (0, 4, 2, 6, 1, 5, 3, 7)
GROUP = 192
HEAD = 64
HEADS_EACH = 3
PAIR = 384
SLOTS = 1536
ID_ROWS = 8


def fits(mesh):
    return mesh.shape["ctx"] == 8 and mesh.shape["fsdp"] == 4


def dot(a, b):
    return lax.dot_general(a, b, (((1,), (0,)), ((), ())), preferred_element_type=jnp.float32)


def dot_nt(a, b):
    return lax.dot_general(a, b, (((1,), (1,)), ((), ())), preferred_element_type=jnp.float32)


def flip(value):
    return jnp.transpose(value.astype(jnp.float32)).astype(jnp.bfloat16)


def split3(value):
    high = value.astype(jnp.bfloat16).astype(jnp.float32)
    mid = (value - high).astype(jnp.bfloat16).astype(jnp.float32)
    return high, mid, value - high - mid


def call(kernel, name, ins, outs, scratch=(), scalars=1, any_ins=0, flops=5 * 10**9, aliases=None):
    vmem = pl.BlockSpec(memory_space=pltpu.VMEM)
    return pl.pallas_call(
        kernel,
        name=name,
        out_shape=[jax.ShapeDtypeStruct(shape, kind) for shape, kind in outs],
        grid_spec=pltpu.PrefetchScalarGridSpec(
            num_scalar_prefetch=scalars,
            in_specs=[vmem] * (len(ins) - scalars - any_ins)
            + [pl.BlockSpec(memory_space=pl.ANY)] * any_ins,
            out_specs=[vmem] * len(outs),
            scratch_shapes=list(scratch),
        ),
        cost_estimate=pl.CostEstimate(flops=flops, bytes_accessed=10**7, transcendentals=10**6),
        compiler_params=pltpu.CompilerParams(vmem_limit_bytes=56 * 2**20),
    )(*ins)


QUAD = 768
TILE = 256
TILES = SLOTS // TILE


def project_kernel(place, *refs):
    x_refs = refs[:2]
    own_ref, near_ref, mid_ref, far_ref = refs[2:6]
    qt_refs, ka_refs = refs[6:9], refs[9:12]
    vt_ref, w_ref, vec_ref, turned = refs[12:]
    me, depth = place[0], place[1]
    for m, ref in enumerate((own_ref, near_ref, mid_ref, far_ref)):
        owner = depth ^ m
        rows = pl.ds(pl.multiple_of(owner * GROUP, GROUP), GROUP)
        w_ref[rows, :] = ref[0:GROUP, :]
        vec_ref[owner] = ref[GROUP : GROUP + 8, :].astype(jnp.float32)
    mine = vec_ref[me & 3]
    turned[0:GROUP] = flip(w_ref[:, 0:GROUP])
    turned[GROUP:] = flip(w_ref[:, 2 * GROUP :])
    bias = jnp.concatenate([mine[:, 0:GROUP], mine[:, GROUP : 2 * GROUP]], axis=1)
    bias = jnp.transpose(bias)[:, 0:1]
    lane = lax.broadcasted_iota(jnp.int32, (QUAD, HEAD), 1)
    row = lax.broadcasted_iota(jnp.int32, (HEAD, QUAD), 0)
    for t in range(2):
        span = slice(t * QUAD, (t + 1) * QUAD)
        x = jnp.concatenate([x_refs[t][i, 0:GROUP] for i in range(4)], axis=0)
        ids = jnp.concatenate(
            [x_refs[t][i, GROUP : GROUP + 8, 0:GROUP] for i in range(4)], axis=1
        ).astype(jnp.float32)
        id_row = ids[0:1, :]
        id_col = jnp.transpose(ids)[:, 0:1]
        k_side = jnp.where(
            lane < 5,
            jnp.where(id_col == lane.astype(jnp.float32), 0.0, MASKED),
            jnp.where(lane < 8, -1.0, 0.0),
        ).astype(jnp.bfloat16)
        q_side = jnp.where((row < 5) & (id_row == row.astype(jnp.float32)), 1.0, 0.0).astype(
            jnp.bfloat16
        )
        k = dot(x, w_ref[:, GROUP : 2 * GROUP]).astype(jnp.bfloat16)
        qv = (dot_nt(turned[...], x) + bias).astype(jnp.bfloat16)
        vt_ref[:, span] = qv[GROUP:]
        q = (qv[:GROUP] * 0.125).astype(jnp.bfloat16)
        for h in range(HEADS_EACH):
            heads = slice(h * HEAD, (h + 1) * HEAD)
            ka_refs[h][span, :] = jnp.concatenate([k[:, heads], k_side], axis=1)
            qt_refs[h][0:HEAD, span] = q[heads]
            qt_refs[h][HEAD : 2 * HEAD, span] = q_side


def turn_kernel(*refs):
    x_refs, qt_refs, ka_refs = refs[:2], refs[2:5], refs[5:8]
    vt_ref, w_ref = refs[8:10]
    xt_ref, qn_ref, kt_ref, va_refs, by_head = refs[10], refs[11], refs[12], refs[13:16], refs[16]
    lane = lax.broadcasted_iota(jnp.int32, (PAIR, HEAD), 1)
    v_side = jnp.where(lane < 3, -1.0, 0.0).astype(jnp.bfloat16)
    for t in range(4):
        span = slice(t * PAIR, (t + 1) * PAIR)
        x = jnp.concatenate([x_refs[t // 2][2 * (t % 2) + i, 0:GROUP] for i in (0, 1)], axis=0)
        xt_ref[:, span] = flip(x)
        for h in range(HEADS_EACH):
            heads = slice(h * HEAD, (h + 1) * HEAD)
            qn_ref[span, heads] = flip(qt_refs[h][0:HEAD, span])
            kt_ref[heads, span] = flip(ka_refs[h][span, 0:HEAD])
            va_refs[h][span, :] = jnp.concatenate([flip(vt_ref[heads, span]), v_side], axis=1)
    for h in range(HEADS_EACH):
        for i in range(3):
            by_head[:, (3 * h + i) * HEAD : (3 * h + i + 1) * HEAD] = w_ref[
                :, i * GROUP + h * HEAD : i * GROUP + (h + 1) * HEAD
            ]


def attend_kernel(heads, place, *refs):
    n = len(heads)
    qt_refs, ka_refs, vt_ref = refs[:n], refs[n : 2 * n], refs[2 * n]
    refs = refs[2 * n + 1 :]
    out_qt, out_ot, o_ref = refs[:n], refs[n : 2 * n], refs[2 * n]
    held = refs[-n:]
    me = place[0]
    at_row = lax.broadcasted_iota(jnp.int32, (16, TILE), 0)

    def one_tile(t, unused):
        here = pl.ds(pl.multiple_of(t * TILE, TILE), TILE)
        top = [jnp.full((8, TILE), LOWEST, jnp.float32)] * n
        total = [jnp.zeros((8, TILE), jnp.float32)] * n
        out = [jnp.zeros((HEAD, TILE), jnp.float32)] * n

        def score(i, j):
            span = slice(j * TILE, (j + 1) * TILE)
            scores = dot(ka_refs[i][span, :], qt_refs[i][:, here])
            held[i][span, :] = scores
            top[i] = jnp.maximum(top[i], jnp.max(scores.reshape(TILE // 8, 8, TILE), axis=0))

        def mix(i, j):
            span = slice(j * TILE, (j + 1) * TILE)
            h = heads[i]
            probs = jnp.exp(held[i][span, :] - top[i])
            total[i] = total[i] + jnp.sum(probs.reshape(TILE // 8, 8, TILE), axis=0)
            low = probs.astype(jnp.bfloat16)
            out[i] = out[i] + dot(vt_ref[h * HEAD : (h + 1) * HEAD, span], low)

        for i in range(n):
            for j in range(TILES):
                score(i, j)
            top[i] = jnp.max(top[i], axis=0, keepdims=True)
        for i in range(n):
            for j in range(TILES):
                mix(i, j)
        for i in range(n):
            sums = jnp.sum(total[i], axis=0, keepdims=True)
            out_ot[i][:, here] = (out[i] / sums).astype(jnp.bfloat16)
            high, mid, low = split3(top[i] + jnp.log(sums))
            side = qt_refs[i][HEAD : HEAD + 16, here].astype(jnp.float32)
            side = jnp.where(at_row == 5, high, side)
            side = jnp.where(at_row == 6, mid, side)
            side = jnp.where(at_row == 7, low, side)
            out_qt[i][0:HEAD, here] = qt_refs[i][0:HEAD, here]
            out_qt[i][HEAD : HEAD + 16, here] = side.astype(jnp.bfloat16)
            out_qt[i][HEAD + 16 :, here] = qt_refs[i][HEAD + 16 :, here]
        return unused

    lax.fori_loop(0, TILES, one_tile, 0)
    for t in range(4):
        span = slice(t * PAIR, (t + 1) * PAIR)
        rows = flip(jnp.concatenate([ref[:, span] for ref in out_ot], axis=0))
        for half in range(2):
            o_ref[me ^ ARRIVAL[2 * t + half]] = rows[half * GROUP : (half + 1) * GROUP, :]


def attend_back_kernel(heads, place, *refs):
    n = len(heads)
    do_ref, kt_ref, qn_ref, xt_ref = refs[:4]
    refs = refs[4:]
    ot_refs, qt_refs, ka_refs, va_refs = [refs[i * n : (i + 1) * n] for i in range(4)]
    refs = refs[4 * n :]
    last = heads[-1] == HEADS_EACH - 1
    if last:
        earlier_ref, w_ref = refs[:2]
        refs = refs[2:]
        sent_ref, keep_ref, give_ref, g_ref = refs[:4]
        refs = refs[4:]
    else:
        sent_ref, g_ref = refs[0], refs[1]
        refs = refs[2:]
    dot_t, don, dqt = refs
    me = place[0]
    row = lax.broadcasted_iota(jnp.int32, (HEAD, PAIR), 0)
    for t in range(4):
        here = slice(t * PAIR, (t + 1) * PAIR)
        a, b = me ^ ARRIVAL[2 * t], me ^ ARRIVAL[2 * t + 1]
        for i, h in enumerate(heads):
            cols = slice(h * HEAD, (h + 1) * HEAD)
            grad = jnp.concatenate([do_ref[a][:, cols], do_ref[b][:, cols]], axis=0)
            don[i, here, :] = grad
            grad_t = jnp.transpose(grad.astype(jnp.float32))
            delta = jnp.sum(grad_t * ot_refs[i][:, here].astype(jnp.float32), axis=0, keepdims=True)
            high, mid, low = split3(delta)
            side = jnp.where(
                row == 0, high, jnp.where(row == 1, mid, jnp.where(row == 2, low, 0.0))
            )
            dot_t[i, 0:HEAD, here] = grad_t.astype(jnp.bfloat16)
            dot_t[i, HEAD : 2 * HEAD, here] = side.astype(jnp.bfloat16)
    dqt[...] = jnp.zeros_like(dqt)

    def keys(j, unused):
        here = pl.ds(pl.multiple_of(j * TILE, TILE), TILE)
        steps = [(i, t) for i in range(n) for t in range(TILES)]
        keys_of = [ka_refs[i][here, :] for i in range(n)]
        vals_of = [va_refs[i][here, :] for i in range(n)]
        turned = [kt_ref[h * HEAD : (h + 1) * HEAD, here] for h in heads]
        dk = [jnp.zeros((HEAD, TILE), jnp.float32) for i in range(n)]
        dv = [jnp.zeros((HEAD, TILE), jnp.float32) for i in range(n)]

        def ahead(step):
            i, t = step
            span = slice(t * TILE, (t + 1) * TILE)
            return dot(keys_of[i], qt_refs[i][:, span]), dot(vals_of[i], dot_t[i, :, span])

        def behind(step, probs, grad_scores):
            i, t = step
            span = slice(t * TILE, (t + 1) * TILE)
            dv[i] = dv[i] + dot_nt(dot_t[i, 0:HEAD, span], probs)
            dk[i] = dk[i] + dot_nt(qt_refs[i][0:HEAD, span], grad_scores)
            dqt[i, :, span] = dqt[i, :, span] + dot(turned[i], grad_scores)

        ready, done = ahead(steps[0]), None
        for at, step in enumerate(steps):
            scores, grad_probs = ready
            if at + 1 < len(steps):
                ready = ahead(steps[at + 1])
            probs = jnp.exp(scores)
            grad_scores = (probs * grad_probs).astype(jnp.bfloat16)
            if done is not None:
                behind(*done)
            done = step, probs.astype(jnp.bfloat16), grad_scores
        behind(*done)
        for i in range(n):
            at = i * GROUP
            both = jnp.transpose(jnp.concatenate([dk[i], dv[i]], axis=0)).astype(jnp.bfloat16)
            g_ref[here, at + HEAD : at + GROUP] = both
        return unused

    lax.fori_loop(0, TILES, keys, 0)
    bias = jnp.zeros((1, n * GROUP), jnp.float32)
    for t in range(4):
        span = slice(t * PAIR, (t + 1) * PAIR)
        for i in range(n):
            g_ref[span, i * GROUP : i * GROUP + HEAD] = (
                jnp.transpose(dqt[i, :, span]) * 0.125
            ).astype(jnp.bfloat16)
        bias = bias + jnp.sum(g_ref[span, :].astype(jnp.float32), axis=0, keepdims=True)
    high = bias.astype(jnp.bfloat16).astype(jnp.float32)
    at_row = lax.broadcasted_iota(jnp.int32, (8, n * GROUP), 0)
    fixed = jnp.where(at_row == 0, high, jnp.where(at_row == 1, bias - high, 0.0))

    def weights_back(t, unused):
        x_rows = xt_ref[pl.ds(pl.multiple_of(t * GROUP, GROUP), GROUP), :]
        part = dot(x_rows, g_ref[...]).astype(jnp.bfloat16)
        for i in range(8):
            sent_ref[8 * t + i, 0:24, :] = part[24 * i : 24 * (i + 1)]
            sent_ref[8 * t + i, 24:32, :] = fixed.astype(jnp.bfloat16)
        return unused

    lax.fori_loop(0, 4, weights_back, 0)
    if last:
        split = earlier_ref.shape[1]

        for t in range(4):
            here = slice(t * PAIR, (t + 1) * PAIR)
            back_ref, at = (keep_ref, 2 * t) if t < 2 else (give_ref, 2 * t - 4)
            part = dot_nt(earlier_ref[here, :], w_ref[:, :split])
            part = (part + dot_nt(g_ref[here, :], w_ref[:, split:])).astype(jnp.bfloat16)
            back_ref[at] = part[:GROUP]
            back_ref[at + 1] = part[GROUP:]


def assemble_kernel(*refs):
    stay, near, mid, deep, deep_far, deep_next, deep_last = refs[:7]
    up_ref, proj_ref, down_ref, vec_ref = refs[7:]
    terms = (deep[0], deep_far[0], deep_next[0], deep_last[...])
    deep_sum = sum(value.astype(jnp.float32) for value in terms)

    def columns(start, stop):
        parts = (stay[0, :, start:stop], near[0, :, start:stop], mid[:, start:stop])
        return sum(value.astype(jnp.float32) for value in parts)

    width = 4 * GROUP
    up_ref[...] = columns(0, 4 * width)
    proj_ref[...] = columns(4 * width, 5 * width)
    vec_ref[...] = jnp.transpose(columns(5 * width, DOWN_AT))[0:16]
    for k in range(4):
        at, end = DOWN_AT + k * width, DOWN_AT + (k + 1) * width
        parts = []
        if at < RIGHT:
            parts.append(columns(at, min(end, RIGHT)))
        if end > RIGHT:
            parts.append(deep_sum[:, max(at, RIGHT) - RIGHT : end - RIGHT])
        down_ref[24 * k : 24 * (k + 1), :] = jnp.concatenate(parts, axis=1)


def pack_kernel(*refs):
    for m in range(3):
        refs[3][m * PART[0] : (m + 1) * PART[0], :] = refs[m][: PART[0], :]
        refs[4][m * PART[1] : (m + 1) * PART[1], :] = refs[m][PART[0] :, :]


def collect_kernel(first_ref, last_ref, out_ref, bias_ref):
    for g in range(4):
        for ref, heads in ((first_ref, (0, 1)), (last_ref, (2,))):
            total = sum(
                ref[16 * y + 4 * g + z].astype(jnp.float32) for y in range(2) for z in range(4)
            )
            for i, h in enumerate(heads):
                for part in range(3):
                    at = i * GROUP + part * HEAD
                    to = g * GROUP + h * HEAD
                    piece = total[:, at : at + HEAD]
                    out_ref[:, part * 4 * GROUP + to : part * 4 * GROUP + to + HEAD] = piece[0:24]
                    if part != 1:
                        row = part // 2
                        bias_ref[row : row + 1, to : to + HEAD] = piece[24:25] + piece[25:26]


LOW, WIDE = jnp.bfloat16, jnp.float32


def project(*ins):
    outs = [((2 * HEAD, SLOTS), LOW)] * 3 + [((SLOTS, 2 * HEAD), LOW)] * 3
    outs += [((GROUP, SLOTS), LOW), ((4 * GROUP, 3 * GROUP), LOW), ((4, 8, 3 * GROUP), WIDE)]
    scratch = [pltpu.VMEM((2 * GROUP, 4 * GROUP), LOW)]
    return call(project_kernel, "project", ins, outs, scratch)


def turn(*ins):
    outs = [((4 * GROUP, SLOTS), LOW), ((SLOTS, GROUP), LOW), ((GROUP, SLOTS), LOW)]
    outs += [((SLOTS, 2 * HEAD), LOW)] * 3 + [((4 * GROUP, 3 * GROUP), LOW)]
    return call(turn_kernel, "turn", ins, outs, scalars=0)


def attend(heads, *ins):
    n = len(heads)
    outs = [((2 * HEAD, SLOTS), LOW)] * n + [((HEAD, SLOTS), LOW)] * n
    outs.append(((8, GROUP, GROUP), LOW))
    scratch = [pltpu.VMEM((SLOTS, TILE), WIDE)] * n
    kernel = functools.partial(attend_kernel, heads)
    return call(kernel, f"attend{heads[0]}", ins, outs, scratch)


def attend_back(heads, *ins):
    n = len(heads)
    scratch = [
        pltpu.VMEM((n, 2 * HEAD, SLOTS), LOW),
        pltpu.VMEM((n, SLOTS, HEAD), LOW),
        pltpu.VMEM((n, HEAD, SLOTS), WIDE),
    ]
    outs = [((32, 32, n * GROUP), LOW)]
    if heads[-1] == HEADS_EACH - 1:
        outs += [((4, GROUP, 4 * GROUP), LOW)] * 2
    outs.append(((SLOTS, n * GROUP), LOW))
    kernel = functools.partial(attend_back_kernel, heads)
    return call(kernel, f"attend_back{heads[0]}", ins, outs, scratch, flops=10**10)


def assemble(*ins):
    width = 4 * GROUP
    shapes = ((24, 4 * width), (24, width), (96, width), (16, 24))
    outs = [(shape, WIDE) for shape in shapes]
    return call(assemble_kernel, "assemble", ins, outs, scalars=0, flops=10**6)


def pack(*ins):
    outs = [((3 * rows, 384), LOW) for rows in PART]
    return call(pack_kernel, "pack", ins, outs, scalars=0, flops=10**6)


def collect(*ins):
    outs = [((24, 12 * GROUP), WIDE), ((2, 4 * GROUP), WIDE)]
    return call(collect_kernel, "collect", ins, outs, scalars=0, flops=10**6)


def from_ctx(value, bits):
    return lax.ppermute(value, "ctx", [(i, i ^ bits) for i in range(8)])


def from_fsdp(value, bits):
    return lax.ppermute(value, "fsdp", [(i, i ^ bits) for i in range(4)])


FF_CUT = 384
PROJ_ROWS = 48
DOWN_ROWS = 96
PART = (240, 192)
DOWN_AT = 3968
COLUMNS = 7040
LEFT = 2816
RIGHT = 5632
BACK_STEP = 768


def norm(value):
    centred = value - jnp.mean(value, axis=1, keepdims=True)
    scale = lax.rsqrt(jnp.mean(centred * centred, axis=1, keepdims=True) + epsilon)
    return centred * scale, scale


def norm_back(grad, normal, scale):
    return scale * (
        grad
        - jnp.mean(grad, axis=1, keepdims=True)
        - normal * jnp.mean(grad * normal, axis=1, keepdims=True)
    )


TAIL_AT = 0.35
TAIL = (
    0.19746588,
    0.197487361,
    0.184996341,
    0.164759887,
    0.106787389,
    0.160058898,
    -0.11534264,
    0.24699889,
    -0.186710954,
    0.0434989602,
)


def gelu_parts(value):
    bell = jnp.exp(-0.5 * value * value)
    t = 1.0 / (1.0 + (TAIL_AT * 2.0**-0.5) * jnp.abs(value))
    tail = jnp.full_like(t, 0.5 * TAIL[-1])
    for term in TAIL[-2::-1]:
        tail = tail * t + 0.5 * term
    tail = tail * t * bell
    return jnp.where(value < 0.0, tail, 1.0 - tail), bell


FF_STEP = 512


def dense_kernel(place, *refs):
    a_ref, tok_ref, cot_ref, keep_ref, vec_ref = refs[:5]
    proj_own, up_own, down_own = refs[5:8]
    shared = refs[8:16]
    block_ref, base_ref, ga_ref, keep_cols, give_cols = refs[16:21]
    up, down, proj, slope, act_ref, att_ref, hid_ref, hid_t, gb_ref = refs[21:30]
    sums_ref, upb_ref, turned, ordered, even, odd, branch, proj_sem, up_sem, down_sem = refs[30:]
    me, depth = place[0], place[1]
    width = 4 * GROUP
    proj_copies, up_copies, down_copies = [], [], []

    def copy(into, source, target, sem):
        made = pltpu.make_async_copy(source, target, sem.at[len(into)])
        made.start()
        into.append(made)

    def owner_rows(m, size, at, rows):
        return pl.ds(pl.multiple_of((depth ^ m) * size + at, PROJ_ROWS), rows)

    def pieces(first, ways, rows):
        for source, pair in zip(shared[first : first + 4], ways):
            for i, k in enumerate(pair):
                for m in (1, 2, 3):
                    yield source, me ^ k, m, (3 * i + m - 1) * rows

    ways = ((0, 2), (4, 6), (1, 3), (5, 7))
    copy(proj_copies, proj_own, proj.at[owner_rows(0, GROUP, 0, GROUP)], proj_sem)
    for source, owner, m, at in pieces(0, ways, PART[0]):
        copy(
            proj_copies,
            source.at[pl.ds(at + GROUP, PROJ_ROWS)],
            proj.at[
                owner_rows(m, GROUP, (owner >> 1) * PROJ_ROWS, PROJ_ROWS),
                pl.ds(pl.multiple_of((owner & 1) * FF_CUT, FF_CUT), FF_CUT),
            ],
            proj_sem,
        )
    copy(up_copies, up_own, up.at[owner_rows(0, GROUP, 0, GROUP)], up_sem)
    for source, owner, m, at in pieces(0, ways, PART[0]):
        copy(
            up_copies,
            source.at[pl.ds(at, GROUP)],
            up.at[
                owner_rows(m, GROUP, 0, GROUP),
                pl.ds(pl.multiple_of(owner * FF_CUT, FF_CUT), FF_CUT),
            ],
            up_sem,
        )
    copy(down_copies, down_own, down.at[owner_rows(0, width, 0, width)], down_sem)
    for source, owner, m, at in pieces(4, ((0, 4), (2, 6), (1, 5), (3, 7)), PART[1]):
        for side in range(2):
            copy(
                down_copies,
                source.at[pl.ds(at + side * DOWN_ROWS, DOWN_ROWS)],
                down.at[
                    owner_rows(m, width, owner * DOWN_ROWS, DOWN_ROWS),
                    pl.ds(side * FF_CUT, FF_CUT),
                ],
                down_sem,
            )

    def vector(i):
        row, at = i // 3, (i % 3) * GROUP
        return jnp.concatenate(
            [vec_ref[j, row : row + 1, at : at + GROUP] for j in range(4)], axis=1
        )

    up_bias = jnp.concatenate(
        [
            part
            for j in range(4)
            for part in (vec_ref[j, 2:3, 2 * GROUP : 3 * GROUP], vec_ref[j, 3:4, :])
        ],
        axis=1,
    )
    proj_bias, gain1, bias1, down_bias, gain2, bias2 = [vector(i) for i in range(2, 8)]
    upb_ref[...] = up_bias
    for mb in range(2):
        att_ref[mb * GROUP : (mb + 1) * GROUP, :] = jnp.concatenate(
            [a_ref[4 * mb + j] for j in range(4)], axis=1
        )
    tokens = jnp.concatenate([tok_ref[0], tok_ref[1]], axis=0).astype(jnp.float32)
    cot = jnp.concatenate([cot_ref[0], cot_ref[1]], axis=0).astype(jnp.float32)
    keep = keep_ref[...]

    for made in proj_copies:
        made.wait()
    mixed = tokens + dot(att_ref[...], proj[...]) + proj_bias
    normal1, scale1 = norm(mixed)
    hidden = normal1 * gain1 + bias1
    hid_ref[...] = hidden.astype(jnp.bfloat16)

    def by_owner(value, target):
        for i in range(8):
            away = me ^ i
            at = (away & 1) * FF_CUT + (away >> 1) * 96
            for j in range(4):
                row = pl.multiple_of(at + (depth ^ j) * 24, 8)
                target[pl.ds(row, 24), :] = value[i * 96 + j * 24 : i * 96 + (j + 1) * 24]

    def out_columns(cols, grad):
        keep_cols[:, cols] = dot(hid_t[0:FF_CUT], grad).astype(jnp.bfloat16)
        give_cols[:, cols] = dot(hid_t[FF_CUT:], grad).astype(jnp.bfloat16)

    by_owner(jnp.transpose(hid_ref[...].astype(jnp.float32)), ordered)
    hid_t[...] = ordered[...].astype(jnp.bfloat16)
    for made in up_copies:
        made.wait()
    for made in down_copies:
        made.wait()

    def columns(j):
        return pl.ds(pl.multiple_of(j * FF_STEP, FF_STEP), FF_STEP)

    def rise(j, target):
        cols = columns(j)
        target[...] = dot(hid_ref[...], up[:, cols]) + upb_ref[:, cols]

    def fall(j, source):
        cols = columns(j)
        inner = source[...]
        share, bell = gelu_parts(inner)
        slope[:, cols] = share + inner * bell * (1.0 / math.sqrt(2.0 * math.pi))
        active = (inner * share).astype(jnp.bfloat16)
        act_ref[:, cols] = active
        branch[...] += dot(active, down[cols, :])

    def forward(i, unused):
        rise(2 * i + 1, odd)
        fall(2 * i, even)
        rise(jnp.minimum(2 * i + 2, 5), even)
        fall(2 * i + 1, odd)
        return unused

    branch[...] = jnp.broadcast_to(down_bias, branch.shape)
    rise(0, even)
    lax.fori_loop(0, 3, forward, 0)
    normal2, scale2 = norm(hidden + branch[...])
    result = normal2 * gain2 + bias2
    block = (keep * result + (1.0 - keep) * tokens).astype(jnp.bfloat16)
    block_ref[0] = block[:GROUP]
    block_ref[1] = block[GROUP:]
    grad = keep * cot
    grad_sum = norm_back(grad * gain2, normal2, scale2)
    grad_branch = grad_sum.astype(jnp.bfloat16)
    gb_ref[...] = grad_branch

    def add_up(value):
        return jnp.sum(value, axis=0, keepdims=True)

    sums_ref[3:4, :] = add_up(grad_branch.astype(jnp.float32))
    sums_ref[4:5, :] = add_up(grad * normal2)
    sums_ref[5:6, :] = add_up(grad)

    def backward(j, total):
        cols = pl.ds(pl.multiple_of(j * BACK_STEP, BACK_STEP), BACK_STEP)
        grad_inner = (dot_nt(gb_ref[...], down[cols, :]) * slope[:, cols]).astype(jnp.bfloat16)
        out_columns(cols, grad_inner)
        active = jnp.transpose(act_ref[:, cols].astype(jnp.float32))
        for i in range(8):
            for k in range(4):
                away = ((i >> 2) ^ (me & 1)) * FF_CUT + k * 96 + ((i & 3) ^ depth) * 24
                at = i * 96 + k * 24
                ordered[pl.ds(pl.multiple_of(away, 8), 24), :] = active[at : at + 24]
        part = dot(ordered[...].astype(jnp.bfloat16), gb_ref[...]).astype(jnp.bfloat16)
        rows = pl.ds(pl.multiple_of((j ^ (me >> 1)) * 96, 96), 96)
        for k in range(4):
            lanes = slice(DOWN_AT + k * width, DOWN_AT + (k + 1) * width)
            keep_cols[rows, lanes] = part[k * 96 : (k + 1) * 96]
            give_cols[rows, lanes] = part[FF_CUT + k * 96 : FF_CUT + (k + 1) * 96]
        upb_ref[:, cols] = add_up(grad_inner.astype(jnp.float32))
        return total + dot_nt(grad_inner, up[:, cols])

    grad_hidden = lax.fori_loop(0, 4, backward, grad_sum)
    sums_ref[1:2, :] = add_up(grad_hidden * normal1)
    sums_ref[2:3, :] = add_up(grad_hidden)
    grad_mixed = norm_back(grad_hidden * gain1, normal1, scale1)
    base_ref[...] = keep * grad_mixed + (1.0 - keep) * cot
    grad_proj = grad_mixed.astype(jnp.bfloat16)
    by_owner(jnp.transpose(att_ref[...].astype(jnp.float32)), ordered)
    hid_t[...] = ordered[...].astype(jnp.bfloat16)
    out_columns(slice(4 * width, 5 * width), grad_proj)
    sums_ref[0:1, :] = add_up(grad_proj.astype(jnp.float32))
    sums_ref[6:8, :] = jnp.zeros((2, width), jnp.float32)
    lane = lax.broadcasted_iota(jnp.int32, (width, 128), 1)
    vectors = jnp.concatenate(
        [jnp.transpose(sums_ref[...]), jnp.zeros((width, 120), jnp.float32)], axis=1
    )
    column = jnp.transpose(jnp.broadcast_to(upb_ref[...], (8, 4 * width)))[:, 0:1]
    for j in range(4):
        part = jnp.concatenate(
            [column[i * 96 + j * 24 : i * 96 + (j + 1) * 24] for i in range(32)], axis=0
        )
        vectors = jnp.where(lane == 6 + j, part, vectors)
    by_owner(vectors, turned)
    keep_cols[:, 5 * width : DOWN_AT] = turned[0:FF_CUT].astype(jnp.bfloat16)
    give_cols[:, 5 * width : DOWN_AT] = turned[FF_CUT:].astype(jnp.bfloat16)
    grad_att = dot_nt(grad_proj, proj[...]).astype(jnp.bfloat16)
    for mb in range(2):
        for j in range(4):
            ga_ref[4 * mb + j] = grad_att[
                mb * GROUP : (mb + 1) * GROUP, j * GROUP : (j + 1) * GROUP
            ]


def dense(*ins):
    rows, width, hidden = 2 * GROUP, 4 * GROUP, 16 * GROUP
    outs = [
        ((2, GROUP, width), LOW),
        ((rows, width), WIDE),
        ((8, GROUP, GROUP), LOW),
        ((FF_CUT, COLUMNS), LOW),
        ((FF_CUT, COLUMNS), LOW),
    ]
    scratch = [
        pltpu.VMEM((width, hidden), LOW),
        pltpu.VMEM((hidden, width), LOW),
        pltpu.VMEM((width, width), LOW),
        pltpu.VMEM((rows, hidden), WIDE),
        pltpu.VMEM((rows, hidden), LOW),
        pltpu.VMEM((rows, width), LOW),
        pltpu.VMEM((rows, width), LOW),
        pltpu.VMEM((width, rows), LOW),
        pltpu.VMEM((rows, width), LOW),
        pltpu.VMEM((8, width), WIDE),
        pltpu.VMEM((1, hidden), WIDE),
        pltpu.VMEM((width, 128), WIDE),
        pltpu.VMEM((width, rows), WIDE),
        pltpu.VMEM((rows, FF_STEP), WIDE),
        pltpu.VMEM((rows, FF_STEP), WIDE),
        pltpu.VMEM((rows, width), WIDE),
        pltpu.SemaphoreType.DMA((25,)),
        pltpu.SemaphoreType.DMA((25,)),
        pltpu.SemaphoreType.DMA((49,)),
    ]
    return call(dense_kernel, "dense", ins, outs, scratch, any_ins=11, flops=2 * 10**10)


def tie(*values):
    return lax.optimization_barrier(values)


def take(value, at, axis):
    return lax.dynamic_index_in_dim(value, at, axis, keepdims=False)


def add(kept, came):
    return (kept.astype(jnp.float32) + came.astype(jnp.float32)).astype(jnp.bfloat16)


def split_plane(kept, came):
    kept, came = [value.reshape(2, 2, 96, COLUMNS) for value in (kept, came)]
    left, right = slice(0, LEFT), slice(LEFT, RIGHT)
    deep = [value[..., RIGHT:].reshape(4, 2, 2, 24, -1) for value in (kept, came)]
    return [
        add(kept[:, 0, :, left], came[:, 0, :, left]),
        add(kept[:, 1, :, left], came[:, 1, :, left]),
        add(kept[0, :, :, right], came[0, :, :, right]),
        add(kept[1, :, :, right], came[1, :, :, right]),
        add(deep[0][:, :, 0], deep[1][:, :, 0]),
        add(deep[0][:, :, 1], deep[1][:, :, 1]),
    ]


def end_plane(left, left_in, right, right_in):
    pairs = [
        (add(left[0], left_in[0]), from_ctx(add(left[1], left_in[1]), 4)),
        (add(right[0], right_in[0]), from_ctx(add(right[1], right_in[1]), 2)),
    ]

    def part(at):
        parts = []
        for values in pairs:
            kept, came = [value.reshape(2, 2, 24, -1)[:, at] for value in values]
            parts.append(add(kept, came))
        return jnp.concatenate(parts, axis=2)

    return part


def fast_on_device(
    tokens,
    doc_ids,
    keep_mask,
    qkv_weight,
    query_bias,
    value_bias,
    proj_weight,
    proj_bias,
    norm1_gain,
    norm1_bias,
    up_weight,
    up_bias,
    down_weight,
    down_bias,
    norm2_gain,
    norm2_bias,
    cotangent,
):
    low = jnp.bfloat16
    me = lax.axis_index("ctx")
    height = me >> 2
    group = me & 3
    depth = lax.axis_index("fsdp")
    place = jnp.stack([me, depth] + [jnp.int32(k) for k in ARRIVAL])
    rows = tokens[:, 0]
    ids = doc_ids[:, 0]
    features = rows.shape[2]

    id_rows = jnp.pad(ids.astype(low)[:, None, :], ((0, 0), (0, ID_ROWS - 1), (0, features - GROUP)))
    marked = jnp.concatenate([rows, id_rows], axis=1)
    own = take(marked, height, 0)
    at = group * GROUP
    columns = jnp.concatenate(
        [lax.dynamic_slice_in_dim(qkv_weight, part * features + at, GROUP, 1) for part in range(3)],
        axis=1,
    )
    vectors = jnp.concatenate(
        [
            query_bias,
            value_bias,
            proj_bias,
            norm1_gain,
            norm1_bias,
            down_bias,
            norm2_gain,
            norm2_bias,
            up_bias,
        ]
    ).reshape(4, 3 * GROUP)
    columns = jnp.concatenate([columns, vectors, jnp.zeros((4, 3 * GROUP), low)], axis=0)
    up_cut = lax.dynamic_slice_in_dim(up_weight, me * FF_CUT, FF_CUT, 1)
    down_cut = lax.dynamic_slice_in_dim(down_weight, me * DOWN_ROWS, DOWN_ROWS, 0)
    proj_cut = lax.dynamic_slice(
        proj_weight, ((me >> 1) * PROJ_ROWS, (me & 1) * FF_CUT), (PROJ_ROWS, FF_CUT)
    )
    cut = jnp.concatenate([up_cut, proj_cut, down_cut[:, :FF_CUT], down_cut[:, FF_CUT:]], axis=0)
    came = from_ctx(take(marked, 1 - height, 0), 4)
    across = from_ctx(own, 2)
    cuts = [from_fsdp(cut, m) for m in (1, 2, 3)]
    came, columns = tie(came, columns)
    corner = from_ctx(came, 2)
    near = from_fsdp(columns, 1)
    own, came, across, corner, near, columns, *cuts = tie(
        own, came, across, corner, near, columns, *cuts
    )
    mid, far = [from_fsdp(columns, m) for m in (2, 3)]
    four = jnp.stack([own, came, across, corner])
    eight = from_ctx(four, 1)
    some, rest = pack(*cuts)
    some_too, rest_too = from_ctx(some, 2), from_ctx(rest, 4)
    eight, some_too, rest_too = tie(eight, some_too, rest_too)
    some = jnp.concatenate([some, some_too], axis=0)
    rest = jnp.concatenate([rest, rest_too], axis=0)
    shared = [some, from_ctx(some, 4), from_ctx(some, 1), None]
    shared += [rest, from_ctx(rest, 2), from_ctx(rest, 1), None]

    documents = jnp.arange(NDOC, dtype=jnp.int32)
    keep_rows = jnp.sum(
        jnp.where(ids[:, :, None] == documents, keep_mask[:, 0][:, None, :], 0), axis=2
    ).astype(jnp.float32).reshape(2 * GROUP, 1)

    made = project(place, four, eight, columns, near, mid, far)
    qt, ka = list(made[:3]), made[3:6]
    vt, qkv_mine, vec = made[6:]
    turned = list(qt)
    *made, o = attend((0, 1, 2), place, *turned, *ka, vt)
    qt, ot = made[:3], made[3:]
    o, shared[1], shared[5] = tie(o, shared[1], shared[5])
    shared[3], shared[7] = from_ctx(shared[1], 1), from_ctx(shared[5], 1)
    heads = lax.all_to_all(o, "ctx", 0, 0, tiled=True)
    xt, qn, kt, *va, by_head = turn(four, eight, *turned, *ka, vt, qkv_mine)
    heads, xt = tie(heads, xt)
    block_rows, base, grad_heads, kept, given = dense(
        place,
        heads,
        rows,
        cotangent[:, 0],
        keep_rows,
        vec,
        proj_weight,
        up_weight,
        down_weight,
        *shared,
    )
    grad_o = lax.all_to_all(grad_heads, "ctx", 0, 0, tiled=True)
    each = features // 32
    came = from_ctx(given, 1)
    grad_o, left, left_out, right, right_out, deep, deep_out = tie(
        grad_o, *split_plane(kept, came)
    )
    left_in, right_in = from_ctx(left_out, 2), from_ctx(right_out, 4)
    deep_in = from_fsdp(deep_out, 1)
    shared = (place, grad_o, kt, qn, xt)
    sent, grads = attend_back((0, 1), *shared, *ot[:2], *qt[:2], *ka[:2], *va[:2])
    last, left, left_in, right, right_in, deep, deep_in, grads = tie(
        qt[2], left, left_in, right, right_in, deep, deep_in, grads
    )
    deep_far = from_fsdp(add(deep[:, 1], deep_in[:, 1]), 2)
    deep = add(deep[:, 0], deep_in[:, 0])
    part = end_plane(left, left_in, right, right_in)
    came_first = lax.all_to_all(sent, ("ctx", "fsdp"), 0, 0, tiled=True)
    sent, kept, given, _ = attend_back(
        (2,), *shared, ot[2], last, ka[2], va[2], grads, by_head
    )
    given, came_first = tie(given, came_first)

    came = from_ctx(given, 1)
    half_out = add(kept[2:], came[2:])
    sent, half_out = tie(sent, half_out)
    near = from_fsdp(part(1), 1)
    half_in = from_ctx(half_out, 2)
    deep_far, _ = tie(deep_far, half_out)
    deep, deep_far = [value.reshape(2, 2, 24, -1) for value in (deep, deep_far)]
    deep_next = from_ctx(add(deep[:, 1], deep_far[:, 1]), 2)
    half_in, near = tie(half_in, near)
    quarter = sum(value.astype(jnp.float32) for value in (kept[:2], came[:2], half_in))
    stay = part(0)
    mid = from_fsdp(add(stay[1], near[1]), 2)
    deep_sum = [deep[:, 0], deep_far[:, 0], deep_next]
    deep_out = sum(value[1].astype(jnp.float32) for value in deep_sum).astype(low)
    deep_last = from_ctx(deep_out, 4)

    out_up, out_proj, out_down, vectors = assemble(
        stay,
        near,
        mid,
        deep.reshape(4, 24, -1),
        deep_far.reshape(4, 24, -1),
        deep_next,
        deep_last,
    )
    mine = quarter[0]
    swapped = from_ctx(quarter[1].astype(low), 4).astype(jnp.float32)
    first = height == 0
    back = jnp.concatenate(
        [jnp.where(first, mine, swapped), jnp.where(first, swapped, mine)], axis=0
    )
    grad_tokens = base + keep_rows * back

    came_last = lax.all_to_all(sent, ("ctx", "fsdp"), 0, 0, tiled=True)
    out_qkv, out_bias = collect(came_first, came_last)
    at = (4 * me + depth) * each
    out_query_bias, out_value_bias = lax.dynamic_slice_in_dim(out_bias, at, each, 1)

    return (
        block_rows.reshape(2, 1, GROUP, features),
        grad_tokens.reshape(2, 1, GROUP, features),
        out_qkv,
        out_query_bias,
        out_value_bias,
        out_proj,
        vectors[0],
        vectors[1],
        vectors[2],
        out_up,
        vectors[6:10].reshape(4 * each),
        out_down,
        vectors[3],
        vectors[4],
        vectors[5],
    )


def solution(mesh):
    in_specs = (
        P(None, "fsdp", "ctx", None),
        P(None, "fsdp", "ctx"),
        P(None, "fsdp", None),
        P("fsdp", None),
        P("fsdp"),
        P("fsdp"),
        P("fsdp", None),
        P("fsdp"),
        P("fsdp"),
        P("fsdp"),
        P("fsdp", None),
        P("fsdp"),
        P("fsdp", None),
        P("fsdp"),
        P("fsdp"),
        P("fsdp"),
        P(None, "fsdp", "ctx", None),
    )
    out_specs = (
        P(None, "fsdp", "ctx", None),
        P(None, "fsdp", "ctx", None),
        P(("ctx", "fsdp"), None),
        P(("ctx", "fsdp")),
        P(("ctx", "fsdp")),
        P(("ctx", "fsdp"), None),
        P(("ctx", "fsdp")),
        P(("ctx", "fsdp")),
        P(("ctx", "fsdp")),
        P(("ctx", "fsdp"), None),
        P(("ctx", "fsdp")),
        P(("ctx", "fsdp"), None),
        P(("ctx", "fsdp")),
        P(("ctx", "fsdp")),
        P(("ctx", "fsdp")),
    )
    work = fast_on_device if fits(mesh) else on_device
    return jax.shard_map(
        work, mesh=mesh, in_specs=in_specs, out_specs=out_specs, check_vma=False
    )
```
